32 devices in a mesh: seq: 8 (over y, x, core), mlp: 4 (over z).
Axes of the slice: x: 2, y: 2, z: 4, core: 2. Of those that a mesh axis runs over, the one named last changes fastest.
Arguments:
- inputs: bfloat16 [4, 2048, 2048], P(None, ('seq', 'mlp')), may hold values from -6 to 6
- mixer_gain: bfloat16 [2048], P(('seq', 'mlp')), may hold values from 0.5 to 1.5
- branch_weight: bfloat16 [2048, 2560], P(('seq', 'mlp')), may hold values from -0.125 to 0.125
- input_weight: bfloat16 [2048, 2560], P(('seq', 'mlp')), may hold values from -0.125 to 0.125
- conv_weight: bfloat16 [4, 2560], P(None, ('seq', 'mlp')), may hold values from -3 to 3
- conv_bias: bfloat16 [2560], P(('seq', 'mlp')), may hold values from -3 to 3
- decay_weight: bfloat16 [2560, 256], P(('seq', 'mlp')), may hold values from -0.375 to 0.375
- decay_bias: bfloat16 [2560], P(('seq', 'mlp')), may hold values from -3 to 3
- inject_weight: bfloat16 [2560, 256], P(('seq', 'mlp')), may hold values from -0.375 to 0.375
- inject_bias: bfloat16 [2560], P(('seq', 'mlp')), may hold values from -3 to 3
- decay_param: bfloat16 [2560], P(('seq', 'mlp')), may hold values from 3.5 to 12, as said below
- output_weight: bfloat16 [2560, 2048], P(('seq', 'mlp')), may hold values from -0.3125 to 0.3125
- feed_gain: bfloat16 [2048], P(('seq', 'mlp')), may hold values from 0.5 to 1.5
- feed_gate: bfloat16 [2048, 6144], P(None, 'mlp'), may hold values from -0.125 to 0.125
- feed_up: bfloat16 [2048, 6144], P(None, 'mlp'), may hold values from -0.125 to 0.125
- feed_down: bfloat16 [6144, 2048], P('mlp'), may hold values from -0.15625 to 0.15625
- cotangent: bfloat16 [4, 2048, 2048], P(None, ('seq', 'mlp')), may hold values from -6 to 6
Outputs:
- result: bfloat16 [4, 2048, 2048], P(None, ('seq', 'mlp'))
- input_grad: float32 [4, 2048, 2048], P(None, ('seq', 'mlp'))
- mixer_gain_grad: float32 [2048], P(('seq', 'mlp'))
- branch_weight_grad: float32 [2048, 2560], P(('seq', 'mlp'))
- input_weight_grad: float32 [2048, 2560], P(('seq', 'mlp'))
- conv_weight_grad: float32 [4, 2560], P(None, ('seq', 'mlp'))
- conv_bias_grad: float32 [2560], P(('seq', 'mlp'))
- decay_weight_grad: float32 [2560, 256], P(('seq', 'mlp'))
- decay_bias_grad: float32 [2560], P(('seq', 'mlp'))
- inject_weight_grad: float32 [2560, 256], P(('seq', 'mlp'))
- inject_bias_grad: float32 [2560], P(('seq', 'mlp'))
- decay_param_grad: float32 [2560], P(('seq', 'mlp'))
- output_weight_grad: float32 [2560, 2048], P(('seq', 'mlp'))
- feed_gain_grad: float32 [2048], P(('seq', 'mlp'))
- feed_gate_grad: float32 [2048, 6144], P('seq', 'mlp')
- feed_up_grad: float32 [2048, 6144], P('seq', 'mlp')
- feed_down_grad: float32 [6144, 2048], P('mlp', 'seq')
The draws below stay inside these ranges and needn't reach their ends.
Inputs may be any that keep to these rules, and one draw needn't show every extreme that they name: decay_param sets each channel's rate through sigmoid(decay_param).
All inputs are finite; a program needn't handle non-finite values.
Results may differ from the reference program's by a relative error of at most 0.015.
Values may be sent and summed in bfloat16 or wider, within the bound.
A program may use at most 256 MiB of HBM per device.

```python
import jax
import jax.numpy as jnp
from jax import lax

D = 2048
R = 2560
HS = 256
F = 6144
CONV = 4
MB = 4
SEQ_LEN = 2048


def draw_decay_param(key, part):
    unit_draw = jax.random.uniform(key, (R,), jnp.float32)
    memory_span = 10.0 * jnp.power(0.2 * SEQ_LEN, unit_draw)
    return jnp.log(4.0 * memory_span).astype(jnp.bfloat16)


def levels(rng, extent, shards, least, top_value):
    level = 1.0
    for position, shards_of in shards:
        heights = jax.random.uniform(jax.random.fold_in(jax.random.fold_in(rng, 6), position), (shards_of,), jnp.float32, least / len(shards), top_value / len(shards))
        level = level * jnp.repeat(jnp.exp(heights), extent[position] // shards_of).reshape((-1,) + (1,) * (len(extent) - 1 - position))
    return level


def scatter_about(rng, dims, width, reach, shards=(), kind=jnp.bfloat16):
    factor_of = levels(rng, dims, shards, -0.22, 0.18) if shards else 1.0
    result = jax.random.normal(rng, dims, jnp.float32) * width * factor_of
    return jnp.minimum(jnp.maximum(result, -reach), reach).astype(kind)


def setup_inputs(seed: int = 0) -> dict:
    key_of = jax.random.split(jax.random.key(seed), 18)
    inputs = scatter_about(key_of[0], (MB, SEQ_LEN, D), 1.0, 6.0, ((1, 32),))
    mixer_gain = jnp.clip(1.0 + 0.1 * jax.random.normal(key_of[1], (D,), jnp.float32), 0.5, 1.5).astype(jnp.bfloat16)
    branch_weight = scatter_about(key_of[2], (D, R), D ** -0.5, 0.125, ((0, 32),))
    input_weight = scatter_about(key_of[3], (D, R), D ** -0.5, 0.125, ((0, 32),))
    conv_weight = scatter_about(key_of[4], (CONV, R), CONV ** -0.5, 3.0, ((1, 32),))
    conv_bias = scatter_about(key_of[5], (R,), 0.5, 3.0, ((0, 32),))
    decay_weight = scatter_about(key_of[6], (R, HS), HS ** -0.5, 0.375, ((0, 32),))
    decay_bias = scatter_about(key_of[7], (R,), 0.5, 3.0, ((0, 32),))
    inject_weight = scatter_about(key_of[8], (R, HS), HS ** -0.5, 0.375, ((0, 32),))
    inject_bias = scatter_about(key_of[9], (R,), 0.5, 3.0, ((0, 32),))
    decay_param = draw_decay_param(jax.random.fold_in(key_of[17], 71), 0)
    output_weight = scatter_about(key_of[11], (R, D), (R // 8) ** -0.5, 0.3125, ((0, 32),))
    feed_gain = jnp.clip(1.0 + 0.1 * jax.random.normal(key_of[12], (D,), jnp.float32), 0.5, 1.5).astype(jnp.bfloat16)
    feed_gate = scatter_about(key_of[13], (D, F), D ** -0.5, 0.125, ((1, 4),))
    feed_up = scatter_about(key_of[14], (D, F), D ** -0.5, 0.125, ((1, 4),))
    feed_down = scatter_about(key_of[15], (F, D), (F // 4) ** -0.5, 0.15625, ((0, 4),))
    cotangent = scatter_about(key_of[16], (MB, SEQ_LEN, D), 1.0, 6.0, ((1, 32),))
    return dict(inputs=inputs, mixer_gain=mixer_gain, branch_weight=branch_weight, input_weight=input_weight, conv_weight=conv_weight, conv_bias=conv_bias, decay_weight=decay_weight, decay_bias=decay_bias, inject_weight=inject_weight, inject_bias=inject_bias, decay_param=decay_param, output_weight=output_weight, feed_gain=feed_gain, feed_gate=feed_gate, feed_up=feed_up, feed_down=feed_down, cotangent=cotangent)


EPS = 1e-06
RATE_SCALE = 8.0
HIGH = lax.Precision.HIGHEST

@jax.custom_vjp
def low(v):
    return lax.optimization_barrier(v.astype(jnp.bfloat16)).astype(jnp.float32)

@jax.custom_vjp
def low_back(v):
    return v

def low_keep(v):
    return (low(v), None)

def low_pass(kept, grad):
    return (grad,)

def back_keep(v):
    return (v, None)

def back_low(kept, grad):
    return (low(grad),)
low.defvjp(low_keep, low_pass)
low_back.defvjp(back_keep, back_low)

def chain_join(first_pair, second_pair):
    return (first_pair[0] * second_pair[0], second_pair[0] * first_pair[1] + second_pair[1])

def norm_rows(values, gain):
    inverse = lax.rsqrt(lax.optimization_barrier(jnp.mean(values * values, axis=-1, keepdims=True)) + EPS)
    return values * inverse * gain

def matmul(left_side, right_side):
    return jnp.dot(left_side, right_side, precision=HIGH, preferred_element_type=jnp.float32)

def head_mix(conv_low, weight):
    seq_rows = conv_low.shape[0]
    conv_heads = conv_low.reshape(seq_rows, R // HS, HS)
    mixed_heads = jnp.einsum('lhi,hij->lhj', conv_heads, weight.reshape(R // HS, HS, HS), precision=HIGH)
    return mixed_heads.reshape(seq_rows, R)

def block_forward(stream, mixer_gain, branch_weight, input_weight, conv_weight, conv_bias, decay_weight, decay_bias, inject_weight, inject_bias, decay_param, output_weight, feed_gain, feed_gate, feed_up, feed_down):
    seq_rows = stream.shape[0]
    normed = low(norm_rows(stream, mixer_gain))
    branch = jax.nn.gelu(low_back(matmul(normed, branch_weight)))
    conv_in = low_back(low(matmul(normed, input_weight)))
    padded = jnp.concatenate([jnp.zeros((CONV - 1, R), jnp.float32), conv_in], axis=0)
    conv_out = jnp.zeros((seq_rows, R), jnp.float32) + conv_bias
    for offset in range(CONV):
        start_row = CONV - 1 - offset
        conv_out = conv_out + conv_weight[offset] * padded[start_row:start_row + seq_rows]
    conv_low = low(conv_out)
    recur_gate = jax.nn.sigmoid(low_back(head_mix(conv_low, decay_weight)) + decay_bias)
    inject_gate = jax.nn.sigmoid(low_back(head_mix(conv_low, inject_weight)) + inject_bias)
    decay_log = -RATE_SCALE * recur_gate * jax.nn.softplus(-decay_param)
    injected = jnp.sqrt(-jnp.expm1(2.0 * decay_log)) * inject_gate * conv_low
    decay_rates = jnp.exp(decay_log)
    scanned = lax.associative_scan(chain_join, (decay_rates, injected), axis=0)
    hidden_state = scanned[1]
    mixed_low = low(hidden_state * branch)
    stream_mid = stream + low_back(matmul(mixed_low, output_weight))
    feed_in = low(norm_rows(stream_mid, feed_gain))
    gate_pre = low_back(matmul(feed_in, feed_gate))
    up_pre = low_back(matmul(feed_in, feed_up))
    hidden = low(jax.nn.gelu(gate_pre) * up_pre)
    return stream_mid + low_back(matmul(hidden, feed_down))

def reference(inputs, mixer_gain, branch_weight, input_weight, conv_weight, conv_bias, decay_weight, decay_bias, inject_weight, inject_bias, decay_param, output_weight, feed_gain, feed_gate, feed_up, feed_down, cotangent):
    params = jax.tree.map(lambda tensor: tensor.astype(jnp.float32), (mixer_gain, branch_weight, input_weight, conv_weight, conv_bias, decay_weight, decay_bias, inject_weight, inject_bias, decay_param, output_weight, feed_gain, feed_gate, feed_up, feed_down))

    def one_sequence(totals, seq_pair):
        stream = seq_pair[0]
        upstream = seq_pair[1]
        output, pullback = jax.vjp(block_forward, stream, *params)
        gradients = pullback(upstream)
        new_totals = jax.tree.map(jnp.add, totals, tuple(gradients[1:]))
        return (new_totals, (output.astype(jnp.bfloat16), gradients[0]))
    zero_totals = jax.tree.map(jnp.zeros_like, params)
    totals, outputs = lax.scan(one_sequence, zero_totals, (inputs.astype(jnp.float32), cotangent.astype(jnp.float32)))
    return (outputs[0], outputs[1], totals[0], totals[1], totals[2], totals[3], totals[4], totals[5], totals[6], totals[7], totals[8], totals[9], totals[10], totals[11], totals[12], totals[13], totals[14])
```

```python
import functools
import math

import jax
import jax.numpy as jnp
from jax import lax
from jax.experimental import pallas as pl
from jax.experimental.pallas import tpu as pltpu
from jax.sharding import PartitionSpec as P

EPS = 1e-06
RATE_SCALE = 8.0
F32 = jnp.float32
BF16 = jnp.bfloat16
MESH = pl.DeviceIdType.MESH
PAD = 8
GELU_C = math.sqrt(2.0 / math.pi)
VMEM_LIMIT = 48 << 20


def gelu_and_slope(v):
    sq = v * v
    t = jnp.tanh(GELU_C * v * (1.0 + 0.044715 * sq))
    half = 0.5 * (1.0 + t)
    slope = half + 0.5 * v * (1.0 - t * t) * GELU_C * (1.0 + 3 * 0.044715 * sq)
    return v * half, slope


def gelu_only(v):
    return 0.5 * v * (1.0 + jnp.tanh(GELU_C * v * (1.0 + 0.044715 * (v * v))))


def decay_terms(recur, soft):
    log_rate = (-RATE_SCALE) * recur * soft
    rate = jnp.exp(log_rate)
    y = -2.0 * log_rate
    e = 1.0 - y * (1.0 / 10.0)
    for n in range(9, 1, -1):
        e = 1.0 - (y * (1.0 / n)) * e
    return rate, jnp.where(y < 0.5, y * e, 1.0 - rate * rate)


def norm_inverse(v):
    return lax.rsqrt(jnp.mean(v * v, axis=-1, keepdims=True) + EPS)


def tile_scan(a, b, reverse):
    row = lax.broadcasted_iota(jnp.int32, a.shape, 1)
    for d in (1, 2, 4):
        ok = (row < 8 - d) if reverse else (row >= d)
        shift = 8 - d if reverse else d
        a_near = jnp.where(ok, pltpu.roll(a, shift, 1), 1.0)
        b_near = jnp.where(ok, pltpu.roll(b, shift, 1), 0.0)
        b = b + a * b_near
        a = a * a_near
    return a, b


def part_scan(a, b, a_ref, b_ref, reverse):
    seqs, rows, lanes = a.shape
    tiles = rows // 8
    a, b = tile_scan(a.reshape(seqs * tiles, 8, lanes), b.reshape(seqs * tiles, 8, lanes), reverse)
    a = a.reshape(seqs, tiles, 8, lanes)
    b = b.reshape(seqs, tiles, 8, lanes)
    a_run = b_run = None
    edge = 0 if reverse else 7
    for i in range(tiles):
        t = tiles - 1 - i if reverse else i
        at, bt = a[:, t], b[:, t]
        if a_run is not None:
            bt = bt + at * b_run
            at = at * a_run
        a_ref[:, t * 8 : (t + 1) * 8, :] = at
        b_ref[:, t * 8 : (t + 1) * 8, :] = bt
        a_run, b_run = at[:, edge : edge + 1, :], bt[:, edge : edge + 1, :]
    return a_run[:, 0, :], b_run[:, 0, :]


def gates_kernel(seqs, n_ref, w_ref, dw_ref, iw_ref, vec_ref,
                 cin_ref, low_ref, rec_ref, inj_ref, prod_ref, loc_ref, ends_ref):
    cin = jnp.dot(n_ref[...], w_ref[...], preferred_element_type=F32).astype(BF16)
    cin_ref[...] = cin
    x = cin.astype(F32)
    ext, lanes = x.shape
    taps = vec_ref[...]
    y = taps[4:5, :] + taps[0:1, :] * x
    for k in range(1, 4):
        y = y + taps[k : k + 1, :] * pltpu.roll(x, k, 0)
    y = y.reshape(seqs, ext // seqs, lanes)[:, PAD:, :]
    low = y.astype(BF16)
    low_ref[...] = low
    shape = y.shape
    low2 = low.reshape(shape[0] * shape[1], lanes)
    dpre = jnp.dot(low2, dw_ref[...], preferred_element_type=F32)
    ipre = jnp.dot(low2, iw_ref[...], preferred_element_type=F32)
    recur = jax.nn.sigmoid(dpre + taps[5:6, :])
    inject = jax.nn.sigmoid(ipre + taps[6:7, :])
    rate, em = decay_terms(recur, taps[7:8, :])
    recur = recur.reshape(shape)
    inject = inject.reshape(shape)
    rec_ref[...] = recur
    inj_ref[...] = inject
    injected = jnp.sqrt(em).reshape(shape) * inject * low.astype(F32)
    pa, pb = part_scan(rate.reshape(shape), injected, prod_ref, loc_ref, False)
    ends_ref[0:seqs, :] = pa
    ends_ref[seqs : 2 * seqs, :] = pb


def mix_kernel(heads, loc_ref, prod_ref, bp_ref, carry_ref, w_ref, x_ref, gain_ref,
               state_ref, mixed_ref, mid_ref, feed_ref, acc_ref):
    h = pl.program_id(0)
    carry = carry_ref[...][:, None, :]
    state = loc_ref[...] + prod_ref[...] * carry
    state_ref[...] = state
    mixed = (state * gelu_only(bp_ref[...])).astype(BF16)
    mixed_ref[...] = mixed
    b, s, lanes = mixed.shape
    part = jnp.dot(mixed.reshape(b * s, lanes), w_ref[...], preferred_element_type=F32)

    @pl.when(h == 0)
    def _():
        acc_ref[...] = x_ref[...].astype(F32) + part

    @pl.when(h > 0)
    def _():
        acc_ref[...] += part

    @pl.when(h == heads - 1)
    def _():
        mid = acc_ref[...]
        mid_ref[...] = mid
        feed_ref[...] = (mid * norm_inverse(mid) * gain_ref[...]).astype(BF16)


def back_scan_kernel(seqs, g_ref, w_ref, bp_ref, state_ref, rec_ref, vec_ref,
                     prod_ref, adj_ref, gbp_ref, ends_ref):
    gm = lax.dot_general(g_ref[...], w_ref[...], (((1,), (1,)), ((), ())), preferred_element_type=F32)
    rows, lanes = gm.shape
    shape = (seqs, rows // seqs, lanes)
    act, slope = gelu_and_slope(bp_ref[...])
    gm = gm.reshape(shape)
    gbp = gm * state_ref[...] * slope
    gbp = jnp.concatenate([jnp.zeros((seqs, PAD, lanes), F32), gbp], axis=1)
    gbp_ref[...] = gbp.reshape(seqs * (shape[1] + PAD), lanes).astype(BF16)
    rate = jnp.exp((-RATE_SCALE) * rec_ref[...] * vec_ref[7:8, :])
    after = pltpu.roll(rate.reshape(rows, lanes), rows - 1, 0).reshape(shape)
    row = lax.broadcasted_iota(jnp.int32, shape, 1)
    after = jnp.where(row == shape[1] - 1, 1.0, after)
    pa, pb = part_scan(after, gm * act, prod_ref, adj_ref, True)
    first = rate[:, 0, :]
    ends_ref[0:seqs, :] = first * pa
    ends_ref[seqs : 2 * seqs, :] = first * pb


def back_gates_kernel(heads, prod_ref, adj_ref, carry_ref, state_ref, sin_ref, rec_ref, inj_ref, low_ref,
                      cin_ref, vec_ref, dw_ref, iw_ref, gbp_ref, bw_ref, cw_ref,
                      gcin_ref, gdw_ref, giw_ref, gvec_ref, gn_ref):
    h = pl.program_id(0)
    vec = vec_ref[...]
    soft = vec[7:8, :]
    adj = adj_ref[...] + prod_ref[...] * carry_ref[...][:, None, :]
    shape = adj.shape
    seqs, rows, lanes = shape
    flat = (seqs * rows, lanes)
    state = state_ref[...]
    prev = pltpu.roll(state.reshape(flat), 1, 0).reshape(shape)
    row = lax.broadcasted_iota(jnp.int32, shape, 1)
    prev = jnp.where(row == 0, sin_ref[...][:, None, :], prev)
    recur, inject = rec_ref[...], inj_ref[...]
    rate, em = decay_terms(recur, soft)
    mult = jnp.sqrt(em)
    low = low_ref[...]
    conv = low.astype(F32)
    g_log = adj * prev * rate - adj * inject * conv * (rate * rate) / mult
    am = adj * mult
    g_elem = am * inject
    g_rec = g_log * ((-RATE_SCALE) * soft)
    g_soft = jnp.sum((g_log * recur).reshape(flat), axis=0, keepdims=True) * (-RATE_SCALE)
    gdp = (g_rec * recur * (1.0 - recur)).reshape(flat)
    gip = (am * conv * inject * (1.0 - inject)).reshape(flat)
    gdp_low, gip_low = gdp.astype(BF16), gip.astype(BF16)
    low2 = low.reshape(flat)
    tok = (((0,), (0,)), ((), ()))
    last = (((1,), (1,)), ((), ()))
    gdw_ref[...] = lax.dot_general(low2, gdp_low, tok, preferred_element_type=F32).astype(BF16)
    giw_ref[...] = lax.dot_general(low2, gip_low, tok, preferred_element_type=F32).astype(BF16)
    gc = (
        g_elem.reshape(flat)
        + lax.dot_general(gdp_low, dw_ref[...], last, preferred_element_type=F32)
        + lax.dot_general(gip_low, iw_ref[...], last, preferred_element_type=F32)
    )
    gce = jnp.concatenate([jnp.zeros((seqs, PAD, lanes), F32), gc.reshape(shape)], axis=1)
    ext = seqs * (rows + PAD)
    gce = gce.reshape(ext, lanes)
    x = cin_ref[...].astype(F32)
    out = vec[0:1, :] * gce
    sums = [jnp.sum(gce * x, axis=0, keepdims=True)]
    for k in range(1, 4):
        out = out + vec[k : k + 1, :] * pltpu.roll(gce, ext - k, 0)
        sums.append(jnp.sum(gce * pltpu.roll(x, k, 0), axis=0, keepdims=True))
    sums.append(jnp.sum(gce, axis=0, keepdims=True))
    sums.append(jnp.sum(gdp, axis=0, keepdims=True))
    sums.append(jnp.sum(gip, axis=0, keepdims=True))
    sums.append(g_soft)
    for i, v in enumerate(sums):
        gvec_ref[i : i + 1, :] = v
    gcin = out.astype(BF16)
    gcin_ref[...] = gcin
    part = lax.dot_general(gcin, cw_ref[...], last, preferred_element_type=F32)
    part += lax.dot_general(gbp_ref[...], bw_ref[...], last, preferred_element_type=F32)

    @pl.when(h == 0)
    def _():
        gn_ref[...] = part

    @pl.when(h > 0)
    def _():
        gn_ref[...] += part


def carry_kernel(seqs, n_seq, n_mlp, reverse, ends_ref, out_ref, zbuf, sbuf, total, ssem, rsem):
    ms, mz = lax.axis_index("seq"), lax.axis_index("mlp")
    barrier = pltpu.get_barrier_semaphore()
    for d in range(1, n_mlp):
        pl.semaphore_signal(barrier, inc=1, device_id=(ms, lax.rem(mz + d, n_mlp)), device_id_type=MESH)
    for d in range(1, n_seq):
        pl.semaphore_signal(barrier, inc=1, device_id=(lax.rem(ms + d, n_seq), mz), device_id_type=MESH)
    pl.semaphore_wait(barrier, n_mlp + n_seq - 2)
    copies = []
    for d in range(1, n_mlp):
        copies.append(pltpu.make_async_remote_copy(
            src_ref=ends_ref, dst_ref=zbuf.at[mz], send_sem=ssem.at[d - 1], recv_sem=rsem.at[d - 1],
            device_id=(ms, lax.rem(mz + d, n_mlp)), device_id_type=MESH))
        copies[-1].start()
    zbuf[mz] = ends_ref[...]
    for c in copies:
        c.wait()
    shape = (seqs, ends_ref.shape[1])
    tp, ts = jnp.ones(shape, F32), jnp.zeros(shape, F32)
    pp, ps = tp, ts
    for i in range(n_mlp):
        z = n_mlp - 1 - i if reverse else i
        val = zbuf[z]
        p, s = val[0:seqs, :], val[seqs : 2 * seqs, :]
        ts = p * ts + s
        tp = p * tp
        mine = jnp.where((z > mz) if reverse else (z < mz), 1.0, 0.0)
        ps = mine * (p * ps + s) + (1.0 - mine) * ps
        pp = (mine * p + (1.0 - mine)) * pp
    total[0:seqs, :] = tp
    total[seqs : 2 * seqs, :] = ts
    copies = []
    for d in range(1, n_seq):
        i = n_mlp - 2 + d
        copies.append(pltpu.make_async_remote_copy(
            src_ref=total, dst_ref=sbuf.at[ms], send_sem=ssem.at[i], recv_sem=rsem.at[i],
            device_id=(lax.rem(ms + d, n_seq), mz), device_id_type=MESH))
        copies[-1].start()
    sbuf[ms] = total[...]
    for c in copies:
        c.wait()
    c = jnp.zeros(shape, F32)
    for i in range(n_seq):
        q = n_seq - 1 - i if reverse else i
        val = sbuf[q]
        p, s = val[0:seqs, :], val[seqs : 2 * seqs, :]
        mine = jnp.where((q > ms) if reverse else (q < ms), 1.0, 0.0)
        c = mine * (p * c + s) + (1.0 - mine) * c
    out_ref[...] = pp * c + ps


def carry_call(ends, seqs, n_seq, n_mlp, reverse):
    rows, width = ends.shape
    n = n_seq + n_mlp - 2
    return pl.pallas_call(
        functools.partial(carry_kernel, seqs, n_seq, n_mlp, reverse),
        out_shape=jax.ShapeDtypeStruct((seqs, width), F32),
        in_specs=[pl.BlockSpec(memory_space=pltpu.VMEM)],
        out_specs=pl.BlockSpec(memory_space=pltpu.VMEM),
        scratch_shapes=[
            pltpu.VMEM((n_mlp, rows, width), F32),
            pltpu.VMEM((n_seq, rows, width), F32),
            pltpu.VMEM((rows, width), F32),
            pltpu.SemaphoreType.DMA((n,)),
            pltpu.SemaphoreType.DMA((n,)),
        ],
        compiler_params=pltpu.CompilerParams(
            collective_id=1 if reverse else 0, has_side_effects=True, vmem_limit_bytes=VMEM_LIMIT
        ),
        name="carry_back" if reverse else "carry_fwd",
    )(ends)


class Seq:
    def __init__(self):
        self.n = lax.axis_size("seq")
        self.me = lax.axis_index("seq")
        self.bits = list(range(self.n.bit_length() - 1))
        chips = self.bits[1:]
        turn = len(chips) // 2
        self.orders = (chips, chips[turn:] + chips[:turn])

    def mine(self, bit):
        return (self.me >> bit) & 1

    def swap(self, v, bit):
        return lax.ppermute(v, "seq", [(i, i ^ (1 << bit)) for i in range(self.n)])

    def gather(self, w):
        g = lax.all_gather(w, "mlp", axis=0, tiled=True)
        half = g.shape[0] // 2
        pieces = []
        for piece, order in zip((g[:half], g[half:]), self.orders):
            rel = piece[None]
            order = order + [0]
            for bit in order:
                rel = jnp.concatenate([rel, self.swap(rel, bit)], axis=0)
            pieces.append((rel, order))
        out = []
        for q in range(self.n):
            for rel, order in pieces:
                e = sum((((q ^ self.me) >> bit) & 1) << i for i, bit in enumerate(order))
                out.append(lax.dynamic_index_in_dim(rel, e, 0, keepdims=False))
        return jnp.concatenate(out, axis=0)

    def scatter_step(self, v, left, bit, kind=BF16):
        pos = left.index(bit)
        rest = v.shape[1:]
        v = v.reshape((1 << pos, 2, 1 << (len(left) - 1 - pos)) + rest)
        keep = lax.dynamic_index_in_dim(v, self.mine(bit), 1, keepdims=False)
        send = lax.dynamic_index_in_dim(v, 1 - self.mine(bit), 1, keepdims=False)
        got = self.swap(send, bit)
        out = (keep.astype(F32) + got.astype(F32)).astype(kind)
        return out.reshape((-1,) + rest), [b for b in left if b != bit]

    def scatter_chips(self, v, left, kind=BF16):
        half = v.shape[1] // 2
        outs = []
        for piece, order in zip((v[:, :half], v[:, half:]), self.orders):
            now = left
            for i, bit in enumerate(order):
                piece, now = self.scatter_step(piece, now, bit, kind if i == len(order) - 1 else BF16)
            outs.append(piece)
        return jnp.concatenate(outs, axis=1)


def flat_dot(left, right):
    shape = left.shape
    out = jnp.dot(left.reshape(-1, shape[-1]), right, preferred_element_type=F32)
    return out.reshape(shape[:-1] + (right.shape[1],))


def dot_against(left, right):
    shape = left.shape
    out = lax.dot_general(
        left.reshape(-1, shape[-1]), right, (((1,), (1,)), ((), ())), preferred_element_type=F32
    )
    return out.reshape(shape[:-1] + (right.shape[0],))


def outer_sum(left, right):
    return lax.dot_general(
        left.reshape(-1, left.shape[-1]),
        right.reshape(-1, right.shape[-1]),
        (((0,), (0,)), ((), ())),
        preferred_element_type=F32,
    )


def gated_unit(gate_pre, up_pre):
    return jax.nn.gelu(gate_pre) * up_pre


def norm_back(values, inverse, gain, upstream):
    scaled = upstream * gain
    gain_grad = jnp.sum(upstream * values * inverse, axis=(0, 1))
    inner_mean = jnp.mean(scaled * values, axis=-1, keepdims=True)
    return (inverse * (scaled - values * inner_mean * inverse * inverse), gain_grad)


def per_device(inputs, mixer_gain, branch_weight, input_weight, conv_weight, conv_bias, decay_weight,
               decay_bias, inject_weight, inject_bias, decay_param, output_weight, feed_gain,
               feed_gate, feed_up, feed_down, cotangent):
    both = ("seq", "mlp")
    seq = Seq()
    n_seq, n_mlp = seq.n, lax.axis_size("mlp")
    n_dev = n_seq * n_mlp
    seqs, rows, width = inputs.shape
    taps, r_own = conv_weight.shape
    edge = taps - 1
    head = decay_weight.shape[1]
    r_all = r_own * n_dev
    heads = r_all // head
    d_own = width // n_dev
    ext_rows = rows + PAD
    ext = seqs * ext_rows
    tokens = seqs * rows

    lanes = 128
    small = [conv_weight.T, conv_bias[:, None], decay_bias[:, None], inject_bias[:, None], decay_param[:, None]]
    gains = [jnp.pad(g, (0, r_own - d_own))[:, None] for g in (mixer_gain, feed_gain)]
    small = jnp.concatenate(small + gains, axis=1)
    small = jnp.pad(small, ((0, 0), (0, lanes - small.shape[1])))
    gates_own = jnp.concatenate([decay_weight, inject_weight, small], axis=1)
    gates_all = lax.all_gather(gates_own, both, axis=0, tiled=True)
    vectors = gates_all[:, 2 * head :].astype(F32)
    gain_rows = vectors[:, 8:10].reshape(n_dev, r_own, 2)[:, :d_own, :].reshape(width, 2)
    gain_mixer, gain_feed = gain_rows[:, 0], gain_rows[:, 1]
    param = vectors[:, 7]
    vec = jnp.concatenate([vectors[:, :7].T, jax.nn.softplus(-param)[None, :]], axis=0)

    last_tokens = lax.ppermute(inputs[:, rows - edge :, :], both, [(i, i + 1) for i in range(n_dev - 1)])
    x_ext = jnp.concatenate(
        [jnp.zeros((seqs, PAD - edge, width), BF16), last_tokens, inputs], axis=1
    )
    full_input = seq.gather(input_weight)
    full_branch = seq.gather(branch_weight)
    full_output = seq.gather(output_weight)

    stream_ext = x_ext.astype(F32)
    inverse_ext = norm_inverse(stream_ext)
    normed_ext = (stream_ext * inverse_ext * gain_mixer).astype(BF16).reshape(ext, width)

    params = lambda **k: pltpu.CompilerParams(dimension_semantics=("arbitrary",), vmem_limit_bytes=VMEM_LIMIT, **k)
    tok_head = pl.BlockSpec((seqs, rows, head), lambda h: (0, 0, h))
    ext_head = pl.BlockSpec((ext, head), lambda h: (0, h))
    vec_head = pl.BlockSpec((8, head), lambda h: (0, h))
    seq_head = pl.BlockSpec((seqs, head), lambda h: (0, h))
    col_head = pl.BlockSpec((width, head), lambda h: (0, h))
    row_head = pl.BlockSpec((head, width), lambda h: (h, 0))
    decay_head = pl.BlockSpec((head, head), lambda h: (h, 0))
    inject_head = pl.BlockSpec((head, head), lambda h: (h, 1))
    whole = lambda *shape: pl.BlockSpec(shape, lambda h: (0,) * len(shape))
    tok = lambda kind: jax.ShapeDtypeStruct((seqs, rows, r_all), kind)
    struct = jax.ShapeDtypeStruct

    conv_in, conv_low, recur, inject, prod, local, ends = pl.pallas_call(
        functools.partial(gates_kernel, seqs),
        grid=(heads,),
        in_specs=[whole(ext, width), col_head, decay_head, inject_head, vec_head],
        out_specs=[ext_head, tok_head, tok_head, tok_head, tok_head, tok_head,
                   pl.BlockSpec((2 * seqs, head), lambda h: (0, h))],
        out_shape=[struct((ext, r_all), BF16), tok(BF16), tok(F32), tok(F32), tok(F32), tok(F32),
                   struct((2 * seqs, r_all), F32)],
        compiler_params=params(),
        name="gates",
    )(normed_ext, full_input, gates_all, gates_all, vec)

    normed = normed_ext.reshape(seqs, ext_rows, width)[:, PAD:, :]
    branch_pre = flat_dot(normed, full_branch)
    state_in = carry_call(ends, seqs, n_seq, n_mlp, False)

    state, mixed, mid, feed_low = pl.pallas_call(
        functools.partial(mix_kernel, heads),
        grid=(heads,),
        in_specs=[tok_head, tok_head, tok_head, seq_head, row_head, whole(tokens, width), whole(1, width)],
        out_specs=[tok_head, tok_head, whole(tokens, width), whole(tokens, width)],
        out_shape=[tok(F32), tok(BF16), struct((tokens, width), F32), struct((tokens, width), BF16)],
        scratch_shapes=[pltpu.VMEM((tokens, width), F32)],
        compiler_params=params(),
        name="mix",
    )(local, prod, branch_pre, state_in, full_output, inputs.reshape(tokens, width), gain_feed[None, :])
    stream_mid = mid.reshape(seqs, rows, width)

    feed_rows = lax.all_gather(feed_low.reshape(seqs, rows, width), "mlp", axis=1, tiled=True)
    grad_rows = lax.all_gather(cotangent, "mlp", axis=1, tiled=True)
    gate_pre = flat_dot(feed_rows, feed_gate)
    up_pre = flat_dot(feed_rows, feed_up)
    hidden = gated_unit(gate_pre, up_pre).astype(BF16)
    grad_hidden = dot_against(grad_rows, feed_down)
    gate_grad, up_grad = jax.vjp(gated_unit, gate_pre, up_pre)[1](grad_hidden)
    gate_low, up_low = gate_grad.astype(BF16), up_grad.astype(BF16)
    feed_back = dot_against(gate_low, feed_gate) + dot_against(up_low, feed_up)
    feed_norm_grad = lax.psum_scatter(
        feed_back.astype(BF16), "mlp", scatter_dimension=1, tiled=True
    ).astype(F32)
    feed_out = lax.psum_scatter(
        flat_dot(hidden, feed_down).astype(BF16), "mlp", scatter_dimension=1, tiled=True
    ).astype(F32)
    result = (stream_mid + feed_out).astype(BF16)

    feed_grads = []
    for left, right in ((feed_rows, gate_low), (feed_rows, up_low), (grad_rows, hidden)):
        g = outer_sum(left, right).astype(BF16)
        g = g.reshape((n_seq, width // n_seq, g.shape[1]))
        g, left_bits = seq.scatter_step(g, seq.bits[::-1], 0)
        feed_grads.append(seq.scatter_chips(g, left_bits, F32)[0])

    feed_inverse = norm_inverse(stream_mid)
    mid_part, feed_gain_grad = norm_back(stream_mid, feed_inverse, gain_feed, feed_norm_grad)
    mid_grad = cotangent.astype(F32) + mid_part
    mid_low = mid_grad.astype(BF16).reshape(tokens, width)

    back_prod, back_local, gbp, back_ends = pl.pallas_call(
        functools.partial(back_scan_kernel, seqs),
        grid=(heads,),
        in_specs=[whole(tokens, width), row_head, tok_head, tok_head, tok_head, vec_head],
        out_specs=[tok_head, tok_head, ext_head, pl.BlockSpec((2 * seqs, head), lambda h: (0, h))],
        out_shape=[tok(F32), tok(F32), struct((ext, r_all), BF16), struct((2 * seqs, r_all), F32)],
        compiler_params=params(),
        name="back_scan",
    )(mid_low, full_output, branch_pre, state, recur, vec)
    adj_in = carry_call(back_ends, seqs, n_seq, n_mlp, True)

    gcin, gdw, giw, gvec, gnorm = pl.pallas_call(
        functools.partial(back_gates_kernel, heads),
        grid=(heads,),
        in_specs=[tok_head, tok_head, seq_head, tok_head, seq_head, tok_head, tok_head, tok_head,
                  ext_head, vec_head, decay_head, inject_head, ext_head, col_head, col_head],
        out_specs=[ext_head, decay_head, decay_head, vec_head, whole(ext, width)],
        out_shape=[struct((ext, r_all), BF16), struct((r_all, head), BF16), struct((r_all, head), BF16),
                   struct((8, r_all), F32), struct((ext, width), F32)],
        compiler_params=params(),
        name="back_gates",
    )(back_prod, back_local, adj_in, state, state_in, recur, inject, conv_low,
      conv_in, vec, gates_all, gates_all, gbp, full_branch, full_input)

    stream_part, mixer_gain_grad = norm_back(
        stream_ext, inverse_ext, gain_mixer, gnorm.reshape(seqs, ext_rows, width)
    )
    next_part = lax.ppermute(
        stream_part[:, PAD - edge : PAD, :], both, [(i + 1, i) for i in range(n_dev - 1)]
    )
    next_part = jnp.pad(next_part, ((0, 0), (rows - edge, 0), (0, 0)))
    input_grad = mid_grad + stream_part[:, PAD:, :] + next_part

    core = seq.mine(0)

    def pair_grad(left, right):
        half = right.shape[1] // 2
        mine = lax.dynamic_slice_in_dim(right, core * half, half, 1)
        other = lax.dynamic_slice_in_dim(right, (1 - core) * half, half, 1)
        left_two = jnp.concatenate([left, seq.swap(left, 0)], axis=0)
        right_two = jnp.concatenate([mine, seq.swap(other, 0)], axis=0)
        g = outer_sum(left_two, right_two).astype(BF16)
        g = g.reshape(n_seq, g.shape[0] // n_seq, half)
        g = seq.scatter_chips(g, seq.bits[::-1])
        g = lax.psum_scatter(g, "mlp", scatter_dimension=1, tiled=True)
        keep = lax.dynamic_index_in_dim(g, core, 0, keepdims=False)
        got = seq.swap(lax.dynamic_index_in_dim(g, 1 - core, 0, keepdims=False), 0)
        first = jnp.where(core == 0, keep, got)
        second = jnp.where(core == 0, got, keep)
        return jnp.concatenate([first, second], axis=1).astype(F32)

    output_out = pair_grad(mixed.reshape(tokens, r_all), mid_low)
    branch_out = pair_grad(normed_ext, gbp)
    input_out = pair_grad(normed_ext, gcin)

    param_grad = gvec[7] * -jax.nn.sigmoid(-param)
    cols = jnp.concatenate([gvec[:7], param_grad[None, :]], axis=0).T
    gain_cols = jnp.stack([mixer_gain_grad, feed_gain_grad], axis=-1).reshape(n_dev, d_own, 2)
    gain_cols = jnp.pad(gain_cols, ((0, 0), (0, r_own - d_own), (0, 0))).reshape(r_all, 2)
    cols = jnp.concatenate([cols, gain_cols], axis=1)
    cols = jnp.pad(cols, ((0, 0), (0, lanes - cols.shape[1]))).astype(BF16)
    rest = jnp.concatenate([gdw, giw, cols], axis=1)
    rest = lax.psum_scatter(rest, "seq", scatter_dimension=0, tiled=True)
    rest = lax.psum_scatter(rest, "mlp", scatter_dimension=0, tiled=True).astype(F32)
    decay_out, inject_out = rest[:, :head], rest[:, head : 2 * head]
    tail = rest[:, 2 * head :]

    return (
        result,
        input_grad,
        tail[:d_own, 8],
        branch_out,
        input_out,
        tail[:, :4].T,
        tail[:, 4],
        decay_out,
        tail[:, 5],
        inject_out,
        tail[:, 6],
        tail[:, 7],
        output_out,
        tail[:d_own, 9],
        feed_grads[0],
        feed_grads[1],
        feed_grads[2].T,
    )


def solution(mesh):
    both = ("seq", "mlp")
    in_specs = (
        P(None, both, None), P(both), P(both, None), P(both, None), P(None, both), P(both),
        P(both, None), P(both), P(both, None), P(both), P(both), P(both, None), P(both),
        P(None, "mlp"), P(None, "mlp"), P("mlp", None), P(None, both, None),
    )
    out_specs = (
        P(None, both, None), P(None, both, None), P(both), P(both, None), P(both, None), P(None, both),
        P(both), P(both, None), P(both), P(both, None), P(both), P(both), P(both, None), P(both),
        P("seq", "mlp"), P("seq", "mlp"), P("mlp", "seq"),
    )
    return jax.shard_map(
        per_device, mesh=mesh, in_specs=in_specs, out_specs=out_specs, check_vma=False
    )
```

```python
import functools
import math

import jax
import jax.numpy as jnp
from jax import lax
from jax.experimental import pallas as pl
from jax.experimental.pallas import tpu as pltpu
from jax.experimental.layout import Layout, with_layout_constraint
from jax.sharding import PartitionSpec as P

EPS = 1e-06
RATE_SCALE = 8.0
F32 = jnp.float32
BF16 = jnp.bfloat16
MESH = pl.DeviceIdType.MESH
PAD = 8
GELU_C = math.sqrt(2.0 / math.pi)
VMEM_LIMIT = 48 << 20


def gelu_and_slope(v):
    sq = v * v
    t = jnp.tanh(GELU_C * v * (1.0 + 0.044715 * sq))
    half = 0.5 * (1.0 + t)
    slope = half + 0.5 * v * (1.0 - t * t) * GELU_C * (1.0 + 3 * 0.044715 * sq)
    return v * half, slope


def gelu_only(v):
    return 0.5 * v * (1.0 + jnp.tanh(GELU_C * v * (1.0 + 0.044715 * (v * v))))


def decay_terms(recur, soft):
    log_rate = (-RATE_SCALE) * recur * soft
    rate = jnp.exp(log_rate)
    y = -2.0 * log_rate
    e = 1.0 - y * (1.0 / 10.0)
    for n in range(9, 1, -1):
        e = 1.0 - (y * (1.0 / n)) * e
    return rate, jnp.where(y < 0.5, y * e, 1.0 - rate * rate)


def norm_inverse(v):
    return lax.rsqrt(jnp.mean(v * v, axis=-1, keepdims=True) + EPS)


def tile_scan(a, b, reverse):
    row = lax.broadcasted_iota(jnp.int32, a.shape, 1)
    for d in (1, 2, 4):
        ok = (row < 8 - d) if reverse else (row >= d)
        shift = 8 - d if reverse else d
        a_near = jnp.where(ok, pltpu.roll(a, shift, 1), 1.0)
        b_near = jnp.where(ok, pltpu.roll(b, shift, 1), 0.0)
        b = b + a * b_near
        a = a * a_near
    return a, b


def part_scan(a, b, a_ref, b_ref, reverse):
    seqs, rows, lanes = a.shape
    tiles = rows // 8
    a, b = tile_scan(a.reshape(seqs * tiles, 8, lanes), b.reshape(seqs * tiles, 8, lanes), reverse)
    a = a.reshape(seqs, tiles, 8, lanes)
    b = b.reshape(seqs, tiles, 8, lanes)
    a_run = b_run = None
    edge = 0 if reverse else 7
    for i in range(tiles):
        t = tiles - 1 - i if reverse else i
        at, bt = a[:, t], b[:, t]
        if a_run is not None:
            bt = bt + at * b_run
            at = at * a_run
        a_ref[:, t * 8 : (t + 1) * 8, :] = at
        b_ref[:, t * 8 : (t + 1) * 8, :] = bt
        a_run, b_run = at[:, edge : edge + 1, :], bt[:, edge : edge + 1, :]
    return a_run[:, 0, :], b_run[:, 0, :]


def gates_kernel(seqs, n_ref, w_ref, dw_ref, iw_ref, vec_ref,
                 cin_ref, low_ref, rec_ref, inj_ref, prod_ref, loc_ref, ends_ref):
    cin = jnp.dot(n_ref[...], w_ref[...], preferred_element_type=F32).astype(BF16)
    cin_ref[...] = cin
    x = cin.astype(F32)
    ext, lanes = x.shape
    taps = vec_ref[...]
    y = taps[4:5, :] + taps[0:1, :] * x
    for k in range(1, 4):
        y = y + taps[k : k + 1, :] * pltpu.roll(x, k, 0)
    y = y.reshape(seqs, ext // seqs, lanes)[:, PAD:, :]
    low = y.astype(BF16)
    low_ref[...] = low
    shape = y.shape
    low2 = low.reshape(shape[0] * shape[1], lanes)
    dpre = jnp.dot(low2, dw_ref[...], preferred_element_type=F32)
    ipre = jnp.dot(low2, iw_ref[...], preferred_element_type=F32)
    recur = jax.nn.sigmoid(dpre + taps[5:6, :])
    inject = jax.nn.sigmoid(ipre + taps[6:7, :])
    rate, em = decay_terms(recur, taps[7:8, :])
    recur = recur.reshape(shape)
    inject = inject.reshape(shape)
    rec_ref[...] = recur
    inj_ref[...] = inject
    injected = jnp.sqrt(em).reshape(shape) * inject * low.astype(F32)
    pa, pb = part_scan(rate.reshape(shape), injected, prod_ref, loc_ref, False)
    ends_ref[0:seqs, :] = pa
    ends_ref[seqs : 2 * seqs, :] = pb


def mix_kernel(heads, loc_ref, prod_ref, bp_ref, carry_ref, w_ref, x_ref, gain_ref,
               state_ref, mixed_ref, mid_ref, feed_ref, acc_ref):
    h = pl.program_id(0)
    carry = carry_ref[...][:, None, :]
    state = loc_ref[...] + prod_ref[...] * carry
    state_ref[...] = state
    mixed = (state * gelu_only(bp_ref[...])).astype(BF16)
    mixed_ref[...] = mixed
    b, s, lanes = mixed.shape
    part = jnp.dot(mixed.reshape(b * s, lanes), w_ref[...], preferred_element_type=F32)

    @pl.when(h == 0)
    def _():
        acc_ref[...] = x_ref[...].astype(F32) + part

    @pl.when(h > 0)
    def _():
        acc_ref[...] += part

    @pl.when(h == heads - 1)
    def _():
        mid = acc_ref[...]
        mid_ref[...] = mid
        feed_ref[...] = (mid * norm_inverse(mid) * gain_ref[...]).astype(BF16)


def back_scan_kernel(seqs, g_ref, w_ref, bp_ref, state_ref, rec_ref, vec_ref,
                     prod_ref, adj_ref, gbp_ref, ends_ref):
    gm = lax.dot_general(g_ref[...], w_ref[...], (((1,), (1,)), ((), ())), preferred_element_type=F32)
    rows, lanes = gm.shape
    shape = (seqs, rows // seqs, lanes)
    act, slope = gelu_and_slope(bp_ref[...])
    gm = gm.reshape(shape)
    gbp = gm * state_ref[...] * slope
    gbp = jnp.concatenate([jnp.zeros((seqs, PAD, lanes), F32), gbp], axis=1)
    gbp_ref[...] = gbp.reshape(seqs * (shape[1] + PAD), lanes).astype(BF16)
    rate = jnp.exp((-RATE_SCALE) * rec_ref[...] * vec_ref[7:8, :])
    after = pltpu.roll(rate.reshape(rows, lanes), rows - 1, 0).reshape(shape)
    row = lax.broadcasted_iota(jnp.int32, shape, 1)
    after = jnp.where(row == shape[1] - 1, 1.0, after)
    pa, pb = part_scan(after, gm * act, prod_ref, adj_ref, True)
    first = rate[:, 0, :]
    ends_ref[0:seqs, :] = first * pa
    ends_ref[seqs : 2 * seqs, :] = first * pb


def back_gates_kernel(heads, prod_ref, adj_ref, carry_ref, state_ref, sin_ref, rec_ref, inj_ref, low_ref,
                      cin_ref, vec_ref, dw_ref, iw_ref, gbp_ref, bw_ref, cw_ref,
                      gcin_ref, gdw_ref, giw_ref, gvec_ref, gn_ref):
    h = pl.program_id(0)
    vec = vec_ref[...]
    soft = vec[7:8, :]
    adj = adj_ref[...] + prod_ref[...] * carry_ref[...][:, None, :]
    shape = adj.shape
    seqs, rows, lanes = shape
    flat = (seqs * rows, lanes)
    state = state_ref[...]
    prev = pltpu.roll(state.reshape(flat), 1, 0).reshape(shape)
    row = lax.broadcasted_iota(jnp.int32, shape, 1)
    prev = jnp.where(row == 0, sin_ref[...][:, None, :], prev)
    recur, inject = rec_ref[...], inj_ref[...]
    rate, em = decay_terms(recur, soft)
    mult = jnp.sqrt(em)
    low = low_ref[...]
    conv = low.astype(F32)
    g_log = adj * prev * rate - adj * inject * conv * (rate * rate) / mult
    am = adj * mult
    g_elem = am * inject
    g_rec = g_log * ((-RATE_SCALE) * soft)
    g_soft = jnp.sum((g_log * recur).reshape(flat), axis=0, keepdims=True) * (-RATE_SCALE)
    gdp = (g_rec * recur * (1.0 - recur)).reshape(flat)
    gip = (am * conv * inject * (1.0 - inject)).reshape(flat)
    gdp_low, gip_low = gdp.astype(BF16), gip.astype(BF16)
    low2 = low.reshape(flat)
    tok = (((0,), (0,)), ((), ()))
    last = (((1,), (1,)), ((), ()))
    gdw_ref[...] = lax.dot_general(low2, gdp_low, tok, preferred_element_type=F32).astype(BF16)
    giw_ref[...] = lax.dot_general(low2, gip_low, tok, preferred_element_type=F32).astype(BF16)
    gc = (
        g_elem.reshape(flat)
        + lax.dot_general(gdp_low, dw_ref[...], last, preferred_element_type=F32)
        + lax.dot_general(gip_low, iw_ref[...], last, preferred_element_type=F32)
    )
    gce = jnp.concatenate([jnp.zeros((seqs, PAD, lanes), F32), gc.reshape(shape)], axis=1)
    ext = seqs * (rows + PAD)
    gce = gce.reshape(ext, lanes)
    x = cin_ref[...].astype(F32)
    out = vec[0:1, :] * gce
    sums = [jnp.sum(gce * x, axis=0, keepdims=True)]
    for k in range(1, 4):
        out = out + vec[k : k + 1, :] * pltpu.roll(gce, ext - k, 0)
        sums.append(jnp.sum(gce * pltpu.roll(x, k, 0), axis=0, keepdims=True))
    sums.append(jnp.sum(gce, axis=0, keepdims=True))
    sums.append(jnp.sum(gdp, axis=0, keepdims=True))
    sums.append(jnp.sum(gip, axis=0, keepdims=True))
    sums.append(g_soft)
    for i, v in enumerate(sums):
        gvec_ref[i : i + 1, :] = v
    gcin = out.astype(BF16)
    gcin_ref[...] = gcin
    part = lax.dot_general(gcin, cw_ref[...], last, preferred_element_type=F32)
    part += lax.dot_general(gbp_ref[...], bw_ref[...], last, preferred_element_type=F32)

    @pl.when(h == 0)
    def _():
        gn_ref[...] = part

    @pl.when(h > 0)
    def _():
        gn_ref[...] += part


def carry_kernel(seqs, n_seq, n_mlp, reverse, ends_ref, out_ref, zbuf, sbuf, total, ssem, rsem):
    ms, mz = lax.axis_index("seq"), lax.axis_index("mlp")
    barrier = pltpu.get_barrier_semaphore()
    for d in range(1, n_mlp):
        pl.semaphore_signal(barrier, inc=1, device_id=(ms, lax.rem(mz + d, n_mlp)), device_id_type=MESH)
    for d in range(1, n_seq):
        pl.semaphore_signal(barrier, inc=1, device_id=(lax.rem(ms + d, n_seq), mz), device_id_type=MESH)
    pl.semaphore_wait(barrier, n_mlp + n_seq - 2)
    copies = []
    for d in range(1, n_mlp):
        copies.append(pltpu.make_async_remote_copy(
            src_ref=ends_ref, dst_ref=zbuf.at[mz], send_sem=ssem.at[d - 1], recv_sem=rsem.at[d - 1],
            device_id=(ms, lax.rem(mz + d, n_mlp)), device_id_type=MESH))
        copies[-1].start()
    zbuf[mz] = ends_ref[...]
    for c in copies:
        c.wait()
    shape = (seqs, ends_ref.shape[1])
    tp, ts = jnp.ones(shape, F32), jnp.zeros(shape, F32)
    pp, ps = tp, ts
    for i in range(n_mlp):
        z = n_mlp - 1 - i if reverse else i
        val = zbuf[z]
        p, s = val[0:seqs, :], val[seqs : 2 * seqs, :]
        ts = p * ts + s
        tp = p * tp
        mine = jnp.where((z > mz) if reverse else (z < mz), 1.0, 0.0)
        ps = mine * (p * ps + s) + (1.0 - mine) * ps
        pp = (mine * p + (1.0 - mine)) * pp
    total[0:seqs, :] = tp
    total[seqs : 2 * seqs, :] = ts
    copies = []
    for d in range(1, n_seq):
        i = n_mlp - 2 + d
        copies.append(pltpu.make_async_remote_copy(
            src_ref=total, dst_ref=sbuf.at[ms], send_sem=ssem.at[i], recv_sem=rsem.at[i],
            device_id=(lax.rem(ms + d, n_seq), mz), device_id_type=MESH))
        copies[-1].start()
    sbuf[ms] = total[...]
    for c in copies:
        c.wait()
    c = jnp.zeros(shape, F32)
    for i in range(n_seq):
        q = n_seq - 1 - i if reverse else i
        val = sbuf[q]
        p, s = val[0:seqs, :], val[seqs : 2 * seqs, :]
        mine = jnp.where((q > ms) if reverse else (q < ms), 1.0, 0.0)
        c = mine * (p * c + s) + (1.0 - mine) * c
    out_ref[...] = pp * c + ps


def carry_call(ends, seqs, n_seq, n_mlp, reverse):
    rows, width = ends.shape
    n = n_seq + n_mlp - 2
    return pl.pallas_call(
        functools.partial(carry_kernel, seqs, n_seq, n_mlp, reverse),
        out_shape=jax.ShapeDtypeStruct((seqs, width), F32),
        in_specs=[pl.BlockSpec(memory_space=pltpu.VMEM)],
        out_specs=pl.BlockSpec(memory_space=pltpu.VMEM),
        scratch_shapes=[
            pltpu.VMEM((n_mlp, rows, width), F32),
            pltpu.VMEM((n_seq, rows, width), F32),
            pltpu.VMEM((rows, width), F32),
            pltpu.SemaphoreType.DMA((n,)),
            pltpu.SemaphoreType.DMA((n,)),
        ],
        compiler_params=pltpu.CompilerParams(
            collective_id=1 if reverse else 0, has_side_effects=True, vmem_limit_bytes=VMEM_LIMIT
        ),
        cost_estimate=pl.CostEstimate(flops=0, bytes_accessed=200 * rows * width * 4, transcendentals=0),
        name="carry_back" if reverse else "carry_fwd",
    )(ends)


def chip_orders(n_seq):
    chips = list(range(1, n_seq.bit_length() - 1))
    turn = len(chips) // 2
    return chips, chips[turn:] + chips[:turn]


def owners_stages(n_seq):
    halves = []
    for order in chip_orders(n_seq):
        left = list(range(n_seq.bit_length() - 1))[::-1]
        stages = []
        for bit in order:
            pos = left.index(bit)
            stages.append((bit, 1 << pos, 1 << (len(left) - 1 - pos)))
            left.remove(bit)
        halves.append(stages)
    return halves


def owners_scratch(n_seq, n_mlp, rows, cols):
    nh = n_mlp // 2
    shapes = []
    for stages in owners_stages(n_seq):
        for i in range(len(stages)):
            blocks = n_seq >> (i + 1)
            shapes.append(pltpu.VMEM((blocks, nh, rows, cols), BF16))
            if i < len(stages) - 1:
                shapes.append(pltpu.VMEM((blocks, nh, rows, cols), BF16))
        shapes.append(pltpu.VMEM((n_seq // 2, nh, rows, cols), BF16))
    shapes.append(pltpu.VMEM((2, n_mlp, rows, cols), BF16))
    shapes.append(pltpu.VMEM((n_mlp - 1, 2, rows, cols), BF16))
    shapes.append(pltpu.VMEM((2, rows, cols), F32))
    shapes.append(pltpu.VMEM((rows, cols), BF16))
    shapes.append(pltpu.VMEM((rows, cols), BF16))
    return shapes


def owners_kernel(n_seq, n_mlp, count, per, n_sem, *refs):
    ms, mz = lax.axis_index("seq"), lax.axis_index("mlp")
    arrays, vec = refs[:count], refs[count]
    outs, vec_out = refs[count + 1 : 2 * count + 1], refs[2 * count + 1]
    scratch = refs[2 * count + 2 :]
    vec_in, vec_sum, ssem, rsem = scratch[-4:]
    n_bits = n_seq.bit_length() - 1
    mine = lambda bit: lax.rem(lax.div(ms, 1 << bit), 2)
    seq_peer = lambda bit: (ms + (1 - 2 * mine(bit)) * (1 << bit), mz)
    core = mine(0)
    used = [0]

    barrier = pltpu.get_barrier_semaphore()
    for bit in range(n_bits):
        pl.semaphore_signal(barrier, inc=1, device_id=seq_peer(bit), device_id_type=MESH)
    for d in range(1, n_mlp):
        pl.semaphore_signal(barrier, inc=1, device_id=(ms, lax.rem(mz + d, n_mlp)), device_id_type=MESH)
    pl.semaphore_wait(barrier, n_bits + n_mlp - 1)

    def send(src, dst, peer):
        i = used[0]
        used[0] += 1
        c = pltpu.make_async_remote_copy(
            src_ref=src, dst_ref=dst, send_sem=ssem.at[i], recv_sem=rsem.at[i],
            device_id=peer, device_id_type=MESH)
        c.start()
        return c

    def load(src, dst):
        i = used[0]
        used[0] += 1
        c = pltpu.make_async_copy(src, dst, rsem.at[i])
        c.start()
        return c

    nh = n_mlp // 2
    all_stages = owners_stages(n_seq)
    n_stages = n_bits - 1
    state, sent = [], []
    for a in range(count):
        bufs = list(scratch[a * per : (a + 1) * per])
        st = {"recv": [[], []], "sum": [[], []], "own": [None, None]}
        for h in range(2):
            for i in range(n_stages):
                st["recv"][h].append(bufs.pop(0))
                st["sum"][h].append(bufs.pop(0) if i < n_stages - 1 else None)
            st["own"][h] = bufs.pop(0)
        st["fin"], st["zrecv"], st["zsum"], st["csend"], st["crecv"] = bufs
        state.append(st)

    def stage_start(a, i):
        st = state[a]
        st["wait"] = []
        for h in range(2):
            bit, runs, length = all_stages[h][i]
            for j in range(runs):
                away = (2 * j + 1 - mine(bit)) * length
                home = (2 * j + mine(bit)) * length
                dst = st["recv"][h][i].at[pl.ds(j * length, length)]
                if i == 0:
                    src = arrays[a].at[pl.ds(away, length), pl.ds(h * nh, nh)]
                    st["wait"].append(load(
                        arrays[a].at[pl.ds(home, length), pl.ds(h * nh, nh)],
                        st["own"][h].at[pl.ds(j * length, length)]))
                else:
                    src = st["sum"][h][i - 1].at[pl.ds(away, length)]
                st["wait"].append(send(src, dst, seq_peer(bit)))

    def stage_end(a, i):
        st = state[a]
        for c in st["wait"]:
            c.wait()
        for h in range(2):
            bit, runs, length = all_stages[h][i]
            recv = st["recv"][h][i]
            for j in range(runs):
                home = (2 * j + mine(bit)) * length

                def add(t, _):
                    b, q = lax.div(t, nh), lax.rem(t, nh)
                    to = j * length + b
                    if i == 0:
                        kept = st["own"][h][to, q]
                    else:
                        kept = st["sum"][h][i - 1][home + b, q]
                    v = (kept.astype(F32) + recv[to, q].astype(F32)).astype(BF16)
                    if i == n_stages - 1:
                        st["fin"][to, h * nh + q] = v
                    else:
                        st["sum"][h][i][to, q] = v
                    return 0

                lax.fori_loop(0, length * nh, add, 0)

    def mlp_start(a):
        st = state[a]
        st["wait"] = []
        for d in range(1, n_mlp):
            z = lax.rem(mz + d, n_mlp)
            st["wait"].append(send(st["fin"].at[:, z], st["zrecv"].at[d - 1], (ms, z)))

    def mlp_end(a):
        st = state[a]
        for c in st["wait"]:
            c.wait()
        for k in range(2):
            v = st["fin"][k, mz].astype(F32)
            for d in range(1, n_mlp):
                v = v + st["zrecv"][d - 1, k].astype(F32)
            st["zsum"][k] = v
        outs[a][core] = st["zsum"][core]
        st["csend"][...] = st["zsum"][1 - core].astype(BF16)
        st["wait"] = [send(st["csend"], st["crecv"], seq_peer(0))]

    def core_end(a):
        st = state[a]
        for c in st["wait"]:
            c.wait()
        outs[a][1 - core] = st["crecv"][...].astype(F32)

    vec_peers = []
    for bit in range(n_mlp.bit_length() - 1):
        side = lax.rem(lax.div(mz, 1 << bit), 2)
        vec_peers.append((ms, mz + (1 - 2 * side) * (1 << bit)))
    vec_peers += [seq_peer(bit) for bit in range(n_bits)]
    vec_state = [None, 0]

    def vec_step():
        copy, i = vec_state
        if copy is not None:
            copy.wait()
            before = vec[...] if i == 1 else vec_sum[i - 2]
            v = before + vec_in[i - 1]
            if i == len(vec_peers):
                vec_out[...] = v
            else:
                vec_sum[i - 1] = v
        vec_state[0] = None
        if i < len(vec_peers):
            src = vec if i == 0 else vec_sum.at[i - 1]
            vec_state[:] = [send(src, vec_in.at[i], vec_peers[i]), i + 1]

    ends = [functools.partial(stage_end, i=i) for i in range(n_stages)] + [mlp_end, core_end]
    starts = [functools.partial(stage_start, i=i) for i in range(n_stages)] + [mlp_start]
    ahead = 1
    for a in range(min(ahead + 1, count)):
        starts[0](a)
    vec_step()
    for t in range(count + len(ends) - 1):
        for i, end in enumerate(ends):
            a = t - i
            if 0 <= a < count:
                end(a)
                if i + 1 < len(starts):
                    starts[i + 1](a)
                if i == 0 and a + ahead + 1 < count:
                    starts[0](a + ahead + 1)
        vec_step()
    while vec_state[0] is not None:
        vec_step()


def owners_call(arrays, vec, n_seq, n_mlp):
    scratch, moves = [], 0
    for v in arrays:
        bufs = owners_scratch(n_seq, n_mlp, v.shape[2], v.shape[3])
        per = len(bufs)
        scratch += bufs
    for stages in owners_stages(n_seq):
        moves += sum(runs for _, runs, _ in stages) + stages[0][1]
    steps = (n_mlp.bit_length() - 1) + (n_seq.bit_length() - 1)
    n_sem = len(arrays) * (moves + n_mlp - 1 + 1) + steps
    vmem = pl.BlockSpec(memory_space=pltpu.VMEM)
    outs = pl.pallas_call(
        functools.partial(owners_kernel, n_seq, n_mlp, len(arrays), per, n_sem),
        out_shape=[jax.ShapeDtypeStruct((2,) + v.shape[2:], F32) for v in arrays]
        + [jax.ShapeDtypeStruct(vec.shape, F32)],
        in_specs=[pl.BlockSpec(memory_space=pl.ANY)] * len(arrays) + [vmem],
        out_specs=[vmem] * (len(arrays) + 1),
        scratch_shapes=scratch + [
            pltpu.VMEM((steps,) + vec.shape, F32),
            pltpu.VMEM((steps,) + vec.shape, F32),
            pltpu.SemaphoreType.DMA((n_sem,)),
            pltpu.SemaphoreType.DMA((n_sem,)),
        ],
        compiler_params=pltpu.CompilerParams(
            collective_id=2, has_side_effects=True, vmem_limit_bytes=56 << 20
        ),
        name="owners",
    )(*arrays, vec)
    return outs[:-1], outs[-1]


def assemble_kernel(places, rows, *refs):
    pieces, out, held, got, sent = refs[: len(places)], refs[-4], refs[-3], refs[-2], refs[-1]
    me = lax.axis_index("seq")
    loads, stores = [], []
    for i in range(len(places)):
        loads.append(pltpu.make_async_copy(pieces[i], held.at[i], got.at[i]))
        loads[-1].start()
    for i, (mask, part) in enumerate(places):
        loads[i].wait()
        at = pl.multiple_of(((me ^ mask) * 2 + part) * rows, 8)
        stores.append(pltpu.make_async_copy(held.at[i], out.at[pl.ds(at, rows), :], sent.at[i]))
        stores[-1].start()
    for c in stores:
        c.wait()


def assemble(n, parts):
    rows, cols = parts[0][2].shape
    size = 2 * n * rows * cols
    return pl.pallas_call(
        functools.partial(assemble_kernel, [p[:2] for p in parts], rows),
        out_shape=jax.ShapeDtypeStruct((2 * n * rows, cols), parts[0][2].dtype),
        in_specs=[pl.BlockSpec(memory_space=pl.ANY)] * len(parts),
        out_specs=pl.BlockSpec(memory_space=pl.ANY),
        scratch_shapes=[pltpu.VMEM((len(parts), rows, cols), parts[0][2].dtype),
                        pltpu.SemaphoreType.DMA((len(parts),)), pltpu.SemaphoreType.DMA((len(parts),))],
        compiler_params=pltpu.CompilerParams(vmem_limit_bytes=VMEM_LIMIT),
        cost_estimate=pl.CostEstimate(flops=0, bytes_accessed=4 * size, transcendentals=0),
        name="assemble",
    )(*[p[2] for p in parts])


class Seq:
    def __init__(self):
        self.n = lax.axis_size("seq")
        self.me = lax.axis_index("seq")
        self.bits = list(range(self.n.bit_length() - 1))
        chips = self.bits[1:]
        turn = len(chips) // 2
        self.orders = (chips, chips[turn:] + chips[:turn])

    def mine(self, bit):
        return (self.me >> bit) & 1

    def swap(self, v, bit):
        return lax.ppermute(v, "seq", [(i, i ^ (1 << bit)) for i in range(self.n)])

    def spread_start(self, g):
        half = g.shape[0] // 2
        return [[(0, g[:half])], [(0, g[half:])]]

    def spread_next(self, halves, stage):
        return [
            have + [(mask | (1 << order[stage]), self.swap(v, order[stage])) for mask, v in have]
            for have, order in zip(halves, self.orders)
        ]

    def spread_core(self, halves, before=None):
        places, pieces = [], []
        for i, have in enumerate(halves):
            places += [(mask, i) for mask, _ in have] + [(mask | 1, i) for mask, _ in have]
            pieces += [v for _, v in have] + [self.swap(v, 0) for _, v in have]
        if before is not None:
            pieces = behind(before, pieces)
        return assemble(self.n, [p + (v,) for p, v in zip(places, pieces)])

    def spread_mlp(self, v):
        n = lax.axis_size("mlp")
        me = lax.axis_index("mlp")
        got = [v] + [
            lax.ppermute(v, "mlp", [(i, (i + d) % n) for i in range(n)]) for d in range(1, n)
        ]
        out = []
        for z in range(n):
            block = got[0]
            for d in range(1, n):
                block = jnp.where(lax.rem(me - z + n, n) == d, got[d], block)
            out.append(block)
        return jnp.stack(out)

    def gather_small(self, g):
        rel = g[None]
        order = self.bits[1:] + [0]
        for bit in order:
            rel = jnp.concatenate([rel, self.swap(rel, bit)], axis=0)
        out = []
        for q in range(self.n):
            e = sum((((q ^ self.me) >> bit) & 1) << i for i, bit in enumerate(order))
            out.append(lax.dynamic_index_in_dim(rel, e, 0, keepdims=False))
        return jnp.concatenate(out, axis=0)

    def scatter_send(self, v, left, bit, keep_from=None):
        pos = left.index(bit)
        shape = (1 << pos, 2, 1 << (len(left) - 1 - pos)) + v.shape[1:]

        def pick(u, side):
            u = lax.dynamic_index_in_dim(u.reshape(shape), side, 1, keepdims=False)
            return u.reshape((-1,) + v.shape[1:])

        got = self.swap(pick(v, 1 - self.mine(bit)), bit)
        keep = pick(v if keep_from is None else keep_from, self.mine(bit))
        return keep, got, [b for b in left if b != bit]

    def scatter_start(self, v, left, keep_from=None):
        half = v.shape[1] // 2
        state = []
        for i, order in enumerate(self.orders):
            rows = slice(i * half, (i + 1) * half)
            base = None if keep_from is None else keep_from[:, rows]
            state.append(self.scatter_send(v[:, rows], left, order[0], base) + (order[1:],))
        return state

    def scatter_next(self, state, kind=BF16):
        sums = [(keep.astype(F32) + got.astype(F32)) for keep, got, _, _ in state]
        if not state[0][3]:
            return jnp.concatenate([v.astype(kind) for v in sums], axis=1)
        return [
            self.scatter_send(v.astype(BF16), left, order[0]) + (order[1:],)
            for v, (_, _, left, order) in zip(sums, state)
        ]

    def scatter_finish(self, state, kind=BF16):
        while isinstance(state, list):
            state = self.scatter_next(state, kind)
        return state

    def butterfly(self, v):
        n_mlp = lax.axis_size("mlp")
        for bit in range(n_mlp.bit_length() - 1):
            v = v + lax.ppermute(v, "mlp", [(i, i ^ (1 << bit)) for i in range(n_mlp)])
        for bit in self.bits:
            v = v + self.swap(v, bit)
        return v


def behind(token, values):
    return lax.optimization_barrier((token, values))[1]


def halves_behind(token, halves):
    pieces = behind(token, [[v for _, v in have] for have in halves])
    return [[(m, p) for (m, _), p in zip(have, ps)] for have, ps in zip(halves, pieces)]


def states_behind(token, states):
    gots = behind(token, [[e[1] for e in state] for state in states])
    return [[(e[0], g) + e[2:] for e, g in zip(state, got)] for state, got in zip(states, gots)]


def gots_of(states):
    return [[e[1] for e in state] for state in states]


def flat_dot(left, right):
    shape = left.shape
    out = jnp.dot(left.reshape(-1, shape[-1]), right, preferred_element_type=F32)
    return out.reshape(shape[:-1] + (right.shape[1],))


def dot_against(left, right):
    shape = left.shape
    out = lax.dot_general(
        left.reshape(-1, shape[-1]), right, (((1,), (1,)), ((), ())), preferred_element_type=F32
    )
    return out.reshape(shape[:-1] + (right.shape[0],))


def outer_sum(left, right):
    return lax.dot_general(
        left.reshape(-1, left.shape[-1]),
        right.reshape(-1, right.shape[-1]),
        (((0,), (0,)), ((), ())),
        preferred_element_type=F32,
    )


def gated_unit(gate_pre, up_pre):
    return jax.nn.gelu(gate_pre) * up_pre


def norm_back(values, inverse, gain, upstream):
    scaled = upstream * gain
    gain_grad = jnp.sum(upstream * values * inverse, axis=(0, 1))
    inner_mean = jnp.mean(scaled * values, axis=-1, keepdims=True)
    return (inverse * (scaled - values * inner_mean * inverse * inverse), gain_grad)


def per_device(inputs, mixer_gain, branch_weight, input_weight, conv_weight, conv_bias, decay_weight,
               decay_bias, inject_weight, inject_bias, decay_param, output_weight, feed_gain,
               feed_gate, feed_up, feed_down, cotangent):
    both = ("seq", "mlp")
    seq = Seq()
    n_seq, n_mlp = seq.n, lax.axis_size("mlp")
    n_dev = n_seq * n_mlp
    seqs, rows, width = inputs.shape
    taps, r_own = conv_weight.shape
    edge = taps - 1
    head = decay_weight.shape[1]
    r_all = r_own * n_dev
    heads = r_all // head
    d_own = width // n_dev
    ext_rows = rows + PAD
    ext = seqs * ext_rows
    tokens = seqs * rows

    lanes = 128
    small = [conv_weight.T, conv_bias[:, None], decay_bias[:, None], inject_bias[:, None], decay_param[:, None]]
    gains = [jnp.pad(g, (0, r_own - d_own))[:, None] for g in (mixer_gain, feed_gain)]
    small = jnp.concatenate(small + gains, axis=1)
    small = jnp.pad(small, ((0, 0), (0, lanes - small.shape[1])))
    gates_own = jnp.concatenate([decay_weight, inject_weight, small], axis=1)
    fold = gates_own.size // r_all
    first = seq.spread_mlp(jnp.concatenate([input_weight, gates_own.reshape(fold, r_all)], axis=0))
    branch_own, output_own, cot_own = behind(first, (branch_weight, output_weight, cotangent))
    branch_rows = lax.all_gather(branch_own, "mlp", axis=0, tiled=True)
    output_rows = lax.all_gather(output_own, "mlp", axis=0, tiled=True)
    grad_rows = lax.all_gather(cot_own, "mlp", axis=1, tiled=True)
    stages = len(seq.bits) - 1
    gates_all = seq.gather_small(first[:, d_own:].reshape(n_mlp * r_own, 2 * head + lanes))
    input_halves = seq.spread_start(first[:, :d_own].reshape(n_mlp * d_own, r_all))
    branch_halves = seq.spread_start(branch_rows)
    output_halves = seq.spread_start(output_rows)
    for i in range(stages):
        input_halves = seq.spread_next(input_halves, i)
    vectors = gates_all[:, 2 * head :].astype(F32)
    gain_rows = vectors[:, 8:10].reshape(n_dev, r_own, 2)[:, :d_own, :].reshape(width, 2)
    gain_mixer, gain_feed = gain_rows[:, 0], gain_rows[:, 1]
    param = vectors[:, 7]
    vec = jnp.concatenate([vectors[:, :7].T, jax.nn.softplus(-param)[None, :]], axis=0)

    last_tokens = lax.ppermute(inputs[:, rows - edge :, :], both, [(i, i + 1) for i in range(n_dev - 1)])
    x_ext = jnp.concatenate(
        [jnp.zeros((seqs, PAD - edge, width), BF16), last_tokens, inputs], axis=1
    )
    stream_ext = x_ext.astype(F32)
    inverse_ext = norm_inverse(stream_ext)
    normed_ext = (stream_ext * inverse_ext * gain_mixer).astype(BF16).reshape(ext, width)

    full_input = seq.spread_core(input_halves, (normed_ext, vec, gates_all))
    for i in range(stages - 1):
        branch_halves = seq.spread_next(branch_halves, i)
    full_input = behind((output_rows, [[v for _, v in have] for have in branch_halves]), full_input)
    branch_halves = seq.spread_next(branch_halves, stages - 1)

    params = lambda **k: pltpu.CompilerParams(dimension_semantics=("arbitrary",), vmem_limit_bytes=VMEM_LIMIT, **k)

    def cost(big_dots, arrays):
        whole_mats = 2 * ext * width * r_all
        return pl.CostEstimate(
            flops=big_dots * whole_mats,
            bytes_accessed=big_dots * 2 * width * r_all + arrays * 4 * tokens * r_all,
            transcendentals=4 * tokens * r_all,
        )

    tok_head = pl.BlockSpec((seqs, rows, head), lambda h: (0, 0, h))
    ext_head = pl.BlockSpec((ext, head), lambda h: (0, h))
    vec_head = pl.BlockSpec((8, head), lambda h: (0, h))
    seq_head = pl.BlockSpec((seqs, head), lambda h: (0, h))
    col_head = pl.BlockSpec((width, head), lambda h: (0, h))
    row_head = pl.BlockSpec((head, width), lambda h: (h, 0))
    decay_head = pl.BlockSpec((head, head), lambda h: (h, 0))
    inject_head = pl.BlockSpec((head, head), lambda h: (h, 1))
    whole = lambda *shape: pl.BlockSpec(shape, lambda h: (0,) * len(shape))
    tok = lambda kind: jax.ShapeDtypeStruct((seqs, rows, r_all), kind)
    struct = jax.ShapeDtypeStruct

    conv_in, conv_low, recur, inject, prod, local, ends = pl.pallas_call(
        functools.partial(gates_kernel, seqs),
        grid=(heads,),
        in_specs=[whole(ext, width), col_head, decay_head, inject_head, vec_head],
        out_specs=[ext_head, tok_head, tok_head, tok_head, tok_head, tok_head,
                   pl.BlockSpec((2 * seqs, head), lambda h: (0, h))],
        out_shape=[struct((ext, r_all), BF16), tok(BF16), tok(F32), tok(F32), tok(F32), tok(F32),
                   struct((2 * seqs, r_all), F32)],
        compiler_params=params(),
        cost_estimate=cost(1, 20),
        name="gates",
    )(normed_ext, full_input, gates_all, gates_all, vec)

    for i in range(stages - 1):
        output_halves = seq.spread_next(output_halves, i)
    arrived = [[v for _, v in have] for have in output_halves]
    output_halves = halves_behind(ends, output_halves)
    ends = behind(arrived, ends)
    output_halves = seq.spread_next(output_halves, stages - 1)
    state_in = carry_call(ends, seqs, n_seq, n_mlp, False)
    full_branch = seq.spread_core(halves_behind(state_in, branch_halves))
    full_output = seq.spread_core(halves_behind(full_branch, output_halves))
    normed = normed_ext.reshape(seqs, ext_rows, width)[:, PAD:, :]
    branch_pre = flat_dot(normed, full_branch)

    state, mixed, mid, feed_low = pl.pallas_call(
        functools.partial(mix_kernel, heads),
        grid=(heads,),
        in_specs=[tok_head, tok_head, tok_head, seq_head, row_head, whole(tokens, width), whole(1, width)],
        out_specs=[tok_head, tok_head, whole(tokens, width), whole(tokens, width)],
        out_shape=[tok(F32), tok(BF16), struct((tokens, width), F32), struct((tokens, width), BF16)],
        scratch_shapes=[pltpu.VMEM((tokens, width), F32)],
        compiler_params=params(),
        cost_estimate=cost(1, 12),
        name="mix",
    )(local, prod, branch_pre, state_in, full_output, inputs.reshape(tokens, width), gain_feed[None, :])
    stream_mid = mid.reshape(seqs, rows, width)

    n_chunks = 2 if seqs % 2 == 0 else 1
    per = seqs // n_chunks
    chunk = lambda v, c: v[c * per : (c + 1) * per]
    feed_own = behind(grad_rows, feed_low.reshape(seqs, rows, width))
    row_major = lambda v: with_layout_constraint(v, Layout(major_to_minor=tuple(range(v.ndim))))
    grad_hidden = [dot_against(chunk(grad_rows, c), feed_down) for c in range(n_chunks)]
    feed_rows, hidden, gate_low, up_low, feed_norm_grad = [], [], [], [], []
    for c in range(n_chunks):
        f = row_major(lax.all_gather(chunk(feed_own, c), "mlp", axis=1, tiled=True))
        if c == 0:
            f, grad_hidden = lax.optimization_barrier((f, grad_hidden))
        else:
            f, back = lax.optimization_barrier((f, back))
            feed_norm_grad.append(lax.psum_scatter(back, "mlp", scatter_dimension=1, tiled=True))
        gate_pre = flat_dot(f, feed_gate)
        up_pre = flat_dot(f, feed_up)
        hidden.append(gated_unit(gate_pre, up_pre).astype(BF16))
        gate_grad, up_grad = jax.vjp(gated_unit, gate_pre, up_pre)[1](grad_hidden[c])
        gate_low.append(gate_grad.astype(BF16))
        up_low.append(up_grad.astype(BF16))
        feed_rows.append(f)
        back = (dot_against(gate_low[-1], feed_gate) + dot_against(up_low[-1], feed_up)).astype(BF16)
    feed_norm_grad.append(lax.psum_scatter(back, "mlp", scatter_dimension=1, tiled=True))
    feed_rows, hidden, gate_low, up_low = (
        jnp.concatenate(v, axis=0) for v in (feed_rows, hidden, gate_low, up_low)
    )
    feed_out = flat_dot(hidden, feed_down).astype(BF16)
    chip_grads = []
    for left, right in ((feed_rows, gate_low), (feed_rows, up_low), (grad_rows, hidden)):
        g = row_major(outer_sum(left, right).astype(BF16)).reshape(n_seq, width // n_seq, feed_gate.shape[1])
        keep, got, chip_bits = seq.scatter_send(g, seq.bits[::-1], 0)
        chip_grads.append((keep.astype(F32) + got.astype(F32)).astype(BF16))
    feed_norm_grad, feed_out, kept = lax.optimization_barrier((feed_norm_grad, feed_out, chip_grads))
    feed_states = [seq.scatter_start(g, chip_bits, k) for g, k in zip(chip_grads, kept)]
    feed_norm_grad = jnp.concatenate(feed_norm_grad, axis=0).astype(F32)
    feed_out = lax.psum_scatter(feed_out, "mlp", scatter_dimension=1, tiled=True).astype(F32)
    result = (stream_mid + feed_out).astype(BF16)

    feed_inverse = norm_inverse(stream_mid)
    mid_part, feed_gain_grad = norm_back(stream_mid, feed_inverse, gain_feed, feed_norm_grad)
    mid_grad = cotangent.astype(F32) + mid_part
    mid_low = mid_grad.astype(BF16).reshape(tokens, width)

    back_prod, back_local, gbp, back_ends = pl.pallas_call(
        functools.partial(back_scan_kernel, seqs),
        grid=(heads,),
        in_specs=[whole(tokens, width), row_head, tok_head, tok_head, tok_head, vec_head],
        out_specs=[tok_head, tok_head, ext_head, pl.BlockSpec((2 * seqs, head), lambda h: (0, h))],
        out_shape=[tok(F32), tok(F32), struct((ext, r_all), BF16), struct((2 * seqs, r_all), F32)],
        compiler_params=params(),
        cost_estimate=cost(1, 14),
        name="back_scan",
    )(mid_low, full_output, branch_pre, state, recur, vec)
    core = seq.mine(0)

    def pair_operands(left, right):
        half = right.shape[1] // 2
        mine = lax.dynamic_slice_in_dim(right, core * half, half, 1)
        other = lax.dynamic_slice_in_dim(right, (1 - core) * half, half, 1)
        return left, jnp.concatenate([mine, seq.swap(other, 0)], axis=0)

    def pair_grad(left, right):
        g = outer_sum(*pair_operands(left, right)).astype(BF16)
        return g.reshape(n_seq, g.shape[0] // n_seq, g.shape[1])

    arrived = gots_of(feed_states)
    back_ends, arrived = lax.optimization_barrier((back_ends, arrived))
    feed_states = [[(e[0], g) + e[2:] for e, g in zip(st, gs)] for st, gs in zip(feed_states, arrived)]
    feed_states = [seq.scatter_next(st, F32) for st in feed_states]
    mixed_two = mixed.reshape(tokens, r_all)
    mixed_two = jnp.concatenate([mixed_two, seq.swap(mixed_two, 0)], axis=0)
    normed_two = jnp.concatenate([normed_ext, seq.swap(normed_ext, 0)], axis=0)
    output_grad = pair_grad(mixed_two, mid_low)
    back_ends, output_grad = lax.optimization_barrier((back_ends, output_grad))
    adj_in = carry_call(back_ends, seqs, n_seq, n_mlp, True)
    branch_grad = pair_grad(normed_two, gbp)
    adj_in, branch_grad = lax.optimization_barrier((adj_in, branch_grad))
    while isinstance(feed_states[0], list):
        arrived = gots_of(feed_states)
        adj_in, arrived = lax.optimization_barrier((adj_in, arrived))
        feed_states = [[(e[0], g) + e[2:] for e, g in zip(st, gs)] for st, gs in zip(feed_states, arrived)]
        feed_states = [seq.scatter_next(st, F32) for st in feed_states]
    feed_grads = [v[0] for v in feed_states]

    gcin, gdw, giw, gvec, gnorm = pl.pallas_call(
        functools.partial(back_gates_kernel, heads),
        grid=(heads,),
        in_specs=[tok_head, tok_head, seq_head, tok_head, seq_head, tok_head, tok_head, tok_head,
                  ext_head, vec_head, decay_head, inject_head, ext_head, col_head, col_head],
        out_specs=[ext_head, decay_head, decay_head, vec_head, whole(ext, width)],
        out_shape=[struct((ext, r_all), BF16), struct((r_all, head), BF16), struct((r_all, head), BF16),
                   struct((8, r_all), F32), struct((ext, width), F32)],
        compiler_params=params(),
        cost_estimate=cost(2, 20),
        name="back_gates",
    )(back_prod, back_local, adj_in, state, state_in, recur, inject, conv_low,
      conv_in, vec, gates_all, gates_all, gbp, full_branch, full_input)

    weight_grad = pair_grad(normed_two, gcin)
    gates_mine = jnp.where(core == 0, gdw, giw)
    gates_got = seq.swap(jnp.where(core == 0, giw, gdw), 0)
    gates_grad = (gates_mine.astype(F32) + gates_got.astype(F32)).astype(BF16)

    stream_part, mixer_gain_grad = norm_back(
        stream_ext, inverse_ext, gain_mixer, gnorm.reshape(seqs, ext_rows, width)
    )
    next_part = lax.ppermute(
        stream_part[:, PAD - edge : PAD, :], both, [(i + 1, i) for i in range(n_dev - 1)]
    )
    next_part = jnp.pad(next_part, ((0, 0), (rows - edge, 0), (0, 0)))
    input_grad = mid_grad + stream_part[:, PAD:, :] + next_part

    param_grad = gvec[7] * -jax.nn.sigmoid(-param)
    gain_grads = jnp.pad(jnp.stack([mixer_gain_grad, feed_gain_grad]), ((0, 0), (0, r_all - width)))
    total = jnp.concatenate([gvec[:7], param_grad[None, :], gain_grads], axis=0)
    total = jnp.pad(total, ((0, 16 - total.shape[0]), (0, 0)))
    blocks = lambda g: g.reshape(n_seq, n_mlp, -1, g.shape[-1])
    owned, total = owners_call(
        [blocks(g) for g in (output_grad, branch_grad, gates_grad, weight_grad)], total, n_seq, n_mlp
    )
    output_out, branch_out, input_out = (
        jnp.concatenate([v[0], v[1]], axis=1) for v in (owned[0], owned[1], owned[3])
    )
    decay_out, inject_out = owned[2][0], owned[2][1]
    place = seq.me * n_mlp + lax.axis_index("mlp")
    tail = lax.dynamic_slice_in_dim(total[:8], place * r_own, r_own, 1)
    gains_out = lax.dynamic_slice_in_dim(total[8:10], place * d_own, d_own, 1)

    return (
        result,
        input_grad,
        gains_out[0],
        branch_out,
        input_out,
        tail[:4],
        tail[4],
        decay_out,
        tail[5],
        inject_out,
        tail[6],
        tail[7],
        output_out,
        gains_out[1],
        feed_grads[0],
        feed_grads[1],
        feed_grads[2].T,
    )


def solution(mesh):
    both = ("seq", "mlp")
    in_specs = (
        P(None, both, None), P(both), P(both, None), P(both, None), P(None, both), P(both),
        P(both, None), P(both), P(both, None), P(both), P(both), P(both, None), P(both),
        P(None, "mlp"), P(None, "mlp"), P("mlp", None), P(None, both, None),
    )
    out_specs = (
        P(None, both, None), P(None, both, None), P(both), P(both, None), P(both, None), P(None, both),
        P(both), P(both, None), P(both), P(both, None), P(both), P(both), P(both, None), P(both),
        P("seq", "mlp"), P("seq", "mlp"), P("mlp", "seq"),
    )
    return jax.shard_map(
        per_device, mesh=mesh, in_specs=in_specs, out_specs=out_specs, check_vma=False
    )
```

```python
import functools
import math

import jax
import jax.numpy as jnp
from jax import lax
from jax.experimental import pallas as pl
from jax.experimental.pallas import tpu as pltpu
from jax.experimental.layout import Layout, with_layout_constraint
from jax.sharding import PartitionSpec as P

EPS = 1e-06
RATE_SCALE = 8.0
F32 = jnp.float32
BF16 = jnp.bfloat16
MESH = pl.DeviceIdType.MESH
PAD = 8
GELU_C = math.sqrt(2.0 / math.pi)
VMEM_LIMIT = 48 << 20


def gelu_and_slope(v):
    sq = v * v
    t = jnp.tanh(GELU_C * v * (1.0 + 0.044715 * sq))
    half = 0.5 * (1.0 + t)
    slope = half + 0.5 * v * (1.0 - t * t) * GELU_C * (1.0 + 3 * 0.044715 * sq)
    return v * half, slope


def gelu_only(v):
    return 0.5 * v * (1.0 + jnp.tanh(GELU_C * v * (1.0 + 0.044715 * (v * v))))


def decay_terms(recur, soft):
    log_rate = (-RATE_SCALE) * recur * soft
    rate = jnp.exp(log_rate)
    y = -2.0 * log_rate
    e = 1.0 - y * (1.0 / 10.0)
    for n in range(9, 1, -1):
        e = 1.0 - (y * (1.0 / n)) * e
    return rate, jnp.where(y < 0.5, y * e, 1.0 - rate * rate)


def norm_inverse(v):
    return lax.rsqrt(jnp.mean(v * v, axis=-1, keepdims=True) + EPS)


def tile_scan(a, b, reverse):
    row = lax.broadcasted_iota(jnp.int32, a.shape, 1)
    for d in (1, 2, 4):
        ok = (row < 8 - d) if reverse else (row >= d)
        shift = 8 - d if reverse else d
        a_near = jnp.where(ok, pltpu.roll(a, shift, 1), 1.0)
        b_near = jnp.where(ok, pltpu.roll(b, shift, 1), 0.0)
        b = b + a * b_near
        a = a * a_near
    return a, b


def part_scan(a, b, a_ref, b_ref, reverse):
    seqs, rows, lanes = a.shape
    tiles = rows // 8
    a, b = tile_scan(a.reshape(seqs * tiles, 8, lanes), b.reshape(seqs * tiles, 8, lanes), reverse)
    a = a.reshape(seqs, tiles, 8, lanes)
    b = b.reshape(seqs, tiles, 8, lanes)
    a_run = b_run = None
    edge = 0 if reverse else 7
    for i in range(tiles):
        t = tiles - 1 - i if reverse else i
        at, bt = a[:, t], b[:, t]
        if a_run is not None:
            bt = bt + at * b_run
            at = at * a_run
        a_ref[:, t * 8 : (t + 1) * 8, :] = at
        b_ref[:, t * 8 : (t + 1) * 8, :] = bt
        a_run, b_run = at[:, edge : edge + 1, :], bt[:, edge : edge + 1, :]
    return a_run[:, 0, :], b_run[:, 0, :]


def gates_kernel(seqs, n_ref, w_ref, dw_ref, iw_ref, vec_ref,
                 cin_ref, low_ref, rec_ref, inj_ref, prod_ref, loc_ref, ends_ref):
    cin = jnp.dot(n_ref[...], w_ref[...], preferred_element_type=F32).astype(BF16)
    cin_ref[...] = cin
    x = cin.astype(F32)
    ext, lanes = x.shape
    taps = vec_ref[...]
    y = taps[4:5, :] + taps[0:1, :] * x
    for k in range(1, 4):
        y = y + taps[k : k + 1, :] * pltpu.roll(x, k, 0)
    y = y.reshape(seqs, ext // seqs, lanes)[:, PAD:, :]
    low = y.astype(BF16)
    low_ref[...] = low
    shape = y.shape
    low2 = low.reshape(shape[0] * shape[1], lanes)
    dpre = jnp.dot(low2, dw_ref[...], preferred_element_type=F32)
    ipre = jnp.dot(low2, iw_ref[...], preferred_element_type=F32)
    recur = jax.nn.sigmoid(dpre + taps[5:6, :])
    inject = jax.nn.sigmoid(ipre + taps[6:7, :])
    rate, em = decay_terms(recur, taps[7:8, :])
    recur = recur.reshape(shape)
    inject = inject.reshape(shape)
    rec_ref[...] = recur
    inj_ref[...] = inject
    injected = jnp.sqrt(em).reshape(shape) * inject * low.astype(F32)
    pa, pb = part_scan(rate.reshape(shape), injected, prod_ref, loc_ref, False)
    ends_ref[0:seqs, :] = pa
    ends_ref[seqs : 2 * seqs, :] = pb


def mix_kernel(heads, loc_ref, prod_ref, bp_ref, carry_ref, w_ref, x_ref, gain_ref,
               state_ref, mixed_ref, mid_ref, feed_ref, acc_ref):
    h = pl.program_id(0)
    carry = carry_ref[...][:, None, :]
    state = loc_ref[...] + prod_ref[...] * carry
    state_ref[...] = state
    mixed = (state * gelu_only(bp_ref[...])).astype(BF16)
    mixed_ref[...] = mixed
    b, s, lanes = mixed.shape
    part = jnp.dot(mixed.reshape(b * s, lanes), w_ref[...], preferred_element_type=F32)

    @pl.when(h == 0)
    def _():
        acc_ref[...] = x_ref[...].astype(F32) + part

    @pl.when(h > 0)
    def _():
        acc_ref[...] += part

    @pl.when(h == heads - 1)
    def _():
        mid = acc_ref[...]
        mid_ref[...] = mid
        feed_ref[...] = (mid * norm_inverse(mid) * gain_ref[...]).astype(BF16)


def back_scan_kernel(seqs, g_ref, w_ref, bp_ref, state_ref, rec_ref, vec_ref,
                     prod_ref, adj_ref, gbp_ref, ends_ref):
    gm = lax.dot_general(g_ref[...], w_ref[...], (((1,), (1,)), ((), ())), preferred_element_type=F32)
    rows, lanes = gm.shape
    shape = (seqs, rows // seqs, lanes)
    act, slope = gelu_and_slope(bp_ref[...])
    gm = gm.reshape(shape)
    gbp = gm * state_ref[...] * slope
    gbp = jnp.concatenate([jnp.zeros((seqs, PAD, lanes), F32), gbp], axis=1)
    gbp_ref[...] = gbp.reshape(seqs * (shape[1] + PAD), lanes).astype(BF16)
    rate = jnp.exp((-RATE_SCALE) * rec_ref[...] * vec_ref[7:8, :])
    after = pltpu.roll(rate.reshape(rows, lanes), rows - 1, 0).reshape(shape)
    row = lax.broadcasted_iota(jnp.int32, shape, 1)
    after = jnp.where(row == shape[1] - 1, 1.0, after)
    pa, pb = part_scan(after, gm * act, prod_ref, adj_ref, True)
    first = rate[:, 0, :]
    ends_ref[0:seqs, :] = first * pa
    ends_ref[seqs : 2 * seqs, :] = first * pb


def back_gates_kernel(heads, prod_ref, adj_ref, carry_ref, state_ref, sin_ref, rec_ref, inj_ref, low_ref,
                      cin_ref, vec_ref, dw_ref, iw_ref, gbp_ref, bw_ref, cw_ref,
                      gcin_ref, gdw_ref, giw_ref, gvec_ref, gn_ref):
    h = pl.program_id(0)
    vec = vec_ref[...]
    soft = vec[7:8, :]
    adj = adj_ref[...] + prod_ref[...] * carry_ref[...][:, None, :]
    shape = adj.shape
    seqs, rows, lanes = shape
    flat = (seqs * rows, lanes)
    state = state_ref[...]
    prev = pltpu.roll(state.reshape(flat), 1, 0).reshape(shape)
    row = lax.broadcasted_iota(jnp.int32, shape, 1)
    prev = jnp.where(row == 0, sin_ref[...][:, None, :], prev)
    recur, inject = rec_ref[...], inj_ref[...]
    rate, em = decay_terms(recur, soft)
    mult = jnp.sqrt(em)
    low = low_ref[...]
    conv = low.astype(F32)
    g_log = adj * prev * rate - adj * inject * conv * (rate * rate) / mult
    am = adj * mult
    g_elem = am * inject
    g_rec = g_log * ((-RATE_SCALE) * soft)
    g_soft = jnp.sum((g_log * recur).reshape(flat), axis=0, keepdims=True) * (-RATE_SCALE)
    gdp = (g_rec * recur * (1.0 - recur)).reshape(flat)
    gip = (am * conv * inject * (1.0 - inject)).reshape(flat)
    gdp_low, gip_low = gdp.astype(BF16), gip.astype(BF16)
    low2 = low.reshape(flat)
    tok = (((0,), (0,)), ((), ()))
    last = (((1,), (1,)), ((), ()))
    gdw_ref[...] = lax.dot_general(low2, gdp_low, tok, preferred_element_type=F32).astype(BF16)
    giw_ref[...] = lax.dot_general(low2, gip_low, tok, preferred_element_type=F32).astype(BF16)
    gc = (
        g_elem.reshape(flat)
        + lax.dot_general(gdp_low, dw_ref[...], last, preferred_element_type=F32)
        + lax.dot_general(gip_low, iw_ref[...], last, preferred_element_type=F32)
    )
    gce = jnp.concatenate([jnp.zeros((seqs, PAD, lanes), F32), gc.reshape(shape)], axis=1)
    ext = seqs * (rows + PAD)
    gce = gce.reshape(ext, lanes)
    x = cin_ref[...].astype(F32)
    out = vec[0:1, :] * gce
    sums = [jnp.sum(gce * x, axis=0, keepdims=True)]
    for k in range(1, 4):
        out = out + vec[k : k + 1, :] * pltpu.roll(gce, ext - k, 0)
        sums.append(jnp.sum(gce * pltpu.roll(x, k, 0), axis=0, keepdims=True))
    sums.append(jnp.sum(gce, axis=0, keepdims=True))
    sums.append(jnp.sum(gdp, axis=0, keepdims=True))
    sums.append(jnp.sum(gip, axis=0, keepdims=True))
    sums.append(g_soft)
    for i, v in enumerate(sums):
        gvec_ref[i : i + 1, :] = v
    gcin = out.astype(BF16)
    gcin_ref[...] = gcin
    part = lax.dot_general(gcin, cw_ref[...], last, preferred_element_type=F32)
    part += lax.dot_general(gbp_ref[...], bw_ref[...], last, preferred_element_type=F32)

    @pl.when(h == 0)
    def _():
        gn_ref[...] = part

    @pl.when(h > 0)
    def _():
        gn_ref[...] += part


def carry_kernel(seqs, n_seq, n_mlp, reverse, ends_ref, out_ref, zbuf, sbuf, mine_low, total, ssem, rsem):
    ms, mz = lax.axis_index("seq"), lax.axis_index("mlp")
    barrier = pltpu.get_barrier_semaphore()
    for d in range(1, n_mlp):
        pl.semaphore_signal(barrier, inc=1, device_id=(ms, lax.rem(mz + d, n_mlp)), device_id_type=MESH)
    for d in range(1, n_seq):
        pl.semaphore_signal(barrier, inc=1, device_id=(lax.rem(ms + d, n_seq), mz), device_id_type=MESH)
    pl.semaphore_wait(barrier, n_mlp + n_seq - 2)
    mine_low[...] = ends_ref[...].astype(BF16)
    copies = []
    for d in range(1, n_mlp):
        copies.append(pltpu.make_async_remote_copy(
            src_ref=mine_low, dst_ref=zbuf.at[mz], send_sem=ssem.at[d - 1], recv_sem=rsem.at[d - 1],
            device_id=(ms, lax.rem(mz + d, n_mlp)), device_id_type=MESH))
        copies[-1].start()
    zbuf[mz] = mine_low[...]
    for c in copies:
        c.wait()
    shape = (seqs, ends_ref.shape[1])
    tp, ts = jnp.ones(shape, F32), jnp.zeros(shape, F32)
    pp, ps = tp, ts
    for i in range(n_mlp):
        z = n_mlp - 1 - i if reverse else i
        val = zbuf[z].astype(F32)
        p, s = val[0:seqs, :], val[seqs : 2 * seqs, :]
        ts = p * ts + s
        tp = p * tp
        mine = jnp.where((z > mz) if reverse else (z < mz), 1.0, 0.0)
        ps = mine * (p * ps + s) + (1.0 - mine) * ps
        pp = (mine * p + (1.0 - mine)) * pp
    total[...] = jnp.concatenate([tp, ts], axis=0).astype(BF16)
    copies = []
    for d in range(1, n_seq):
        i = n_mlp - 2 + d
        copies.append(pltpu.make_async_remote_copy(
            src_ref=total, dst_ref=sbuf.at[ms], send_sem=ssem.at[i], recv_sem=rsem.at[i],
            device_id=(lax.rem(ms + d, n_seq), mz), device_id_type=MESH))
        copies[-1].start()
    sbuf[ms] = total[...]
    for c in copies:
        c.wait()
    c = jnp.zeros(shape, F32)
    for i in range(n_seq):
        q = n_seq - 1 - i if reverse else i
        val = sbuf[q].astype(F32)
        p, s = val[0:seqs, :], val[seqs : 2 * seqs, :]
        mine = jnp.where((q > ms) if reverse else (q < ms), 1.0, 0.0)
        c = mine * (p * c + s) + (1.0 - mine) * c
    out_ref[...] = pp * c + ps


def carry_call(ends, seqs, n_seq, n_mlp, reverse):
    rows, width = ends.shape
    n = n_seq + n_mlp - 2
    return pl.pallas_call(
        functools.partial(carry_kernel, seqs, n_seq, n_mlp, reverse),
        out_shape=jax.ShapeDtypeStruct((seqs, width), F32),
        in_specs=[pl.BlockSpec(memory_space=pltpu.VMEM)],
        out_specs=pl.BlockSpec(memory_space=pltpu.VMEM),
        scratch_shapes=[
            pltpu.VMEM((n_mlp, rows, width), BF16),
            pltpu.VMEM((n_seq, rows, width), BF16),
            pltpu.VMEM((rows, width), BF16),
            pltpu.VMEM((rows, width), BF16),
            pltpu.SemaphoreType.DMA((n,)),
            pltpu.SemaphoreType.DMA((n,)),
        ],
        compiler_params=pltpu.CompilerParams(
            collective_id=1 if reverse else 0, has_side_effects=True, vmem_limit_bytes=VMEM_LIMIT
        ),
        cost_estimate=pl.CostEstimate(flops=0, bytes_accessed=200 * rows * width * 4, transcendentals=0),
        name="carry_back" if reverse else "carry_fwd",
    )(ends)


def spread_kernel(n_seq, n_mlp, plans, starts, order, *refs):
    ms, mz = lax.axis_index("seq"), lax.axis_index("mlp")
    count = len(plans)
    shards, outs = refs[:count], refs[count : 2 * count]
    ssem, rsem = refs[2 * count :]
    n_bits = n_seq.bit_length() - 1
    digit = lambda bit: lax.rem(lax.div(ms, 1 << bit), 2)
    seq_peer = lambda bit: (ms + (1 - 2 * digit(bit)) * (1 << bit), mz)
    used = [0]

    def block_of(mask):
        at = ms
        for bit in range(n_bits):
            if (mask >> bit) & 1:
                at = at + (1 - 2 * digit(bit)) * (1 << bit)
        return at

    barrier = pltpu.get_barrier_semaphore()
    for bit in range(n_bits):
        pl.semaphore_signal(barrier, inc=1, device_id=seq_peer(bit), device_id_type=MESH)
    for d in range(1, n_mlp):
        pl.semaphore_signal(barrier, inc=1, device_id=(ms, lax.rem(mz + d, n_mlp)), device_id_type=MESH)
    local = []
    for a, parts in enumerate(plans):
        dst = outs[a].at[ms, mz] if len(parts[0]) > 1 else outs[a].at[:, mz]
        local.append(pltpu.make_async_copy(shards[a], dst, rsem.at[used[0]]))
        local[-1].start()
        used[0] += 1
    pl.semaphore_wait(barrier, n_bits + n_mlp - 1)

    def send(src, dst, peer):
        i = used[0]
        used[0] += 1
        c = pltpu.make_async_remote_copy(
            src_ref=src, dst_ref=dst, send_sem=ssem.at[i], recv_sem=rsem.at[i],
            device_id=peer, device_id_type=MESH)
        c.start()
        return c

    state = [[{"held": [0], "all": False, "moved": False} for _ in parts] for parts in plans]
    pending = [[] for _ in plans]

    def start(a, level):
        parts = plans[a]
        if level >= len(parts[0]):
            return
        if level > 0 and local[a] is not None:
            local[a].wait()
            local[a] = None
        for h, (stages, st) in enumerate(zip(parts, state[a])):
            stage = stages[level]
            if len(stages) == 1:
                for d in range(1, n_mlp):
                    z = lax.rem(mz + d, n_mlp)
                    pending[a].append(send(shards[a], outs[a].at[:, mz], (ms, z)))
                continue
            width = shards[a].shape[1] // len(parts)
            cols = pl.ds(h * width, width)

            def place(mask, dst):
                at = block_of(mask)
                if not dst and not st["moved"]:
                    return shards[a].at[:, cols]
                if st["all"]:
                    return outs[a].at[at, :, :, cols]
                return outs[a].at[at, mz, :, cols]

            moves = [(place(mask, False), place(mask, True)) for mask in st["held"]]
            if stage == "z":
                peers = [(ms, lax.rem(mz + d, n_mlp)) for d in range(1, n_mlp)]
                st["all"] = True
            else:
                peers = [seq_peer(stage)]
                st["held"] = st["held"] + [mask | (1 << stage) for mask in st["held"]]
            st["moved"] = True
            for peer in peers:
                for src, dst in moves:
                    pending[a].append(send(src, dst, peer))

    def end(a):
        for c in pending[a]:
            c.wait()
        pending[a] = []

    for a in starts:
        start(a, 0)
    for a, level, after in order:
        if level < len(plans[a][0]):
            end(a)
            start(a, level + 1)
        for b in after:
            start(b, 0)
    for c in local:
        if c is not None:
            c.wait()


def spread_call(small, first, second, third, tokens, n_seq, n_mlp):
    chips, turned = chip_orders(n_seq)
    line = ["z"] + chips + [0]
    pair = [line, ["z"] + turned + [0]]
    cross = [chips[:1] + ["z"] + chips[1:] + [0], turned[:1] + ["z"] + turned[1:] + [0]]
    arrays = [small, first, second, third, tokens]
    plans = [[line], pair, pair, cross, [["z"]]]
    levels = len(line)
    order = []
    for t in range(levels + 1):
        if t < levels:
            order += [(0, t, []), (1, t, [2] if t == 0 else [])]
        if t > 0:
            order += [(2, t - 1, []), (3, t - 1, [4] if t == 1 else [])]
    order.append((4, 0, []))
    n_sem = len(arrays)
    for parts in plans:
        for stages in parts:
            held = 1
            for stage in stages:
                n_sem += held * (n_mlp - 1 if stage == "z" else 1)
                held *= 1 if stage == "z" else 2
    shapes = [(n_seq, n_mlp) + v.shape for v in arrays[:4]]
    shapes.append((tokens.shape[0], n_mlp) + tokens.shape[1:])
    return pl.pallas_call(
        functools.partial(spread_kernel, n_seq, n_mlp, plans, (0, 1, 3), order),
        out_shape=[jax.ShapeDtypeStruct(s, BF16) for s in shapes],
        in_specs=[pl.BlockSpec(memory_space=pltpu.VMEM)] * len(arrays),
        out_specs=[pl.BlockSpec(memory_space=pl.ANY)] * len(arrays),
        scratch_shapes=[pltpu.SemaphoreType.DMA((n_sem,)), pltpu.SemaphoreType.DMA((n_sem,))],
        compiler_params=pltpu.CompilerParams(
            collective_id=3, has_side_effects=True, vmem_limit_bytes=VMEM_LIMIT
        ),
        name="spread",
    )(*arrays)


def chip_orders(n_seq):
    chips = list(range(1, n_seq.bit_length() - 1))
    turn = len(chips) // 2
    return chips, chips[turn:] + chips[:turn]


def owners_plan(cols, n_seq, crossed, last):
    orders = chip_orders(n_seq)
    if crossed:
        orders = [o[:1] + ["z"] + o[1:] for o in orders]
    else:
        orders = [o + ["z"] for o in orders]
    tiles = cols // 128
    sizes = [tiles // 2, tiles - tiles // 2]
    if last and tiles >= 8:
        small = tiles // 5
        big = (tiles - 2 * small) // 2
        sizes = [big, big, small, tiles - 2 * big - small]
    units, at = [], 0
    for i in range(0, len(sizes), 2):
        unit = []
        for j in range(2):
            unit.append((at, sizes[i + j] * 128, tuple(orders[j])))
            at += sizes[i + j] * 128
        units.append(unit)
    return units


def owners_shapes(n_seq, n_mlp, rows, width, stages):
    blocks, z = n_seq, n_mlp
    out = []
    for stage in stages:
        if stage == "z":
            arrive = (n_mlp - 1, blocks, rows, width)
            z = 1
        else:
            blocks //= 2
            arrive = (blocks, z, rows, width)
        out.append((arrive, (blocks, z, rows, width)))
    return out


def owners_kernel(n_seq, n_mlp, count, units, *refs):
    ms, mz = lax.axis_index("seq"), lax.axis_index("mlp")
    arrays, vec = refs[:count], refs[count]
    outs, vec_out = refs[count + 1 : 2 * count + 1], refs[2 * count + 1]
    scratch = list(refs[2 * count + 2 :])
    vec_in, vec_sum, ssem, rsem = scratch[-4:]
    n_bits = n_seq.bit_length() - 1
    mine = lambda bit: lax.rem(lax.div(ms, 1 << bit), 2)
    seq_peer = lambda bit: (ms + (1 - 2 * mine(bit)) * (1 << bit), mz)
    core = mine(0)
    used = [0]

    barrier = pltpu.get_barrier_semaphore()
    for bit in range(n_bits):
        pl.semaphore_signal(barrier, inc=1, device_id=seq_peer(bit), device_id_type=MESH)
    for d in range(1, n_mlp):
        pl.semaphore_signal(barrier, inc=1, device_id=(ms, lax.rem(mz + d, n_mlp)), device_id_type=MESH)
    pl.semaphore_wait(barrier, n_bits + n_mlp - 1)

    def send(src, dst, peer):
        i = used[0]
        used[0] += 1
        c = pltpu.make_async_remote_copy(
            src_ref=src, dst_ref=dst, send_sem=ssem.at[i], recv_sem=rsem.at[i],
            device_id=peer, device_id_type=MESH)
        c.start()
        return c

    def load(src, dst):
        i = used[0]
        used[0] += 1
        c = pltpu.make_async_copy(src, dst, rsem.at[i])
        c.start()
        return c

    tasks = []
    for unit in units:
        group = []
        for a, at, width, stages in unit:
            t = {"a": a, "at": at, "cols": pl.ds(at, width), "stages": stages, "recv": [], "sum": []}
            t["own"] = scratch.pop(0)
            for _ in stages:
                t["recv"].append(scratch.pop(0))
                t["sum"].append(scratch.pop(0))
            t["csend"], t["crecv"] = scratch.pop(0), scratch.pop(0)
            left, t["runs"] = list(range(n_bits))[::-1], []
            for stage in stages:
                if stage == "z":
                    t["runs"].append(None)
                    continue
                pos = left.index(stage)
                t["runs"].append((1 << pos, 1 << (len(left) - 1 - pos)))
                left.remove(stage)
            group.append(t)
        tasks.append(group)

    def joined(t, side):
        half = arrays[t["a"]].shape[3]
        return pl.ds(pl.multiple_of(side * half + t["at"], 128), t["csend"].shape[1])

    def begin(t, i):
        stage = t["stages"][i]
        t["wait"] = []
        if stage == "z":
            for d in range(1, n_mlp):
                z = lax.rem(mz + d, n_mlp)
                t["wait"].append(send(t["sum"][i - 1].at[:, z], t["recv"][i].at[d - 1], (ms, z)))
            return
        runs, length = t["runs"][i]
        for j in range(runs):
            away = pl.ds((2 * j + 1 - mine(stage)) * length, length)
            home = pl.ds((2 * j + mine(stage)) * length, length)
            to = pl.ds(j * length, length)
            if i == 0:
                src = arrays[t["a"]].at[away, :, :, t["cols"]]
                t["wait"].append(load(arrays[t["a"]].at[home, :, :, t["cols"]], t["own"].at[to]))
            else:
                src = t["sum"][i - 1].at[away]
            t["wait"].append(send(src, t["recv"][i].at[to], seq_peer(stage)))

    def finish(t, i):
        for c in t["wait"]:
            c.wait()
        stage = t["stages"][i]
        recv, total = t["recv"][i], t["sum"][i]
        blocks, zs = total.shape[0], total.shape[1]
        kind = total.dtype
        if stage == "z":
            for k in range(blocks):
                v = t["sum"][i - 1][k, mz].astype(F32)
                for d in range(1, n_mlp):
                    v = v + recv[d - 1, k].astype(F32)
                total[k, 0] = v.astype(kind)
        else:
            runs, length = t["runs"][i]
            for j in range(runs):

                def add(n, _, j=j):
                    b, q = lax.div(n, zs), lax.rem(n, zs)
                    if i == 0:
                        kept = t["own"][j * length + b, q]
                    else:
                        kept = t["sum"][i - 1][(2 * j + mine(stage)) * length + b, q]
                    v = kept.astype(F32) + recv[j * length + b, q].astype(F32)
                    total[j * length + b, q] = v.astype(kind)
                    return 0

                lax.fori_loop(0, length * zs, add, 0)
        if i + 1 < len(t["stages"]):
            begin(t, i + 1)
        else:
            outs[t["a"]][:, joined(t, core)] = total[core, 0]
            t["csend"][...] = total[1 - core, 0].astype(BF16)
            t["wait"] = [send(t["csend"], t["crecv"], seq_peer(0))]

    def close(t):
        for c in t["wait"]:
            c.wait()
        outs[t["a"]][:, joined(t, 1 - core)] = t["crecv"][...].astype(F32)

    vec_peers = []
    for bit in range(n_mlp.bit_length() - 1):
        side = lax.rem(lax.div(mz, 1 << bit), 2)
        vec_peers.append((ms, mz + (1 - 2 * side) * (1 << bit)))
    vec_peers += [seq_peer(bit) for bit in range(n_bits)]
    vec_state = [None, 0]

    def vec_step():
        copy, i = vec_state
        if copy is not None:
            copy.wait()
            before = vec[...] if i == 1 else vec_sum[i - 2]
            v = before + vec_in[i - 1]
            if i == len(vec_peers):
                vec_out[...] = v
            else:
                vec_sum[i - 1] = v
        vec_state[0] = None
        if i < len(vec_peers):
            src = vec if i == 0 else vec_sum.at[i - 1]
            vec_state[:] = [send(src, vec_in.at[i], vec_peers[i]), i + 1]

    n_stages = len(tasks[0][0]["stages"])
    for group in tasks[:2]:
        for t in group:
            begin(t, 0)
    vec_step()
    for step in range(len(tasks) + n_stages):
        for i in range(n_stages + 1):
            u = step - i
            if not 0 <= u < len(tasks):
                continue
            for t in tasks[u]:
                if i < n_stages:
                    finish(t, i)
                else:
                    close(t)
            if i == 0 and u + 2 < len(tasks):
                for t in tasks[u + 2]:
                    begin(t, 0)
        vec_step()
    while vec_state[0] is not None:
        vec_step()


def owners_call(arrays, vec, n_seq, n_mlp):
    units, scratch, n_sem = [], [], 0
    for a, v in enumerate(arrays):
        plan = owners_plan(v.shape[3], n_seq, a == 0, a == len(arrays) - 1)
        units += [[(a,) + part for part in unit] for unit in plan]
    for unit in units:
        for a, at, width, stages in unit:
            rows = arrays[a].shape[2]
            scratch.append(pltpu.VMEM((n_seq // 2, n_mlp, rows, width), BF16))
            shapes = owners_shapes(n_seq, n_mlp, rows, width, stages)
            for i, (arrive, total) in enumerate(shapes):
                scratch.append(pltpu.VMEM(arrive, BF16))
                scratch.append(pltpu.VMEM(total, F32 if i == len(shapes) - 1 else BF16))
            scratch += [pltpu.VMEM((rows, width), BF16)] * 2
            n_sem += 3 * n_seq + n_mlp
    steps = (n_mlp.bit_length() - 1) + (n_seq.bit_length() - 1)
    n_sem += steps
    vmem = pl.BlockSpec(memory_space=pltpu.VMEM)
    outs = pl.pallas_call(
        functools.partial(owners_kernel, n_seq, n_mlp, len(arrays), units),
        out_shape=[jax.ShapeDtypeStruct((v.shape[2], 2 * v.shape[3]), F32) for v in arrays]
        + [jax.ShapeDtypeStruct(vec.shape, F32)],
        in_specs=[pl.BlockSpec(memory_space=pl.ANY)] * len(arrays) + [vmem],
        out_specs=[vmem] * (len(arrays) + 1),
        scratch_shapes=scratch + [
            pltpu.VMEM((steps,) + vec.shape, F32),
            pltpu.VMEM((steps,) + vec.shape, F32),
            pltpu.SemaphoreType.DMA((n_sem,)),
            pltpu.SemaphoreType.DMA((n_sem,)),
        ],
        compiler_params=pltpu.CompilerParams(
            collective_id=2, has_side_effects=True, vmem_limit_bytes=60 << 20
        ),
        name="owners",
    )(*arrays, vec)
    return outs[:-1], outs[-1]


def split_kernel(parts, kept, sides_ref, *refs):
    ins, outs = refs[: 2 * parts], refs[2 * parts + kept :]
    for i in range(parts):
        total = ins[2 * i][...].astype(F32) + ins[2 * i + 1][...].astype(F32)
        outs[i][...] = total.reshape(outs[i].shape).astype(outs[i].dtype)


def split_place(j, pos, blocks, side):
    length = blocks >> (pos + 1)
    return (2 * lax.div(j, length) + side) * length + lax.rem(j, length)


def split_cores(own, got, a, arrays, seq, bufs):
    blocks, rows, cols = got.shape
    half = rows // 2
    left = seq.bits[::-1][:-1]
    own = own.reshape(2 * blocks, 2, half, cols)
    got = got.reshape(blocks, 2, half, cols)
    sides = jnp.stack([seq.mine(0)] + [seq.mine(o[0]) for o in seq.orders])
    block = (1, 1, half, cols)
    ins, args = [], []
    for h in range(2):
        pos = left.index(seq.orders[h][0])
        for flip in (1, 0):

            def at(j, s, h=h, pos=pos, flip=flip):
                side = 1 - s[1 + h] if flip else s[1 + h]
                return split_place(j, pos, blocks, side)

            ins.append(pl.BlockSpec(block, lambda j, s, at=at, h=h: (2 * at(j, s) + s[0], h, 0, 0)))
            ins.append(pl.BlockSpec(block, lambda j, s, at=at, h=h: (at(j, s), h, 0, 0)))
            args += [own, got]
    kept = 0 if bufs is None else 4
    shape = (arrays, blocks // 2, half, cols)
    return pl.pallas_call(
        functools.partial(split_kernel, 4, kept),
        grid_spec=pltpu.PrefetchScalarGridSpec(
            num_scalar_prefetch=1,
            grid=(blocks // 2,),
            in_specs=ins + [pl.BlockSpec(memory_space=pl.ANY)] * kept,
            out_specs=[pl.BlockSpec(block, lambda j, s: (a, j, 0, 0))] * 4,
        ),
        out_shape=[jax.ShapeDtypeStruct(shape, BF16)] * 4,
        input_output_aliases={9 + i: i for i in range(kept)},
        compiler_params=pltpu.CompilerParams(vmem_limit_bytes=VMEM_LIMIT),
        cost_estimate=pl.CostEstimate(flops=0, bytes_accessed=6 * own.size, transcendentals=0),
        name="split_cores",
    )(sides, *args, *(bufs or ()))


def split_chips(keep, got, left, bit, seq):
    arrays, blocks, rows, cols = keep.shape
    pos = left.index(bit)
    block = (1, 1, rows, cols)
    sides = seq.mine(bit)[None]
    ins, args = [], []
    for flip in (1, 0):

        def at(j, s, flip=flip):
            return split_place(j, pos, blocks, 1 - s[0] if flip else s[0])

        ins += [pl.BlockSpec(block, lambda i, j, s, at=at: (i, at(j, s), 0, 0))] * 2
        args += [keep, got]
    return pl.pallas_call(
        functools.partial(split_kernel, 2, 0),
        grid_spec=pltpu.PrefetchScalarGridSpec(
            num_scalar_prefetch=1,
            grid=(arrays, blocks // 2),
            in_specs=ins,
            out_specs=[pl.BlockSpec(block, lambda i, j, s: (i, j, 0, 0))] * 2,
        ),
        out_shape=[jax.ShapeDtypeStruct((arrays, blocks // 2, rows, cols), BF16)] * 2,
        compiler_params=pltpu.CompilerParams(vmem_limit_bytes=VMEM_LIMIT),
        cost_estimate=pl.CostEstimate(flops=0, bytes_accessed=6 * keep.size, transcendentals=0),
        name="split_chips",
    )(sides, *args)


class Seq:
    def __init__(self):
        self.n = lax.axis_size("seq")
        self.me = lax.axis_index("seq")
        self.bits = list(range(self.n.bit_length() - 1))
        chips = self.bits[1:]
        turn = len(chips) // 2
        self.orders = (chips, chips[turn:] + chips[:turn])

    def mine(self, bit):
        return (self.me >> bit) & 1

    def swap(self, v, bit):
        return lax.ppermute(v, "seq", [(i, i ^ (1 << bit)) for i in range(self.n)])


def flat_dot(left, right):
    shape = left.shape
    out = jnp.dot(left.reshape(-1, shape[-1]), right, preferred_element_type=F32)
    return out.reshape(shape[:-1] + (right.shape[1],))


def dot_against(left, right):
    shape = left.shape
    out = lax.dot_general(
        left.reshape(-1, shape[-1]), right, (((1,), (1,)), ((), ())), preferred_element_type=F32
    )
    return out.reshape(shape[:-1] + (right.shape[0],))


def outer_sum(left, right):
    return lax.dot_general(
        left.reshape(-1, left.shape[-1]),
        right.reshape(-1, right.shape[-1]),
        (((0,), (0,)), ((), ())),
        preferred_element_type=F32,
    )


def gated_unit(gate_pre, up_pre):
    return jax.nn.gelu(gate_pre) * up_pre


def norm_back(values, inverse, gain, upstream):
    scaled = upstream * gain
    gain_grad = jnp.sum(upstream * values * inverse, axis=(0, 1))
    inner_mean = jnp.mean(scaled * values, axis=-1, keepdims=True)
    return (inverse * (scaled - values * inner_mean * inverse * inverse), gain_grad)


def per_device(inputs, mixer_gain, branch_weight, input_weight, conv_weight, conv_bias, decay_weight,
               decay_bias, inject_weight, inject_bias, decay_param, output_weight, feed_gain,
               feed_gate, feed_up, feed_down, cotangent):
    both = ("seq", "mlp")
    seq = Seq()
    n_seq, n_mlp = seq.n, lax.axis_size("mlp")
    n_dev = n_seq * n_mlp
    seqs, rows, width = inputs.shape
    taps, r_own = conv_weight.shape
    edge = taps - 1
    head = decay_weight.shape[1]
    r_all = r_own * n_dev
    heads = r_all // head
    d_own = width // n_dev
    ext_rows = rows + PAD
    ext = seqs * ext_rows
    tokens = seqs * rows

    lanes = 128
    small = [conv_weight.T, conv_bias[:, None], decay_bias[:, None], inject_bias[:, None], decay_param[:, None]]
    gains = [jnp.pad(g, (0, r_own - d_own))[:, None] for g in (mixer_gain, feed_gain)]
    small = jnp.concatenate(small + gains, axis=1)
    small = jnp.pad(small, ((0, 0), (0, lanes - small.shape[1])))
    gates_own = jnp.concatenate([decay_weight, inject_weight, small], axis=1)
    n_chunks = 2 if seqs % 2 == 0 else 1
    per = seqs // n_chunks
    chunk = lambda v, c: v[c * per : (c + 1) * per]
    gates_all, full_input, full_branch, full_output, first_cot = spread_call(
        gates_own, input_weight, branch_weight, output_weight, chunk(cotangent, 0), n_seq, n_mlp
    )
    gates_all = gates_all.reshape(r_all, -1)
    full_input, full_branch = (v.reshape(width, r_all) for v in (full_input, full_branch))
    full_output = full_output.reshape(r_all, width)
    grad_rows = [first_cot.reshape(per, n_mlp * rows, width)]
    for c in range(1, n_chunks):
        gates_all, cot = lax.optimization_barrier((gates_all, chunk(cotangent, c)))
        grad_rows.append(lax.all_gather(cot, "mlp", axis=1, tiled=True))
    vectors = gates_all[:, 2 * head :].astype(F32)
    gain_rows = vectors[:, 8:10].reshape(n_dev, r_own, 2)[:, :d_own, :].reshape(width, 2)
    gain_mixer, gain_feed = gain_rows[:, 0], gain_rows[:, 1]
    param = vectors[:, 7]
    vec = jnp.concatenate([vectors[:, :7].T, jax.nn.softplus(-param)[None, :]], axis=0)

    last_tokens = lax.ppermute(inputs[:, rows - edge :, :], both, [(i, i + 1) for i in range(n_dev - 1)])
    x_ext = jnp.concatenate(
        [jnp.zeros((seqs, PAD - edge, width), BF16), last_tokens, inputs], axis=1
    )
    stream_ext = x_ext.astype(F32)
    inverse_ext = norm_inverse(stream_ext)
    normed_ext = (stream_ext * inverse_ext * gain_mixer).astype(BF16).reshape(ext, width)

    params = lambda **k: pltpu.CompilerParams(dimension_semantics=("arbitrary",), vmem_limit_bytes=VMEM_LIMIT, **k)

    def cost(big_dots, arrays):
        whole_mats = 2 * ext * width * r_all
        return pl.CostEstimate(
            flops=big_dots * whole_mats,
            bytes_accessed=big_dots * 2 * width * r_all + arrays * 4 * tokens * r_all,
            transcendentals=4 * tokens * r_all,
        )

    tok_head = pl.BlockSpec((seqs, rows, head), lambda h: (0, 0, h))
    ext_head = pl.BlockSpec((ext, head), lambda h: (0, h))
    vec_head = pl.BlockSpec((8, head), lambda h: (0, h))
    seq_head = pl.BlockSpec((seqs, head), lambda h: (0, h))
    col_head = pl.BlockSpec((width, head), lambda h: (0, h))
    row_head = pl.BlockSpec((head, width), lambda h: (h, 0))
    decay_head = pl.BlockSpec((head, head), lambda h: (h, 0))
    inject_head = pl.BlockSpec((head, head), lambda h: (h, 1))
    whole = lambda *shape: pl.BlockSpec(shape, lambda h: (0,) * len(shape))
    tok = lambda kind: jax.ShapeDtypeStruct((seqs, rows, r_all), kind)
    struct = jax.ShapeDtypeStruct

    conv_in, conv_low, recur, inject, prod, local, ends = pl.pallas_call(
        functools.partial(gates_kernel, seqs),
        grid=(heads,),
        in_specs=[whole(ext, width), col_head, decay_head, inject_head, vec_head],
        out_specs=[ext_head, tok_head, tok_head, tok_head, tok_head, tok_head,
                   pl.BlockSpec((2 * seqs, head), lambda h: (0, h))],
        out_shape=[struct((ext, r_all), BF16), tok(BF16), tok(F32), tok(F32), tok(F32), tok(F32),
                   struct((2 * seqs, r_all), F32)],
        compiler_params=params(),
        cost_estimate=cost(1, 20),
        name="gates",
    )(normed_ext, full_input, gates_all, gates_all, vec)

    state_in = carry_call(ends, seqs, n_seq, n_mlp, False)
    normed = normed_ext.reshape(seqs, ext_rows, width)[:, PAD:, :]
    branch_pre = flat_dot(normed, full_branch)

    state, mixed, mid, feed_low = pl.pallas_call(
        functools.partial(mix_kernel, heads),
        grid=(heads,),
        in_specs=[tok_head, tok_head, tok_head, seq_head, row_head, whole(tokens, width), whole(1, width)],
        out_specs=[tok_head, tok_head, whole(tokens, width), whole(tokens, width)],
        out_shape=[tok(F32), tok(BF16), struct((tokens, width), F32), struct((tokens, width), BF16)],
        scratch_shapes=[pltpu.VMEM((tokens, width), F32)],
        compiler_params=params(),
        cost_estimate=cost(1, 12),
        name="mix",
    )(local, prod, branch_pre, state_in, full_output, inputs.reshape(tokens, width), gain_feed[None, :])
    stream_mid = mid.reshape(seqs, rows, width)

    feed_own = feed_low.reshape(seqs, rows, width)
    row_major = lambda v: with_layout_constraint(v, Layout(major_to_minor=tuple(range(v.ndim))))
    mixed_two = mixed.reshape(tokens, r_all)
    mixed_two = jnp.concatenate([mixed_two, seq.swap(mixed_two, 0)], axis=0)
    normed_two = jnp.concatenate([normed_ext, seq.swap(normed_ext, 0)], axis=0)
    grad_hidden = [dot_against(v, feed_down) for v in grad_rows]
    grad_rows = jnp.concatenate(grad_rows, axis=0)
    feed_rows, hidden, gate_low, up_low, feed_norm_grad = [], [], [], [], []
    for c in range(n_chunks):
        f = row_major(lax.all_gather(chunk(feed_own, c), "mlp", axis=1, tiled=True))
        if c == 0:
            f, grad_hidden, mixed_two, normed_two = lax.optimization_barrier(
                (f, grad_hidden, mixed_two, normed_two)
            )
        else:
            f, back = lax.optimization_barrier((f, back))
            feed_norm_grad.append(lax.psum_scatter(back, "mlp", scatter_dimension=1, tiled=True))
        gate_pre = flat_dot(f, feed_gate)
        up_pre = flat_dot(f, feed_up)
        hidden.append(gated_unit(gate_pre, up_pre).astype(BF16))
        gate_grad, up_grad = jax.vjp(gated_unit, gate_pre, up_pre)[1](grad_hidden[c])
        gate_low.append(gate_grad.astype(BF16))
        up_low.append(up_grad.astype(BF16))
        feed_rows.append(f)
        back = (dot_against(gate_low[-1], feed_gate) + dot_against(up_low[-1], feed_up)).astype(BF16)
    back, feed_rows, hidden, gate_low, up_low = lax.optimization_barrier(
        (back, feed_rows, hidden, gate_low, up_low)
    )
    feed_norm_grad, back, hidden = lax.optimization_barrier((feed_norm_grad, back, hidden))
    feed_norm_grad.append(lax.psum_scatter(back, "mlp", scatter_dimension=1, tiled=True))
    feed_rows, hidden, gate_low, up_low = (
        jnp.concatenate(v, axis=0) for v in (feed_rows, hidden, gate_low, up_low)
    )
    feed_out = flat_dot(hidden, feed_down).astype(BF16)
    bufs = None
    pairs = ((feed_rows, gate_low), (feed_rows, up_low), (grad_rows, hidden))
    for a, (left, right) in enumerate(pairs):
        g = row_major(outer_sum(left, right).astype(BF16)).reshape(n_seq, width // n_seq, feed_gate.shape[1])
        other = lax.dynamic_index_in_dim(
            g.reshape((n_seq // 2, 2) + g.shape[1:]), 1 - seq.mine(0), 1, keepdims=False
        )
        bufs = list(split_cores(g, seq.swap(other, 0), a, len(pairs), seq, bufs))
    feed_norm_grad, feed_out, bufs[1], bufs[3] = lax.optimization_barrier(
        (feed_norm_grad, feed_out, bufs[1], bufs[3])
    )
    chip_bits = seq.bits[::-1][:-1]
    feed_state = [
        (bufs[2 * h + 1], seq.swap(bufs[2 * h], order[0]), [b for b in chip_bits if b != order[0]], order[1:])
        for h, order in enumerate(seq.orders)
    ]
    feed_norm_grad = jnp.concatenate(feed_norm_grad, axis=0).astype(F32)
    feed_out = lax.psum_scatter(feed_out, "mlp", scatter_dimension=1, tiled=True).astype(F32)
    result = (stream_mid + feed_out).astype(BF16)

    feed_inverse = norm_inverse(stream_mid)
    mid_part, feed_gain_grad = norm_back(stream_mid, feed_inverse, gain_feed, feed_norm_grad)
    mid_grad = cotangent.astype(F32) + mid_part
    mid_low = mid_grad.astype(BF16).reshape(tokens, width)

    back_prod, back_local, gbp, back_ends = pl.pallas_call(
        functools.partial(back_scan_kernel, seqs),
        grid=(heads,),
        in_specs=[whole(tokens, width), row_head, tok_head, tok_head, tok_head, vec_head],
        out_specs=[tok_head, tok_head, ext_head, pl.BlockSpec((2 * seqs, head), lambda h: (0, h))],
        out_shape=[tok(F32), tok(F32), struct((ext, r_all), BF16), struct((2 * seqs, r_all), F32)],
        compiler_params=params(),
        cost_estimate=cost(1, 14),
        name="back_scan",
    )(mid_low, full_output, branch_pre, state, recur, vec)
    core = seq.mine(0)

    def pair_operands(left, right):
        half = right.shape[1] // 2
        mine = lax.dynamic_slice_in_dim(right, core * half, half, 1)
        other = lax.dynamic_slice_in_dim(right, (1 - core) * half, half, 1)
        return left, jnp.concatenate([mine, seq.swap(other, 0)], axis=0)

    def pair_grad(left, right):
        g = outer_sum(*pair_operands(left, right)).astype(BF16)
        return g.reshape(n_seq, g.shape[0] // n_seq, g.shape[1])

    output_grad = pair_grad(mixed_two, mid_low)
    back_ends, output_grad = lax.optimization_barrier((back_ends, output_grad))
    adj_in = carry_call(back_ends, seqs, n_seq, n_mlp, True)
    branch_grad = pair_grad(normed_two, gbp)
    adj_in, branch_grad = lax.optimization_barrier((adj_in, branch_grad))
    while feed_state[0][3]:
        nexts = []
        for keep, got, left, order in feed_state:
            send, keep = split_chips(keep, got, left, order[0], seq)
            nexts.append((keep, send, [b for b in left if b != order[0]], order))
        adj_in, sends = lax.optimization_barrier((adj_in, [e[1] for e in nexts]))
        feed_state = [
            (keep, seq.swap(send, order[0]), left, order[1:])
            for (keep, _, left, order), send in zip(nexts, sends)
        ]

    gcin, gdw, giw, gvec, gnorm = pl.pallas_call(
        functools.partial(back_gates_kernel, heads),
        grid=(heads,),
        in_specs=[tok_head, tok_head, seq_head, tok_head, seq_head, tok_head, tok_head, tok_head,
                  ext_head, vec_head, decay_head, inject_head, ext_head, col_head, col_head],
        out_specs=[ext_head, decay_head, decay_head, vec_head, whole(ext, width)],
        out_shape=[struct((ext, r_all), BF16), struct((r_all, head), BF16), struct((r_all, head), BF16),
                   struct((8, r_all), F32), struct((ext, width), F32)],
        compiler_params=params(),
        cost_estimate=cost(2, 20),
        name="back_gates",
    )(back_prod, back_local, adj_in, state, state_in, recur, inject, conv_low,
      conv_in, vec, gates_all, gates_all, gbp, full_branch, full_input)

    weight_grad = pair_grad(normed_two, gcin)
    gates_mine = jnp.where(core == 0, gdw, giw)
    gates_got = seq.swap(jnp.where(core == 0, giw, gdw), 0)
    gates_grad = (gates_mine.astype(F32) + gates_got.astype(F32)).astype(BF16)

    stream_part, mixer_gain_grad = norm_back(
        stream_ext, inverse_ext, gain_mixer, gnorm.reshape(seqs, ext_rows, width)
    )
    next_part = lax.ppermute(
        stream_part[:, PAD - edge : PAD, :], both, [(i + 1, i) for i in range(n_dev - 1)]
    )
    next_part = jnp.pad(next_part, ((0, 0), (rows - edge, 0), (0, 0)))
    input_grad = mid_grad + stream_part[:, PAD:, :] + next_part

    param_grad = gvec[7] * -jax.nn.sigmoid(-param)
    gain_grads = jnp.pad(jnp.stack([mixer_gain_grad, feed_gain_grad]), ((0, 0), (0, r_all - width)))
    total = jnp.concatenate([gvec[:7], param_grad[None, :], gain_grads], axis=0)
    total = jnp.pad(total, ((0, 16 - total.shape[0]), (0, 0)))
    blocks = lambda g: g.reshape(n_seq, n_mlp, -1, g.shape[-1])
    owned, total = owners_call(
        [blocks(g) for g in (output_grad, branch_grad, gates_grad, weight_grad)], total, n_seq, n_mlp
    )
    output_out, branch_out, gates_out, input_out = owned
    decay_out, inject_out = gates_out[:, :head], gates_out[:, head:]
    total, arrived = lax.optimization_barrier((total, [e[1] for e in feed_state]))
    halves = [e[0].astype(F32) + got.astype(F32) for e, got in zip(feed_state, arrived)]
    feed_grads = [jnp.concatenate([v[i, 0] for v in halves], axis=0) for i in range(3)]
    place = seq.me * n_mlp + lax.axis_index("mlp")
    tail = lax.dynamic_slice_in_dim(total[:8], place * r_own, r_own, 1)
    gains_out = lax.dynamic_slice_in_dim(total[8:10], place * d_own, d_own, 1)

    return (
        result,
        input_grad,
        gains_out[0],
        branch_out,
        input_out,
        tail[:4],
        tail[4],
        decay_out,
        tail[5],
        inject_out,
        tail[6],
        tail[7],
        output_out,
        gains_out[1],
        feed_grads[0],
        feed_grads[1],
        feed_grads[2].T,
    )


def solution(mesh):
    both = ("seq", "mlp")
    in_specs = (
        P(None, both, None), P(both), P(both, None), P(both, None), P(None, both), P(both),
        P(both, None), P(both), P(both, None), P(both), P(both), P(both, None), P(both),
        P(None, "mlp"), P(None, "mlp"), P("mlp", None), P(None, both, None),
    )
    out_specs = (
        P(None, both, None), P(None, both, None), P(both), P(both, None), P(both, None), P(None, both),
        P(both), P(both, None), P(both), P(both, None), P(both), P(both), P(both, None), P(both),
        P("seq", "mlp"), P("seq", "mlp"), P("mlp", "seq"),
    )
    return jax.shard_map(
        per_device, mesh=mesh, in_specs=in_specs, out_specs=out_specs, check_vma=False
    )
```

```python
import functools
import math

import jax
import jax.numpy as jnp
from jax import lax
from jax.experimental import pallas as pl
from jax.experimental.pallas import tpu as pltpu
from jax.experimental.layout import Layout, with_layout_constraint
from jax.sharding import PartitionSpec as P

EPS = 1e-06
RATE_SCALE = 8.0
F32 = jnp.float32
BF16 = jnp.bfloat16
MESH = pl.DeviceIdType.MESH
PAD = 8
GELU_C = math.sqrt(2.0 / math.pi)
VMEM_LIMIT = 48 << 20


def gelu_and_slope(v):
    sq = v * v
    t = jnp.tanh(GELU_C * v * (1.0 + 0.044715 * sq))
    half = 0.5 * (1.0 + t)
    slope = half + 0.5 * v * (1.0 - t * t) * GELU_C * (1.0 + 3 * 0.044715 * sq)
    return v * half, slope


def gelu_only(v):
    return 0.5 * v * (1.0 + jnp.tanh(GELU_C * v * (1.0 + 0.044715 * (v * v))))


def decay_terms(recur, soft):
    log_rate = (-RATE_SCALE) * recur * soft
    rate = jnp.exp(log_rate)
    y = -2.0 * log_rate
    e = 1.0 - y * (1.0 / 10.0)
    for n in range(9, 1, -1):
        e = 1.0 - (y * (1.0 / n)) * e
    return rate, jnp.where(y < 0.5, y * e, 1.0 - rate * rate)


def norm_inverse(v):
    return lax.rsqrt(jnp.mean(v * v, axis=-1, keepdims=True) + EPS)


def tile_scan(a, b, reverse):
    row = lax.broadcasted_iota(jnp.int32, a.shape, 1)
    for d in (1, 2, 4):
        ok = (row < 8 - d) if reverse else (row >= d)
        shift = 8 - d if reverse else d
        a_near = jnp.where(ok, pltpu.roll(a, shift, 1), 1.0)
        b_near = jnp.where(ok, pltpu.roll(b, shift, 1), 0.0)
        b = b + a * b_near
        a = a * a_near
    return a, b


def part_scan(a, b, a_ref, b_ref, reverse):
    seqs, rows, lanes = a.shape
    tiles = rows // 8
    a, b = tile_scan(a.reshape(seqs * tiles, 8, lanes), b.reshape(seqs * tiles, 8, lanes), reverse)
    a = a.reshape(seqs, tiles, 8, lanes)
    b = b.reshape(seqs, tiles, 8, lanes)
    a_run = b_run = None
    edge = 0 if reverse else 7
    for i in range(tiles):
        t = tiles - 1 - i if reverse else i
        at, bt = a[:, t], b[:, t]
        if a_run is not None:
            bt = bt + at * b_run
            at = at * a_run
        a_ref[:, t * 8 : (t + 1) * 8, :] = at
        b_ref[:, t * 8 : (t + 1) * 8, :] = bt
        a_run, b_run = at[:, edge : edge + 1, :], bt[:, edge : edge + 1, :]
    return a_run[:, 0, :], b_run[:, 0, :]


def gates_kernel(seqs, n_ref, w_ref, dw_ref, iw_ref, vec_ref,
                 cin_ref, low_ref, rec_ref, inj_ref, prod_ref, loc_ref, ends_ref):
    cin = jnp.dot(n_ref[...], w_ref[...], preferred_element_type=F32).astype(BF16)
    cin_ref[...] = cin
    x = cin.astype(F32)
    ext, lanes = x.shape
    taps = vec_ref[...]
    y = taps[4:5, :] + taps[0:1, :] * x
    for k in range(1, 4):
        y = y + taps[k : k + 1, :] * pltpu.roll(x, k, 0)
    y = y.reshape(seqs, ext // seqs, lanes)[:, PAD:, :]
    low = y.astype(BF16)
    low_ref[...] = low
    shape = y.shape
    low2 = low.reshape(shape[0] * shape[1], lanes)
    dpre = jnp.dot(low2, dw_ref[...], preferred_element_type=F32)
    ipre = jnp.dot(low2, iw_ref[...], preferred_element_type=F32)
    recur = jax.nn.sigmoid(dpre + taps[5:6, :])
    inject = jax.nn.sigmoid(ipre + taps[6:7, :])
    rate, em = decay_terms(recur, taps[7:8, :])
    recur = recur.reshape(shape)
    inject = inject.reshape(shape)
    rec_ref[...] = recur
    inj_ref[...] = inject
    injected = jnp.sqrt(em).reshape(shape) * inject * low.astype(F32)
    pa, pb = part_scan(rate.reshape(shape), injected, prod_ref, loc_ref, False)
    ends_ref[0:seqs, :] = pa
    ends_ref[seqs : 2 * seqs, :] = pb


def mix_kernel(heads, loc_ref, prod_ref, bp_ref, carry_ref, w_ref, x_ref, gain_ref,
               state_ref, mixed_ref, mid_ref, feed_ref, acc_ref):
    h = pl.program_id(0)
    carry = carry_ref[...][:, None, :]
    state = loc_ref[...] + prod_ref[...] * carry
    state_ref[...] = state
    mixed = (state * gelu_only(bp_ref[...])).astype(BF16)
    mixed_ref[...] = mixed
    b, s, lanes = mixed.shape
    part = jnp.dot(mixed.reshape(b * s, lanes), w_ref[...], preferred_element_type=F32)

    @pl.when(h == 0)
    def _():
        acc_ref[...] = x_ref[...].astype(F32) + part

    @pl.when(h > 0)
    def _():
        acc_ref[...] += part

    @pl.when(h == heads - 1)
    def _():
        mid = acc_ref[...]
        mid_ref[...] = mid
        feed_ref[...] = (mid * norm_inverse(mid) * gain_ref[...]).astype(BF16)


def back_scan_kernel(seqs, g_ref, w_ref, bp_ref, state_ref, rec_ref, vec_ref,
                     prod_ref, adj_ref, gbp_ref, ends_ref):
    gm = lax.dot_general(g_ref[...], w_ref[...], (((1,), (1,)), ((), ())), preferred_element_type=F32)
    rows, lanes = gm.shape
    shape = (seqs, rows // seqs, lanes)
    act, slope = gelu_and_slope(bp_ref[...])
    gm = gm.reshape(shape)
    gbp = gm * state_ref[...] * slope
    gbp = jnp.concatenate([jnp.zeros((seqs, PAD, lanes), F32), gbp], axis=1)
    gbp_ref[...] = gbp.reshape(seqs * (shape[1] + PAD), lanes).astype(BF16)
    rate = jnp.exp((-RATE_SCALE) * rec_ref[...] * vec_ref[7:8, :])
    after = pltpu.roll(rate.reshape(rows, lanes), rows - 1, 0).reshape(shape)
    row = lax.broadcasted_iota(jnp.int32, shape, 1)
    after = jnp.where(row == shape[1] - 1, 1.0, after)
    pa, pb = part_scan(after, gm * act, prod_ref, adj_ref, True)
    first = rate[:, 0, :]
    ends_ref[0:seqs, :] = first * pa
    ends_ref[seqs : 2 * seqs, :] = first * pb


def back_gates_kernel(heads, prod_ref, adj_ref, carry_ref, state_ref, sin_ref, rec_ref, inj_ref, low_ref,
                      cin_ref, vec_ref, dw_ref, iw_ref, gbp_ref, bw_ref, cw_ref,
                      gcin_ref, gdw_ref, giw_ref, gvec_ref, gn_ref):
    h = pl.program_id(0)
    vec = vec_ref[...]
    soft = vec[7:8, :]
    adj = adj_ref[...] + prod_ref[...] * carry_ref[...][:, None, :]
    shape = adj.shape
    seqs, rows, lanes = shape
    flat = (seqs * rows, lanes)
    state = state_ref[...]
    prev = pltpu.roll(state.reshape(flat), 1, 0).reshape(shape)
    row = lax.broadcasted_iota(jnp.int32, shape, 1)
    prev = jnp.where(row == 0, sin_ref[...][:, None, :], prev)
    recur, inject = rec_ref[...], inj_ref[...]
    rate, em = decay_terms(recur, soft)
    mult = jnp.sqrt(em)
    low = low_ref[...]
    conv = low.astype(F32)
    g_log = adj * prev * rate - adj * inject * conv * (rate * rate) / mult
    am = adj * mult
    g_elem = am * inject
    g_rec = g_log * ((-RATE_SCALE) * soft)
    g_soft = jnp.sum((g_log * recur).reshape(flat), axis=0, keepdims=True) * (-RATE_SCALE)
    gdp = (g_rec * recur * (1.0 - recur)).reshape(flat)
    gip = (am * conv * inject * (1.0 - inject)).reshape(flat)
    gdp_low, gip_low = gdp.astype(BF16), gip.astype(BF16)
    low2 = low.reshape(flat)
    tok = (((0,), (0,)), ((), ()))
    last = (((1,), (1,)), ((), ()))
    gdw_ref[...] = lax.dot_general(low2, gdp_low, tok, preferred_element_type=F32).astype(BF16)
    giw_ref[...] = lax.dot_general(low2, gip_low, tok, preferred_element_type=F32).astype(BF16)
    gc = (
        g_elem.reshape(flat)
        + lax.dot_general(gdp_low, dw_ref[...], last, preferred_element_type=F32)
        + lax.dot_general(gip_low, iw_ref[...], last, preferred_element_type=F32)
    )
    gce = jnp.concatenate([jnp.zeros((seqs, PAD, lanes), F32), gc.reshape(shape)], axis=1)
    ext = seqs * (rows + PAD)
    gce = gce.reshape(ext, lanes)
    x = cin_ref[...].astype(F32)
    out = vec[0:1, :] * gce
    sums = [jnp.sum(gce * x, axis=0, keepdims=True)]
    for k in range(1, 4):
        out = out + vec[k : k + 1, :] * pltpu.roll(gce, ext - k, 0)
        sums.append(jnp.sum(gce * pltpu.roll(x, k, 0), axis=0, keepdims=True))
    sums.append(jnp.sum(gce, axis=0, keepdims=True))
    sums.append(jnp.sum(gdp, axis=0, keepdims=True))
    sums.append(jnp.sum(gip, axis=0, keepdims=True))
    sums.append(g_soft)
    for i, v in enumerate(sums):
        gvec_ref[i : i + 1, :] = v
    gcin = out.astype(BF16)
    gcin_ref[...] = gcin
    part = lax.dot_general(gcin, cw_ref[...], last, preferred_element_type=F32)
    part += lax.dot_general(gbp_ref[...], bw_ref[...], last, preferred_element_type=F32)

    @pl.when(h == 0)
    def _():
        gn_ref[...] = part

    @pl.when(h > 0)
    def _():
        gn_ref[...] += part


def carry_kernel(seqs, n_seq, n_mlp, reverse, ends_ref, out_ref, zbuf, sbuf, mine_low, total, ssem, rsem):
    ms, mz = lax.axis_index("seq"), lax.axis_index("mlp")
    barrier = pltpu.get_barrier_semaphore()
    for d in range(1, n_mlp):
        pl.semaphore_signal(barrier, inc=1, device_id=(ms, lax.rem(mz + d, n_mlp)), device_id_type=MESH)
    for d in range(1, n_seq):
        pl.semaphore_signal(barrier, inc=1, device_id=(lax.rem(ms + d, n_seq), mz), device_id_type=MESH)
    pl.semaphore_wait(barrier, n_mlp + n_seq - 2)
    mine_low[...] = ends_ref[...].astype(BF16)
    copies = []
    for d in range(1, n_mlp):
        copies.append(pltpu.make_async_remote_copy(
            src_ref=mine_low, dst_ref=zbuf.at[mz], send_sem=ssem.at[d - 1], recv_sem=rsem.at[d - 1],
            device_id=(ms, lax.rem(mz + d, n_mlp)), device_id_type=MESH))
        copies[-1].start()
    zbuf[mz] = mine_low[...]
    for c in copies:
        c.wait()
    shape = (seqs, ends_ref.shape[1])
    tp, ts = jnp.ones(shape, F32), jnp.zeros(shape, F32)
    pp, ps = tp, ts
    for i in range(n_mlp):
        z = n_mlp - 1 - i if reverse else i
        val = zbuf[z].astype(F32)
        p, s = val[0:seqs, :], val[seqs : 2 * seqs, :]
        ts = p * ts + s
        tp = p * tp
        mine = jnp.where((z > mz) if reverse else (z < mz), 1.0, 0.0)
        ps = mine * (p * ps + s) + (1.0 - mine) * ps
        pp = (mine * p + (1.0 - mine)) * pp
    total[...] = jnp.concatenate([tp, ts], axis=0).astype(BF16)
    copies = []
    for d in range(1, n_seq):
        i = n_mlp - 2 + d
        copies.append(pltpu.make_async_remote_copy(
            src_ref=total, dst_ref=sbuf.at[ms], send_sem=ssem.at[i], recv_sem=rsem.at[i],
            device_id=(lax.rem(ms + d, n_seq), mz), device_id_type=MESH))
        copies[-1].start()
    sbuf[ms] = total[...]
    for c in copies:
        c.wait()
    c = jnp.zeros(shape, F32)
    for i in range(n_seq):
        q = n_seq - 1 - i if reverse else i
        val = sbuf[q].astype(F32)
        p, s = val[0:seqs, :], val[seqs : 2 * seqs, :]
        mine = jnp.where((q > ms) if reverse else (q < ms), 1.0, 0.0)
        c = mine * (p * c + s) + (1.0 - mine) * c
    out_ref[...] = pp * c + ps


def carry_call(ends, seqs, n_seq, n_mlp, reverse):
    rows, width = ends.shape
    n = n_seq + n_mlp - 2
    return pl.pallas_call(
        functools.partial(carry_kernel, seqs, n_seq, n_mlp, reverse),
        out_shape=jax.ShapeDtypeStruct((seqs, width), F32),
        in_specs=[pl.BlockSpec(memory_space=pltpu.VMEM)],
        out_specs=pl.BlockSpec(memory_space=pltpu.VMEM),
        scratch_shapes=[
            pltpu.VMEM((n_mlp, rows, width), BF16),
            pltpu.VMEM((n_seq, rows, width), BF16),
            pltpu.VMEM((rows, width), BF16),
            pltpu.VMEM((rows, width), BF16),
            pltpu.SemaphoreType.DMA((n,)),
            pltpu.SemaphoreType.DMA((n,)),
        ],
        compiler_params=pltpu.CompilerParams(
            collective_id=1 if reverse else 0, has_side_effects=True, vmem_limit_bytes=VMEM_LIMIT
        ),
        cost_estimate=pl.CostEstimate(flops=0, bytes_accessed=200 * rows * width * 4, transcendentals=0),
        name="carry_back" if reverse else "carry_fwd",
    )(ends)


def spread_kernel(n_seq, n_mlp, plans, starts, order, *refs):
    ms, mz = lax.axis_index("seq"), lax.axis_index("mlp")
    count = len(plans)
    shards, outs = refs[:count], refs[count : 2 * count]
    ssem, rsem = refs[2 * count :]
    n_bits = n_seq.bit_length() - 1
    digit = lambda bit: lax.rem(lax.div(ms, 1 << bit), 2)
    seq_peer = lambda bit: (ms + (1 - 2 * digit(bit)) * (1 << bit), mz)
    used = [0]

    def block_of(mask):
        at = ms
        for bit in range(n_bits):
            if (mask >> bit) & 1:
                at = at + (1 - 2 * digit(bit)) * (1 << bit)
        return at

    barrier = pltpu.get_barrier_semaphore()
    for bit in range(n_bits):
        pl.semaphore_signal(barrier, inc=1, device_id=seq_peer(bit), device_id_type=MESH)
    for d in range(1, n_mlp):
        pl.semaphore_signal(barrier, inc=1, device_id=(ms, lax.rem(mz + d, n_mlp)), device_id_type=MESH)
    local = []
    for a, parts in enumerate(plans):
        dst = outs[a].at[ms, mz] if len(parts[0]) > 1 else outs[a].at[:, mz]
        local.append(pltpu.make_async_copy(shards[a], dst, rsem.at[used[0]]))
        local[-1].start()
        used[0] += 1
    pl.semaphore_wait(barrier, n_bits + n_mlp - 1)

    def send(src, dst, peer):
        i = used[0]
        used[0] += 1
        c = pltpu.make_async_remote_copy(
            src_ref=src, dst_ref=dst, send_sem=ssem.at[i], recv_sem=rsem.at[i],
            device_id=peer, device_id_type=MESH)
        c.start()
        return c

    state = [
        [{"held": [0], "all": False, "moved": False, "core": set()} for _ in parts] for parts in plans
    ]
    pending = [[] for _ in plans]

    def start(a, level):
        parts = plans[a]
        if level >= len(parts[0]):
            return
        if level > 0 and local[a] is not None:
            local[a].wait()
            local[a] = None
        for h, (stages, st) in enumerate(zip(parts, state[a])):
            stage = stages[level]
            if len(stages) == 1:
                for d in range(1, n_mlp):
                    z = lax.rem(mz + d, n_mlp)
                    pending[a].append(send(shards[a], outs[a].at[:, mz], (ms, z)))
                continue
            width = shards[a].shape[1] // len(parts)
            cols = pl.ds(h * width, width)

            def place(mask, dst):
                at = block_of(mask)
                if not dst and not st["moved"]:
                    return shards[a].at[:, cols]
                if st["all"]:
                    return outs[a].at[at, :, :, cols]
                return outs[a].at[at, mz, :, cols]

            if stage != "z" and st["all"]:
                for mask in st["held"]:
                    if mask not in st["core"]:
                        st["core"].add(mask)
                        pending[a].append(send(place(mask, False), place(mask, True), seq_peer(0)))
            if stage == 0:
                continue
            moves = [(place(mask, False), place(mask, True)) for mask in st["held"]]
            if stage == "z":
                peers = [(ms, lax.rem(mz + d, n_mlp)) for d in range(1, n_mlp)]
                st["all"] = True
            else:
                peers = [seq_peer(stage)]
                st["held"] = st["held"] + [mask | (1 << stage) for mask in st["held"]]
            st["moved"] = True
            for peer in peers:
                for src, dst in moves:
                    pending[a].append(send(src, dst, peer))

    def end(a):
        for c in pending[a]:
            c.wait()
        pending[a] = []

    for a in starts:
        start(a, 0)
    for a, level, after in order:
        if level < len(plans[a][0]):
            end(a)
            start(a, level + 1)
        for b in after:
            start(b, 0)
    for c in local:
        if c is not None:
            c.wait()


def spread_call(small, first, second, third, tokens, n_seq, n_mlp):
    chips, turned = chip_orders(n_seq)
    line = ["z"] + chips + [0]
    pair = [line, ["z"] + turned + [0]]
    cross = [chips[:1] + ["z"] + chips[1:] + [0], turned[:1] + ["z"] + turned[1:] + [0]]
    arrays = [small, first, second, third, tokens]
    plans = [[line], pair, pair, cross, [["z"]]]
    levels = len(line)
    order = []
    for t in range(levels + 1):
        if t < levels:
            order += [(0, t, []), (1, t, [2] if t == 0 else [])]
        if t > 0:
            order += [(2, t - 1, []), (3, t - 1, [4] if t == 1 else [])]
    order.append((4, 0, []))
    n_sem = len(arrays)
    for parts in plans:
        for stages in parts:
            held = 1
            for stage in stages:
                n_sem += held * (n_mlp - 1 if stage == "z" else 1)
                held *= 1 if stage == "z" else 2
    shapes = [(n_seq, n_mlp) + v.shape for v in arrays[:4]]
    shapes.append((tokens.shape[0], n_mlp) + tokens.shape[1:])
    return pl.pallas_call(
        functools.partial(spread_kernel, n_seq, n_mlp, plans, (0, 1, 3), order),
        out_shape=[jax.ShapeDtypeStruct(s, BF16) for s in shapes],
        in_specs=[pl.BlockSpec(memory_space=pltpu.VMEM)] * len(arrays),
        out_specs=[pl.BlockSpec(memory_space=pl.ANY)] * len(arrays),
        scratch_shapes=[pltpu.SemaphoreType.DMA((n_sem,)), pltpu.SemaphoreType.DMA((n_sem,))],
        compiler_params=pltpu.CompilerParams(
            collective_id=3, has_side_effects=True, vmem_limit_bytes=VMEM_LIMIT
        ),
        name="spread",
    )(*arrays)


def chip_orders(n_seq):
    chips = list(range(1, n_seq.bit_length() - 1))
    turn = len(chips) // 2
    return chips, chips[turn:] + chips[:turn]


def owners_plan(cols, n_seq, crossed, last):
    orders = chip_orders(n_seq)
    if crossed:
        orders = [o[:1] + ["z"] + o[1:] for o in orders]
    else:
        orders = [o + ["z"] for o in orders]
    tiles = cols // 128
    sizes = [tiles // 2, tiles - tiles // 2]
    if last and tiles >= 8:
        small = tiles // 5
        big = (tiles - 2 * small) // 2
        sizes = [big, big, small, tiles - 2 * big - small]
    units, at = [], 0
    for i in range(0, len(sizes), 2):
        unit = []
        for j in range(2):
            unit.append((at, sizes[i + j] * 128, tuple(orders[j])))
            at += sizes[i + j] * 128
        units.append(unit)
    return units


def owners_shapes(n_seq, n_mlp, rows, width, stages):
    blocks, z = n_seq, n_mlp
    out = []
    for stage in stages:
        if stage == "z":
            arrive = (n_mlp - 1, blocks, rows, width)
            z = 1
        else:
            blocks //= 2
            arrive = (blocks, z, rows, width)
        out.append((arrive, (blocks, z, rows, width)))
    return out


def owners_kernel(n_seq, n_mlp, count, units, *refs):
    ms, mz = lax.axis_index("seq"), lax.axis_index("mlp")
    arrays, vec = refs[:count], refs[count]
    outs, vec_out = refs[count + 1 : 2 * count + 1], refs[2 * count + 1]
    scratch = list(refs[2 * count + 2 :])
    vec_in, vec_sum, ssem, rsem = scratch[-4:]
    n_bits = n_seq.bit_length() - 1
    mine = lambda bit: lax.rem(lax.div(ms, 1 << bit), 2)
    seq_peer = lambda bit: (ms + (1 - 2 * mine(bit)) * (1 << bit), mz)
    core = mine(0)
    used = [0]

    barrier = pltpu.get_barrier_semaphore()
    for bit in range(n_bits):
        pl.semaphore_signal(barrier, inc=1, device_id=seq_peer(bit), device_id_type=MESH)
    for d in range(1, n_mlp):
        pl.semaphore_signal(barrier, inc=1, device_id=(ms, lax.rem(mz + d, n_mlp)), device_id_type=MESH)
    pl.semaphore_wait(barrier, n_bits + n_mlp - 1)

    def send(src, dst, peer):
        i = used[0]
        used[0] += 1
        c = pltpu.make_async_remote_copy(
            src_ref=src, dst_ref=dst, send_sem=ssem.at[i], recv_sem=rsem.at[i],
            device_id=peer, device_id_type=MESH)
        c.start()
        return c

    def load(src, dst):
        i = used[0]
        used[0] += 1
        c = pltpu.make_async_copy(src, dst, rsem.at[i])
        c.start()
        return c

    tasks = []
    for unit in units:
        group = []
        for a, at, width, stages in unit:
            t = {"a": a, "at": at, "cols": pl.ds(at, width), "stages": stages, "recv": [], "sum": []}
            t["own"] = scratch.pop(0)
            for _ in stages:
                t["recv"].append(scratch.pop(0))
                t["sum"].append(scratch.pop(0))
            t["csend"], t["crecv"] = scratch.pop(0), scratch.pop(0)
            left, t["runs"] = list(range(n_bits))[::-1], []
            for stage in stages:
                if stage == "z":
                    t["runs"].append(None)
                    continue
                pos = left.index(stage)
                t["runs"].append((1 << pos, 1 << (len(left) - 1 - pos)))
                left.remove(stage)
            group.append(t)
        tasks.append(group)

    def joined(t, side):
        half = arrays[t["a"]].shape[3]
        return pl.ds(pl.multiple_of(side * half + t["at"], 128), t["csend"].shape[1])

    def begin(t, i):
        stage = t["stages"][i]
        t["wait"] = []
        if stage == "z":
            for d in range(1, n_mlp):
                z = lax.rem(mz + d, n_mlp)
                t["wait"].append(send(t["sum"][i - 1].at[:, z], t["recv"][i].at[d - 1], (ms, z)))
            return
        runs, length = t["runs"][i]
        for j in range(runs):
            away = pl.ds((2 * j + 1 - mine(stage)) * length, length)
            home = pl.ds((2 * j + mine(stage)) * length, length)
            to = pl.ds(j * length, length)
            if i == 0:
                src = arrays[t["a"]].at[away, :, :, t["cols"]]
                t["wait"].append(load(arrays[t["a"]].at[home, :, :, t["cols"]], t["own"].at[to]))
            else:
                src = t["sum"][i - 1].at[away]
            t["wait"].append(send(src, t["recv"][i].at[to], seq_peer(stage)))

    def finish(t, i):
        for c in t["wait"]:
            c.wait()
        stage = t["stages"][i]
        recv, total = t["recv"][i], t["sum"][i]
        blocks, zs = total.shape[0], total.shape[1]
        kind = total.dtype
        if stage == "z":
            for k in range(blocks):
                v = t["sum"][i - 1][k, mz].astype(F32)
                for d in range(1, n_mlp):
                    v = v + recv[d - 1, k].astype(F32)
                total[k, 0] = v.astype(kind)
        else:
            runs, length = t["runs"][i]
            for j in range(runs):

                def add(n, _, j=j):
                    b, q = lax.div(n, zs), lax.rem(n, zs)
                    if i == 0:
                        kept = t["own"][j * length + b, q]
                    else:
                        kept = t["sum"][i - 1][(2 * j + mine(stage)) * length + b, q]
                    v = kept.astype(F32) + recv[j * length + b, q].astype(F32)
                    total[j * length + b, q] = v.astype(kind)
                    return 0

                lax.fori_loop(0, length * zs, add, 0)
        if i + 1 < len(t["stages"]):
            begin(t, i + 1)
        else:
            outs[t["a"]][:, joined(t, core)] = total[core, 0]
            t["csend"][...] = total[1 - core, 0].astype(BF16)
            t["wait"] = [send(t["csend"], t["crecv"], seq_peer(0))]

    def close(t):
        for c in t["wait"]:
            c.wait()
        outs[t["a"]][:, joined(t, 1 - core)] = t["crecv"][...].astype(F32)

    vec_peers = []
    for bit in range(n_mlp.bit_length() - 1):
        side = lax.rem(lax.div(mz, 1 << bit), 2)
        vec_peers.append((ms, mz + (1 - 2 * side) * (1 << bit)))
    vec_peers += [seq_peer(bit) for bit in range(n_bits)]
    vec_state = [None, 0]

    def vec_step():
        copy, i = vec_state
        if copy is not None:
            copy.wait()
            before = vec[...] if i == 1 else vec_sum[i - 2]
            v = before + vec_in[i - 1]
            if i == len(vec_peers):
                vec_out[...] = v
            else:
                vec_sum[i - 1] = v
        vec_state[0] = None
        if i < len(vec_peers):
            src = vec if i == 0 else vec_sum.at[i - 1]
            vec_state[:] = [send(src, vec_in.at[i], vec_peers[i]), i + 1]

    n_stages = len(tasks[0][0]["stages"])
    for group in tasks[:2]:
        for t in group:
            begin(t, 0)
    vec_step()
    for step in range(len(tasks) + n_stages):
        for i in range(n_stages + 1):
            u = step - i
            if not 0 <= u < len(tasks):
                continue
            for t in tasks[u]:
                if i < n_stages:
                    finish(t, i)
                else:
                    close(t)
            if i == 0 and u + 2 < len(tasks):
                for t in tasks[u + 2]:
                    begin(t, 0)
        vec_step()
    while vec_state[0] is not None:
        vec_step()


def owners_call(arrays, vec, n_seq, n_mlp):
    units, scratch, n_sem = [], [], 0
    for a, v in enumerate(arrays):
        plan = owners_plan(v.shape[3], n_seq, a == 0, a == len(arrays) - 1)
        units += [[(a,) + part for part in unit] for unit in plan]
    for unit in units:
        for a, at, width, stages in unit:
            rows = arrays[a].shape[2]
            scratch.append(pltpu.VMEM((n_seq // 2, n_mlp, rows, width), BF16))
            shapes = owners_shapes(n_seq, n_mlp, rows, width, stages)
            for i, (arrive, total) in enumerate(shapes):
                scratch.append(pltpu.VMEM(arrive, BF16))
                scratch.append(pltpu.VMEM(total, F32 if i == len(shapes) - 1 else BF16))
            scratch += [pltpu.VMEM((rows, width), BF16)] * 2
            n_sem += 3 * n_seq + n_mlp
    steps = (n_mlp.bit_length() - 1) + (n_seq.bit_length() - 1)
    n_sem += steps
    vmem = pl.BlockSpec(memory_space=pltpu.VMEM)
    outs = pl.pallas_call(
        functools.partial(owners_kernel, n_seq, n_mlp, len(arrays), units),
        out_shape=[jax.ShapeDtypeStruct((v.shape[2], 2 * v.shape[3]), F32) for v in arrays]
        + [jax.ShapeDtypeStruct(vec.shape, F32)],
        in_specs=[pl.BlockSpec(memory_space=pl.ANY)] * len(arrays) + [vmem],
        out_specs=[vmem] * (len(arrays) + 1),
        scratch_shapes=scratch + [
            pltpu.VMEM((steps,) + vec.shape, F32),
            pltpu.VMEM((steps,) + vec.shape, F32),
            pltpu.SemaphoreType.DMA((n_sem,)),
            pltpu.SemaphoreType.DMA((n_sem,)),
        ],
        compiler_params=pltpu.CompilerParams(
            collective_id=2, has_side_effects=True, vmem_limit_bytes=60 << 20
        ),
        name="owners",
    )(*arrays, vec)
    return outs[:-1], outs[-1]


def split_kernel(parts, kept, sides_ref, *refs):
    ins, outs = refs[: 2 * parts], refs[2 * parts + kept :]
    for i in range(parts):
        total = ins[2 * i][...].astype(F32) + ins[2 * i + 1][...].astype(F32)
        outs[i][...] = total.reshape(outs[i].shape).astype(outs[i].dtype)


def split_place(j, pos, blocks, side):
    length = blocks >> (pos + 1)
    return (2 * lax.div(j, length) + side) * length + lax.rem(j, length)


def split_cores(own, got, a, arrays, seq, bufs):
    blocks, rows, cols = got.shape
    half = rows // 2
    left = seq.bits[::-1][:-1]
    own = own.reshape(2 * blocks, 2, half, cols)
    got = got.reshape(blocks, 2, half, cols)
    sides = jnp.stack([seq.mine(0)] + [seq.mine(o[0]) for o in seq.orders])
    block = (1, 1, half, cols)
    ins, args = [], []
    for h in range(2):
        pos = left.index(seq.orders[h][0])
        for flip in (1, 0):

            def at(j, s, h=h, pos=pos, flip=flip):
                side = 1 - s[1 + h] if flip else s[1 + h]
                return split_place(j, pos, blocks, side)

            ins.append(pl.BlockSpec(block, lambda j, s, at=at, h=h: (2 * at(j, s) + s[0], h, 0, 0)))
            ins.append(pl.BlockSpec(block, lambda j, s, at=at, h=h: (at(j, s), h, 0, 0)))
            args += [own, got]
    kept = 0 if bufs is None else 4
    shape = (arrays, blocks // 2, half, cols)
    return pl.pallas_call(
        functools.partial(split_kernel, 4, kept),
        grid_spec=pltpu.PrefetchScalarGridSpec(
            num_scalar_prefetch=1,
            grid=(blocks // 2,),
            in_specs=ins + [pl.BlockSpec(memory_space=pl.ANY)] * kept,
            out_specs=[pl.BlockSpec(block, lambda j, s: (a, j, 0, 0))] * 4,
        ),
        out_shape=[jax.ShapeDtypeStruct(shape, BF16)] * 4,
        input_output_aliases={9 + i: i for i in range(kept)},
        compiler_params=pltpu.CompilerParams(vmem_limit_bytes=VMEM_LIMIT),
        cost_estimate=pl.CostEstimate(flops=0, bytes_accessed=6 * own.size, transcendentals=0),
        name="split_cores",
    )(sides, *args, *(bufs or ()))


def split_chips(keep, got, left, bit, seq):
    arrays, blocks, rows, cols = keep.shape
    pos = left.index(bit)
    block = (1, 1, rows, cols)
    sides = seq.mine(bit)[None]
    ins, args = [], []
    for flip in (1, 0):

        def at(j, s, flip=flip):
            return split_place(j, pos, blocks, 1 - s[0] if flip else s[0])

        ins += [pl.BlockSpec(block, lambda i, j, s, at=at: (i, at(j, s), 0, 0))] * 2
        args += [keep, got]
    return pl.pallas_call(
        functools.partial(split_kernel, 2, 0),
        grid_spec=pltpu.PrefetchScalarGridSpec(
            num_scalar_prefetch=1,
            grid=(arrays, blocks // 2),
            in_specs=ins,
            out_specs=[pl.BlockSpec(block, lambda i, j, s: (i, j, 0, 0))] * 2,
        ),
        out_shape=[jax.ShapeDtypeStruct((arrays, blocks // 2, rows, cols), BF16)] * 2,
        compiler_params=pltpu.CompilerParams(vmem_limit_bytes=VMEM_LIMIT),
        cost_estimate=pl.CostEstimate(flops=0, bytes_accessed=6 * keep.size, transcendentals=0),
        name="split_chips",
    )(sides, *args)


def join_kernel(*refs):
    ins, outs = refs[:4], refs[4:]
    for i, out in enumerate(outs):
        halves = [ins[k][i, 0].astype(F32) + ins[k + 1][i, 0].astype(F32) for k in (0, 2)]
        v = jnp.concatenate(halves, axis=0)
        out[...] = v.T if i == len(outs) - 1 else v


def join_halves(feed_state):
    arrays, _, half, cols = feed_state[0][0].shape
    shapes = [(2 * half, cols)] * (arrays - 1) + [(cols, 2 * half)]
    args = [v for e in feed_state for v in e[:2]]
    vmem = pl.BlockSpec(memory_space=pltpu.VMEM)
    return pl.pallas_call(
        join_kernel,
        out_shape=[jax.ShapeDtypeStruct(v, F32) for v in shapes],
        in_specs=[vmem] * len(args),
        out_specs=[vmem] * arrays,
        compiler_params=pltpu.CompilerParams(vmem_limit_bytes=VMEM_LIMIT),
        cost_estimate=pl.CostEstimate(
            flops=0, bytes_accessed=4 * arrays * 2 * half * cols * 2, transcendentals=0
        ),
        name="join_halves",
    )(*args)


class Seq:
    def __init__(self):
        self.n = lax.axis_size("seq")
        self.me = lax.axis_index("seq")
        self.bits = list(range(self.n.bit_length() - 1))
        chips = self.bits[1:]
        turn = len(chips) // 2
        self.orders = (chips, chips[turn:] + chips[:turn])

    def mine(self, bit):
        return (self.me >> bit) & 1

    def swap(self, v, bit):
        return lax.ppermute(v, "seq", [(i, i ^ (1 << bit)) for i in range(self.n)])


def flat_dot(left, right):
    shape = left.shape
    out = jnp.dot(left.reshape(-1, shape[-1]), right, preferred_element_type=F32)
    return out.reshape(shape[:-1] + (right.shape[1],))


def dot_against(left, right):
    shape = left.shape
    out = lax.dot_general(
        left.reshape(-1, shape[-1]), right, (((1,), (1,)), ((), ())), preferred_element_type=F32
    )
    return out.reshape(shape[:-1] + (right.shape[0],))


def outer_sum(left, right):
    return lax.dot_general(
        left.reshape(-1, left.shape[-1]),
        right.reshape(-1, right.shape[-1]),
        (((0,), (0,)), ((), ())),
        preferred_element_type=F32,
    )


def gated_unit(gate_pre, up_pre):
    return jax.nn.gelu(gate_pre) * up_pre


def norm_back(values, inverse, gain, upstream):
    scaled = upstream * gain
    gain_grad = jnp.sum(upstream * values * inverse, axis=(0, 1))
    inner_mean = jnp.mean(scaled * values, axis=-1, keepdims=True)
    return (inverse * (scaled - values * inner_mean * inverse * inverse), gain_grad)


def per_device(inputs, mixer_gain, branch_weight, input_weight, conv_weight, conv_bias, decay_weight,
               decay_bias, inject_weight, inject_bias, decay_param, output_weight, feed_gain,
               feed_gate, feed_up, feed_down, cotangent):
    both = ("seq", "mlp")
    seq = Seq()
    n_seq, n_mlp = seq.n, lax.axis_size("mlp")
    n_dev = n_seq * n_mlp
    seqs, rows, width = inputs.shape
    taps, r_own = conv_weight.shape
    edge = taps - 1
    head = decay_weight.shape[1]
    r_all = r_own * n_dev
    heads = r_all // head
    d_own = width // n_dev
    ext_rows = rows + PAD
    ext = seqs * ext_rows
    tokens = seqs * rows

    lanes = 128
    small = [conv_weight.T, conv_bias[:, None], decay_bias[:, None], inject_bias[:, None], decay_param[:, None]]
    gains = [jnp.pad(g, (0, r_own - d_own))[:, None] for g in (mixer_gain, feed_gain)]
    small = jnp.concatenate(small + gains, axis=1)
    small = jnp.pad(small, ((0, 0), (0, lanes - small.shape[1])))
    gates_own = jnp.concatenate([decay_weight, inject_weight, small], axis=1)
    n_chunks = 2 if seqs % 2 == 0 else 1
    per = seqs // n_chunks
    chunk = lambda v, c: v[c * per : (c + 1) * per]
    gates_all, full_input, full_branch, full_output, first_cot = spread_call(
        gates_own, input_weight, branch_weight, output_weight, chunk(cotangent, 0), n_seq, n_mlp
    )
    gates_all = gates_all.reshape(r_all, -1)
    full_input, full_branch = (v.reshape(width, r_all) for v in (full_input, full_branch))
    full_output = full_output.reshape(r_all, width)
    grad_rows = [first_cot.reshape(per, n_mlp * rows, width)]
    for c in range(1, n_chunks):
        gates_all, cot = lax.optimization_barrier((gates_all, chunk(cotangent, c)))
        grad_rows.append(lax.all_gather(cot, "mlp", axis=1, tiled=True))
    vectors = gates_all[:, 2 * head :].astype(F32)
    gain_rows = vectors[:, 8:10].reshape(n_dev, r_own, 2)[:, :d_own, :].reshape(width, 2)
    gain_mixer, gain_feed = gain_rows[:, 0], gain_rows[:, 1]
    param = vectors[:, 7]
    vec = jnp.concatenate([vectors[:, :7].T, jax.nn.softplus(-param)[None, :]], axis=0)

    last_tokens = lax.ppermute(inputs[:, rows - edge :, :], both, [(i, i + 1) for i in range(n_dev - 1)])
    x_ext = jnp.concatenate(
        [jnp.zeros((seqs, PAD - edge, width), BF16), last_tokens, inputs], axis=1
    )
    stream_ext = x_ext.astype(F32)
    inverse_ext = norm_inverse(stream_ext)
    normed_ext = (stream_ext * inverse_ext * gain_mixer).astype(BF16).reshape(ext, width)

    params = lambda **k: pltpu.CompilerParams(dimension_semantics=("arbitrary",), vmem_limit_bytes=VMEM_LIMIT, **k)

    def cost(big_dots, arrays):
        whole_mats = 2 * ext * width * r_all
        return pl.CostEstimate(
            flops=big_dots * whole_mats,
            bytes_accessed=big_dots * 2 * width * r_all + arrays * 4 * tokens * r_all,
            transcendentals=4 * tokens * r_all,
        )

    tok_head = pl.BlockSpec((seqs, rows, head), lambda h: (0, 0, h))
    ext_head = pl.BlockSpec((ext, head), lambda h: (0, h))
    vec_head = pl.BlockSpec((8, head), lambda h: (0, h))
    seq_head = pl.BlockSpec((seqs, head), lambda h: (0, h))
    col_head = pl.BlockSpec((width, head), lambda h: (0, h))
    row_head = pl.BlockSpec((head, width), lambda h: (h, 0))
    decay_head = pl.BlockSpec((head, head), lambda h: (h, 0))
    inject_head = pl.BlockSpec((head, head), lambda h: (h, 1))
    whole = lambda *shape: pl.BlockSpec(shape, lambda h: (0,) * len(shape))
    tok = lambda kind: jax.ShapeDtypeStruct((seqs, rows, r_all), kind)
    struct = jax.ShapeDtypeStruct

    conv_in, conv_low, recur, inject, prod, local, ends = pl.pallas_call(
        functools.partial(gates_kernel, seqs),
        grid=(heads,),
        in_specs=[whole(ext, width), col_head, decay_head, inject_head, vec_head],
        out_specs=[ext_head, tok_head, tok_head, tok_head, tok_head, tok_head,
                   pl.BlockSpec((2 * seqs, head), lambda h: (0, h))],
        out_shape=[struct((ext, r_all), BF16), tok(BF16), tok(F32), tok(F32), tok(F32), tok(F32),
                   struct((2 * seqs, r_all), F32)],
        compiler_params=params(),
        cost_estimate=cost(1, 20),
        name="gates",
    )(normed_ext, full_input, gates_all, gates_all, vec)

    state_in = carry_call(ends, seqs, n_seq, n_mlp, False)
    normed = normed_ext.reshape(seqs, ext_rows, width)[:, PAD:, :]
    branch_pre = flat_dot(normed, full_branch)

    state, mixed, mid, feed_low = pl.pallas_call(
        functools.partial(mix_kernel, heads),
        grid=(heads,),
        in_specs=[tok_head, tok_head, tok_head, seq_head, row_head, whole(tokens, width), whole(1, width)],
        out_specs=[tok_head, tok_head, whole(tokens, width), whole(tokens, width)],
        out_shape=[tok(F32), tok(BF16), struct((tokens, width), F32), struct((tokens, width), BF16)],
        scratch_shapes=[pltpu.VMEM((tokens, width), F32)],
        compiler_params=params(),
        cost_estimate=cost(1, 12),
        name="mix",
    )(local, prod, branch_pre, state_in, full_output, inputs.reshape(tokens, width), gain_feed[None, :])
    stream_mid = mid.reshape(seqs, rows, width)

    feed_own = feed_low.reshape(seqs, rows, width)
    row_major = lambda v: with_layout_constraint(v, Layout(major_to_minor=tuple(range(v.ndim))))
    mixed_two = mixed.reshape(tokens, r_all)
    mixed_two = jnp.concatenate([mixed_two, seq.swap(mixed_two, 0)], axis=0)
    normed_two = jnp.concatenate([normed_ext, seq.swap(normed_ext, 0)], axis=0)
    grad_hidden = [dot_against(v, feed_down) for v in grad_rows]
    grad_rows = jnp.concatenate(grad_rows, axis=0)
    feed_rows, hidden, gate_low, up_low, feed_norm_grad = [], [], [], [], []
    for c in range(n_chunks):
        f = row_major(lax.all_gather(chunk(feed_own, c), "mlp", axis=1, tiled=True))
        if c == 0:
            f, grad_hidden, mixed_two, normed_two = lax.optimization_barrier(
                (f, grad_hidden, mixed_two, normed_two)
            )
        else:
            f, back = lax.optimization_barrier((f, back))
            feed_norm_grad.append(lax.psum_scatter(back, "mlp", scatter_dimension=1, tiled=True))
        gate_pre = flat_dot(f, feed_gate)
        up_pre = flat_dot(f, feed_up)
        hidden.append(gated_unit(gate_pre, up_pre).astype(BF16))
        gate_grad, up_grad = jax.vjp(gated_unit, gate_pre, up_pre)[1](grad_hidden[c])
        gate_low.append(gate_grad.astype(BF16))
        up_low.append(up_grad.astype(BF16))
        feed_rows.append(f)
        back = (dot_against(gate_low[-1], feed_gate) + dot_against(up_low[-1], feed_up)).astype(BF16)
    back, feed_rows, hidden, gate_low, up_low = lax.optimization_barrier(
        (back, feed_rows, hidden, gate_low, up_low)
    )
    feed_norm_grad, back, hidden = lax.optimization_barrier((feed_norm_grad, back, hidden))
    feed_norm_grad.append(lax.psum_scatter(back, "mlp", scatter_dimension=1, tiled=True))
    feed_rows, hidden, gate_low, up_low = (
        jnp.concatenate(v, axis=0) for v in (feed_rows, hidden, gate_low, up_low)
    )
    feed_out = flat_dot(hidden, feed_down).astype(BF16)
    bufs = None
    pairs = ((feed_rows, gate_low), (feed_rows, up_low), (grad_rows, hidden))
    for a, (left, right) in enumerate(pairs):
        g = row_major(outer_sum(left, right).astype(BF16)).reshape(n_seq, width // n_seq, feed_gate.shape[1])
        other = lax.dynamic_index_in_dim(
            g.reshape((n_seq // 2, 2) + g.shape[1:]), 1 - seq.mine(0), 1, keepdims=False
        )
        bufs = list(split_cores(g, seq.swap(other, 0), a, len(pairs), seq, bufs))
    feed_norm_grad, feed_out, bufs[1], bufs[3] = lax.optimization_barrier(
        (feed_norm_grad, feed_out, bufs[1], bufs[3])
    )
    chip_bits = seq.bits[::-1][:-1]
    feed_state = [
        (bufs[2 * h + 1], seq.swap(bufs[2 * h], order[0]), [b for b in chip_bits if b != order[0]], order[1:])
        for h, order in enumerate(seq.orders)
    ]
    feed_norm_grad = jnp.concatenate(feed_norm_grad, axis=0).astype(F32)
    feed_out = lax.psum_scatter(feed_out, "mlp", scatter_dimension=1, tiled=True).astype(F32)
    result = (stream_mid + feed_out).astype(BF16)

    feed_inverse = norm_inverse(stream_mid)
    mid_part, feed_gain_grad = norm_back(stream_mid, feed_inverse, gain_feed, feed_norm_grad)
    mid_grad = cotangent.astype(F32) + mid_part
    mid_low = mid_grad.astype(BF16).reshape(tokens, width)

    back_prod, back_local, gbp, back_ends = pl.pallas_call(
        functools.partial(back_scan_kernel, seqs),
        grid=(heads,),
        in_specs=[whole(tokens, width), row_head, tok_head, tok_head, tok_head, vec_head],
        out_specs=[tok_head, tok_head, ext_head, pl.BlockSpec((2 * seqs, head), lambda h: (0, h))],
        out_shape=[tok(F32), tok(F32), struct((ext, r_all), BF16), struct((2 * seqs, r_all), F32)],
        compiler_params=params(),
        cost_estimate=cost(1, 14),
        name="back_scan",
    )(mid_low, full_output, branch_pre, state, recur, vec)
    core = seq.mine(0)

    def pair_operands(left, right):
        half = right.shape[1] // 2
        mine = lax.dynamic_slice_in_dim(right, core * half, half, 1)
        other = lax.dynamic_slice_in_dim(right, (1 - core) * half, half, 1)
        return left, jnp.concatenate([mine, seq.swap(other, 0)], axis=0)

    def pair_grad(left, right):
        g = outer_sum(*pair_operands(left, right)).astype(BF16)
        return g.reshape(n_seq, g.shape[0] // n_seq, g.shape[1])

    output_grad = pair_grad(mixed_two, mid_low)
    back_ends, output_grad = lax.optimization_barrier((back_ends, output_grad))
    adj_in = carry_call(back_ends, seqs, n_seq, n_mlp, True)
    branch_grad = pair_grad(normed_two, gbp)
    adj_in, branch_grad = lax.optimization_barrier((adj_in, branch_grad))
    while feed_state[0][3]:
        nexts = []
        for keep, got, left, order in feed_state:
            send, keep = split_chips(keep, got, left, order[0], seq)
            nexts.append((keep, send, [b for b in left if b != order[0]], order))
        adj_in, sends = lax.optimization_barrier((adj_in, [e[1] for e in nexts]))
        feed_state = [
            (keep, seq.swap(send, order[0]), left, order[1:])
            for (keep, _, left, order), send in zip(nexts, sends)
        ]

    gcin, gdw, giw, gvec, gnorm = pl.pallas_call(
        functools.partial(back_gates_kernel, heads),
        grid=(heads,),
        in_specs=[tok_head, tok_head, seq_head, tok_head, seq_head, tok_head, tok_head, tok_head,
                  ext_head, vec_head, decay_head, inject_head, ext_head, col_head, col_head],
        out_specs=[ext_head, decay_head, decay_head, vec_head, whole(ext, width)],
        out_shape=[struct((ext, r_all), BF16), struct((r_all, head), BF16), struct((r_all, head), BF16),
                   struct((8, r_all), F32), struct((ext, width), F32)],
        compiler_params=params(),
        cost_estimate=cost(2, 20),
        name="back_gates",
    )(back_prod, back_local, adj_in, state, state_in, recur, inject, conv_low,
      conv_in, vec, gates_all, gates_all, gbp, full_branch, full_input)

    weight_grad = pair_grad(normed_two, gcin)
    gates_mine = jnp.where(core == 0, gdw, giw)
    gates_got = seq.swap(jnp.where(core == 0, giw, gdw), 0)
    gates_grad = (gates_mine.astype(F32) + gates_got.astype(F32)).astype(BF16)

    stream_part, mixer_gain_grad = norm_back(
        stream_ext, inverse_ext, gain_mixer, gnorm.reshape(seqs, ext_rows, width)
    )
    next_part = lax.ppermute(
        stream_part[:, PAD - edge : PAD, :], both, [(i + 1, i) for i in range(n_dev - 1)]
    )
    next_part = jnp.pad(next_part, ((0, 0), (rows - edge, 0), (0, 0)))
    input_grad = mid_grad + stream_part[:, PAD:, :] + next_part

    param_grad = gvec[7] * -jax.nn.sigmoid(-param)
    gain_grads = jnp.pad(jnp.stack([mixer_gain_grad, feed_gain_grad]), ((0, 0), (0, r_all - width)))
    total = jnp.concatenate([gvec[:7], param_grad[None, :], gain_grads], axis=0)
    total = jnp.pad(total, ((0, 16 - total.shape[0]), (0, 0)))
    blocks = lambda g: g.reshape(n_seq, n_mlp, -1, g.shape[-1])
    owned, total = owners_call(
        [blocks(g) for g in (output_grad, branch_grad, gates_grad, weight_grad)], total, n_seq, n_mlp
    )
    output_out, branch_out, gates_out, input_out = owned
    decay_out, inject_out = gates_out[:, :head], gates_out[:, head:]
    total, arrived = lax.optimization_barrier((total, [e[1] for e in feed_state]))
    feed_grads = join_halves([(e[0], got) for e, got in zip(feed_state, arrived)])
    place = seq.me * n_mlp + lax.axis_index("mlp")
    tail = lax.dynamic_slice_in_dim(total[:8], place * r_own, r_own, 1)
    gains_out = lax.dynamic_slice_in_dim(total[8:10], place * d_own, d_own, 1)

    return (
        result,
        input_grad,
        gains_out[0],
        branch_out,
        input_out,
        tail[:4],
        tail[4],
        decay_out,
        tail[5],
        inject_out,
        tail[6],
        tail[7],
        output_out,
        gains_out[1],
        feed_grads[0],
        feed_grads[1],
        feed_grads[2],
    )


def solution(mesh):
    both = ("seq", "mlp")
    in_specs = (
        P(None, both, None), P(both), P(both, None), P(both, None), P(None, both), P(both),
        P(both, None), P(both), P(both, None), P(both), P(both), P(both, None), P(both),
        P(None, "mlp"), P(None, "mlp"), P("mlp", None), P(None, both, None),
    )
    out_specs = (
        P(None, both, None), P(None, both, None), P(both), P(both, None), P(both, None), P(None, both),
        P(both), P(both, None), P(both), P(both, None), P(both), P(both), P(both, None), P(both),
        P("seq", "mlp"), P("seq", "mlp"), P("mlp", "seq"),
    )
    return jax.shard_map(
        per_device, mesh=mesh, in_specs=in_specs, out_specs=out_specs, check_vma=False
    )
```

```python
import functools
import math

import jax
import jax.numpy as jnp
from jax import lax
from jax.experimental import pallas as pl
from jax.experimental.pallas import tpu as pltpu
from jax.experimental.layout import Layout, with_layout_constraint
from jax.sharding import PartitionSpec as P

EPS = 1e-06
RATE_SCALE = 8.0
F32 = jnp.float32
BF16 = jnp.bfloat16
MESH = pl.DeviceIdType.MESH
PAD = 8
GELU_C = math.sqrt(2.0 / math.pi)
VMEM_LIMIT = 48 << 20


def gelu_and_slope(v):
    sq = v * v
    t = jnp.tanh(GELU_C * v * (1.0 + 0.044715 * sq))
    half = 0.5 * (1.0 + t)
    slope = half + 0.5 * v * (1.0 - t * t) * GELU_C * (1.0 + 3 * 0.044715 * sq)
    return v * half, slope


def gelu_only(v):
    return 0.5 * v * (1.0 + jnp.tanh(GELU_C * v * (1.0 + 0.044715 * (v * v))))


def decay_terms(recur, soft):
    log_rate = (-RATE_SCALE) * recur * soft
    rate = jnp.exp(log_rate)
    y = -2.0 * log_rate
    e = 1.0 - y * (1.0 / 10.0)
    for n in range(9, 1, -1):
        e = 1.0 - (y * (1.0 / n)) * e
    return rate, jnp.where(y < 0.5, y * e, 1.0 - rate * rate)


def norm_inverse(v):
    return lax.rsqrt(jnp.mean(v * v, axis=-1, keepdims=True) + EPS)


def tile_scan(a, b, reverse):
    row = lax.broadcasted_iota(jnp.int32, a.shape, 1)
    for d in (1, 2, 4):
        ok = (row < 8 - d) if reverse else (row >= d)
        shift = 8 - d if reverse else d
        a_near = jnp.where(ok, pltpu.roll(a, shift, 1), 1.0)
        b_near = jnp.where(ok, pltpu.roll(b, shift, 1), 0.0)
        b = b + a * b_near
        a = a * a_near
    return a, b


def part_scan(a, b, a_ref, b_ref, reverse):
    seqs, rows, lanes = a.shape
    tiles = rows // 8
    a, b = tile_scan(a.reshape(seqs * tiles, 8, lanes), b.reshape(seqs * tiles, 8, lanes), reverse)
    a = a.reshape(seqs, tiles, 8, lanes)
    b = b.reshape(seqs, tiles, 8, lanes)
    a_run = b_run = None
    edge = 0 if reverse else 7
    for i in range(tiles):
        t = tiles - 1 - i if reverse else i
        at, bt = a[:, t], b[:, t]
        if a_run is not None:
            bt = bt + at * b_run
            at = at * a_run
        a_ref[:, t * 8 : (t + 1) * 8, :] = at
        b_ref[:, t * 8 : (t + 1) * 8, :] = bt
        a_run, b_run = at[:, edge : edge + 1, :], bt[:, edge : edge + 1, :]
    return a_run[:, 0, :], b_run[:, 0, :]


def gates_kernel(seqs, n_ref, w_ref, dw_ref, iw_ref, vec_ref,
                 cin_ref, low_ref, rec_ref, inj_ref, prod_ref, loc_ref, ends_ref):
    cin = jnp.dot(n_ref[...], w_ref[...], preferred_element_type=F32).astype(BF16)
    cin_ref[...] = cin
    x = cin.astype(F32)
    ext, lanes = x.shape
    taps = vec_ref[...]
    y = taps[4:5, :] + taps[0:1, :] * x
    for k in range(1, 4):
        y = y + taps[k : k + 1, :] * pltpu.roll(x, k, 0)
    y = y.reshape(seqs, ext // seqs, lanes)[:, PAD:, :]
    low = y.astype(BF16)
    low_ref[...] = low
    shape = y.shape
    low2 = low.reshape(shape[0] * shape[1], lanes)
    dpre = jnp.dot(low2, dw_ref[...], preferred_element_type=F32)
    ipre = jnp.dot(low2, iw_ref[...], preferred_element_type=F32)
    recur = jax.nn.sigmoid(dpre + taps[5:6, :])
    inject = jax.nn.sigmoid(ipre + taps[6:7, :])
    rate, em = decay_terms(recur, taps[7:8, :])
    recur = recur.reshape(shape)
    inject = inject.reshape(shape)
    rec_ref[...] = recur
    inj_ref[...] = inject
    injected = jnp.sqrt(em).reshape(shape) * inject * low.astype(F32)
    pa, pb = part_scan(rate.reshape(shape), injected, prod_ref, loc_ref, False)
    ends_ref[0:seqs, :] = pa
    ends_ref[seqs : 2 * seqs, :] = pb


def mix_kernel(heads, loc_ref, prod_ref, bp_ref, carry_ref, w_ref, x_ref, gain_ref,
               state_ref, mixed_ref, mid_ref, feed_ref, acc_ref):
    h = pl.program_id(0)
    carry = carry_ref[...][:, None, :]
    state = loc_ref[...] + prod_ref[...] * carry
    state_ref[...] = state
    mixed = (state * gelu_only(bp_ref[...])).astype(BF16)
    mixed_ref[...] = mixed
    b, s, lanes = mixed.shape
    part = jnp.dot(mixed.reshape(b * s, lanes), w_ref[...], preferred_element_type=F32)

    @pl.when(h == 0)
    def _():
        acc_ref[...] = x_ref[...].astype(F32) + part

    @pl.when(h > 0)
    def _():
        acc_ref[...] += part

    @pl.when(h == heads - 1)
    def _():
        mid = acc_ref[...]
        mid_ref[...] = mid
        feed_ref[...] = (mid * norm_inverse(mid) * gain_ref[...]).astype(BF16)


def back_scan_kernel(seqs, g_ref, w_ref, bp_ref, state_ref, rec_ref, vec_ref,
                     prod_ref, adj_ref, gbp_ref, ends_ref):
    gm = lax.dot_general(g_ref[...], w_ref[...], (((1,), (1,)), ((), ())), preferred_element_type=F32)
    rows, lanes = gm.shape
    shape = (seqs, rows // seqs, lanes)
    act, slope = gelu_and_slope(bp_ref[...])
    gm = gm.reshape(shape)
    gbp = gm * state_ref[...] * slope
    gbp = jnp.concatenate([jnp.zeros((seqs, PAD, lanes), F32), gbp], axis=1)
    gbp_ref[...] = gbp.reshape(seqs * (shape[1] + PAD), lanes).astype(BF16)
    rate = jnp.exp((-RATE_SCALE) * rec_ref[...] * vec_ref[7:8, :])
    after = pltpu.roll(rate.reshape(rows, lanes), rows - 1, 0).reshape(shape)
    row = lax.broadcasted_iota(jnp.int32, shape, 1)
    after = jnp.where(row == shape[1] - 1, 1.0, after)
    pa, pb = part_scan(after, gm * act, prod_ref, adj_ref, True)
    first = rate[:, 0, :]
    ends_ref[0:seqs, :] = first * pa
    ends_ref[seqs : 2 * seqs, :] = first * pb


def back_gates_kernel(heads, prod_ref, adj_ref, carry_ref, state_ref, sin_ref, rec_ref, inj_ref, low_ref,
                      cin_ref, vec_ref, dw_ref, iw_ref, gbp_ref, bw_ref, cw_ref,
                      gcin_ref, gdw_ref, giw_ref, gvec_ref, gn_ref):
    h = pl.program_id(0)
    vec = vec_ref[...]
    soft = vec[7:8, :]
    adj = adj_ref[...] + prod_ref[...] * carry_ref[...][:, None, :]
    shape = adj.shape
    seqs, rows, lanes = shape
    flat = (seqs * rows, lanes)
    state = state_ref[...]
    prev = pltpu.roll(state.reshape(flat), 1, 0).reshape(shape)
    row = lax.broadcasted_iota(jnp.int32, shape, 1)
    prev = jnp.where(row == 0, sin_ref[...][:, None, :], prev)
    recur, inject = rec_ref[...], inj_ref[...]
    rate, em = decay_terms(recur, soft)
    mult = jnp.sqrt(em)
    low = low_ref[...]
    conv = low.astype(F32)
    g_log = adj * prev * rate - adj * inject * conv * (rate * rate) / mult
    am = adj * mult
    g_elem = am * inject
    g_rec = g_log * ((-RATE_SCALE) * soft)
    g_soft = jnp.sum((g_log * recur).reshape(flat), axis=0, keepdims=True) * (-RATE_SCALE)
    gdp = (g_rec * recur * (1.0 - recur)).reshape(flat)
    gip = (am * conv * inject * (1.0 - inject)).reshape(flat)
    gdp_low, gip_low = gdp.astype(BF16), gip.astype(BF16)
    low2 = low.reshape(flat)
    tok = (((0,), (0,)), ((), ()))
    last = (((1,), (1,)), ((), ()))
    gdw_ref[...] = lax.dot_general(low2, gdp_low, tok, preferred_element_type=F32).astype(BF16)
    giw_ref[...] = lax.dot_general(low2, gip_low, tok, preferred_element_type=F32).astype(BF16)
    gc = (
        g_elem.reshape(flat)
        + lax.dot_general(gdp_low, dw_ref[...], last, preferred_element_type=F32)
        + lax.dot_general(gip_low, iw_ref[...], last, preferred_element_type=F32)
    )
    gce = jnp.concatenate([jnp.zeros((seqs, PAD, lanes), F32), gc.reshape(shape)], axis=1)
    ext = seqs * (rows + PAD)
    gce = gce.reshape(ext, lanes)
    x = cin_ref[...].astype(F32)
    out = vec[0:1, :] * gce
    sums = [jnp.sum(gce * x, axis=0, keepdims=True)]
    for k in range(1, 4):
        out = out + vec[k : k + 1, :] * pltpu.roll(gce, ext - k, 0)
        sums.append(jnp.sum(gce * pltpu.roll(x, k, 0), axis=0, keepdims=True))
    sums.append(jnp.sum(gce, axis=0, keepdims=True))
    sums.append(jnp.sum(gdp, axis=0, keepdims=True))
    sums.append(jnp.sum(gip, axis=0, keepdims=True))
    sums.append(g_soft)
    for i, v in enumerate(sums):
        gvec_ref[i : i + 1, :] = v
    gcin = out.astype(BF16)
    gcin_ref[...] = gcin
    part = lax.dot_general(gcin, cw_ref[...], last, preferred_element_type=F32)
    part += lax.dot_general(gbp_ref[...], bw_ref[...], last, preferred_element_type=F32)

    @pl.when(h == 0)
    def _():
        gn_ref[...] = part

    @pl.when(h > 0)
    def _():
        gn_ref[...] += part


def carry_kernel(seqs, n_seq, n_mlp, reverse, ends_ref, out_ref, zbuf, sbuf, mine_low, total, ssem, rsem):
    ms, mz = lax.axis_index("seq"), lax.axis_index("mlp")
    barrier = pltpu.get_barrier_semaphore()
    for d in range(1, n_mlp):
        pl.semaphore_signal(barrier, inc=1, device_id=(ms, lax.rem(mz + d, n_mlp)), device_id_type=MESH)
    for d in range(1, n_seq):
        pl.semaphore_signal(barrier, inc=1, device_id=(lax.rem(ms + d, n_seq), mz), device_id_type=MESH)
    pl.semaphore_wait(barrier, n_mlp + n_seq - 2)
    mine_low[...] = ends_ref[...].astype(BF16)
    copies = []
    for d in range(1, n_mlp):
        copies.append(pltpu.make_async_remote_copy(
            src_ref=mine_low, dst_ref=zbuf.at[mz], send_sem=ssem.at[d - 1], recv_sem=rsem.at[d - 1],
            device_id=(ms, lax.rem(mz + d, n_mlp)), device_id_type=MESH))
        copies[-1].start()
    zbuf[mz] = mine_low[...]
    for c in copies:
        c.wait()
    shape = (seqs, ends_ref.shape[1])
    tp, ts = jnp.ones(shape, F32), jnp.zeros(shape, F32)
    pp, ps = tp, ts
    for i in range(n_mlp):
        z = n_mlp - 1 - i if reverse else i
        val = zbuf[z].astype(F32)
        p, s = val[0:seqs, :], val[seqs : 2 * seqs, :]
        ts = p * ts + s
        tp = p * tp
        mine = jnp.where((z > mz) if reverse else (z < mz), 1.0, 0.0)
        ps = mine * (p * ps + s) + (1.0 - mine) * ps
        pp = (mine * p + (1.0 - mine)) * pp
    total[...] = jnp.concatenate([tp, ts], axis=0).astype(BF16)
    copies = []
    for d in range(1, n_seq):
        i = n_mlp - 2 + d
        copies.append(pltpu.make_async_remote_copy(
            src_ref=total, dst_ref=sbuf.at[ms], send_sem=ssem.at[i], recv_sem=rsem.at[i],
            device_id=(lax.rem(ms + d, n_seq), mz), device_id_type=MESH))
        copies[-1].start()
    sbuf[ms] = total[...]
    for c in copies:
        c.wait()
    c = jnp.zeros(shape, F32)
    for i in range(n_seq):
        q = n_seq - 1 - i if reverse else i
        val = sbuf[q].astype(F32)
        p, s = val[0:seqs, :], val[seqs : 2 * seqs, :]
        mine = jnp.where((q > ms) if reverse else (q < ms), 1.0, 0.0)
        c = mine * (p * c + s) + (1.0 - mine) * c
    out_ref[...] = pp * c + ps


def carry_call(ends, seqs, n_seq, n_mlp, reverse):
    rows, width = ends.shape
    n = n_seq + n_mlp - 2
    return pl.pallas_call(
        functools.partial(carry_kernel, seqs, n_seq, n_mlp, reverse),
        out_shape=jax.ShapeDtypeStruct((seqs, width), F32),
        in_specs=[pl.BlockSpec(memory_space=pltpu.VMEM)],
        out_specs=pl.BlockSpec(memory_space=pltpu.VMEM),
        scratch_shapes=[
            pltpu.VMEM((n_mlp, rows, width), BF16),
            pltpu.VMEM((n_seq, rows, width), BF16),
            pltpu.VMEM((rows, width), BF16),
            pltpu.VMEM((rows, width), BF16),
            pltpu.SemaphoreType.DMA((n,)),
            pltpu.SemaphoreType.DMA((n,)),
        ],
        compiler_params=pltpu.CompilerParams(
            collective_id=1 if reverse else 0, has_side_effects=True, vmem_limit_bytes=VMEM_LIMIT
        ),
        cost_estimate=pl.CostEstimate(flops=0, bytes_accessed=200 * rows * width * 4, transcendentals=0),
        name="carry_back" if reverse else "carry_fwd",
    )(ends)


def spread_kernel(n_seq, n_mlp, plans, starts, order, *refs):
    ms, mz = lax.axis_index("seq"), lax.axis_index("mlp")
    count = len(plans)
    shards, outs = refs[:count], refs[count : 2 * count]
    ssem, rsem = refs[2 * count :]
    n_bits = n_seq.bit_length() - 1
    digit = lambda bit: lax.rem(lax.div(ms, 1 << bit), 2)
    seq_peer = lambda bit: (ms + (1 - 2 * digit(bit)) * (1 << bit), mz)
    used = [0]

    def block_of(mask):
        at = ms
        for bit in range(n_bits):
            if (mask >> bit) & 1:
                at = at + (1 - 2 * digit(bit)) * (1 << bit)
        return at

    barrier = pltpu.get_barrier_semaphore()
    for bit in range(n_bits):
        pl.semaphore_signal(barrier, inc=1, device_id=seq_peer(bit), device_id_type=MESH)
    for d in range(1, n_mlp):
        pl.semaphore_signal(barrier, inc=1, device_id=(ms, lax.rem(mz + d, n_mlp)), device_id_type=MESH)
    local = []
    for a, parts in enumerate(plans):
        dst = outs[a].at[ms, mz] if len(parts[0]) > 1 else outs[a].at[:, mz]
        local.append(pltpu.make_async_copy(shards[a], dst, rsem.at[used[0]]))
        local[-1].start()
        used[0] += 1
    pl.semaphore_wait(barrier, n_bits + n_mlp - 1)

    def send(src, dst, peer):
        i = used[0]
        used[0] += 1
        c = pltpu.make_async_remote_copy(
            src_ref=src, dst_ref=dst, send_sem=ssem.at[i], recv_sem=rsem.at[i],
            device_id=peer, device_id_type=MESH)
        c.start()
        return c

    state = [
        [{"held": [0], "all": False, "moved": False, "core": set()} for _ in parts] for parts in plans
    ]
    pending = [[] for _ in plans]

    def start(a, level):
        parts = plans[a]
        if level >= len(parts[0]):
            return
        if level > 0 and local[a] is not None:
            local[a].wait()
            local[a] = None
        for h, (stages, st) in enumerate(zip(parts, state[a])):
            stage = stages[level]
            if len(stages) == 1:
                for d in range(1, n_mlp):
                    z = lax.rem(mz + d, n_mlp)
                    pending[a].append(send(shards[a], outs[a].at[:, mz], (ms, z)))
                continue
            width = shards[a].shape[1] // len(parts)
            cols = pl.ds(h * width, width)

            def place(mask, dst):
                at = block_of(mask)
                if not dst and not st["moved"]:
                    return shards[a].at[:, cols]
                if st["all"]:
                    return outs[a].at[at, :, :, cols]
                return outs[a].at[at, mz, :, cols]

            if stage != "z" and st["all"]:
                for mask in st["held"]:
                    if mask not in st["core"]:
                        st["core"].add(mask)
                        pending[a].append(send(place(mask, False), place(mask, True), seq_peer(0)))
            if stage == 0:
                continue
            moves = [(place(mask, False), place(mask, True)) for mask in st["held"]]
            if stage == "z":
                peers = [(ms, lax.rem(mz + d, n_mlp)) for d in range(1, n_mlp)]
                st["all"] = True
            else:
                peers = [seq_peer(stage)]
                st["held"] = st["held"] + [mask | (1 << stage) for mask in st["held"]]
            st["moved"] = True
            for peer in peers:
                for src, dst in moves:
                    pending[a].append(send(src, dst, peer))

    def end(a):
        for c in pending[a]:
            c.wait()
        pending[a] = []

    for a in starts:
        start(a, 0)
    for a, level, after in order:
        if level < len(plans[a][0]):
            end(a)
            start(a, level + 1)
        for b in after:
            start(b, 0)
    for c in local:
        if c is not None:
            c.wait()


def spread_call(small, first, second, third, tokens, n_seq, n_mlp):
    chips, turned = chip_orders(n_seq)
    line = ["z"] + chips + [0]
    pair = [line, ["z"] + turned + [0]]
    cross = [chips[:1] + ["z"] + chips[1:] + [0], turned[:1] + ["z"] + turned[1:] + [0]]
    arrays = [small, first, second, third, tokens]
    plans = [[line], pair, pair, cross, [["z"]]]
    levels = len(line)
    order = []
    for t in range(levels + 1):
        if t < levels:
            order += [(0, t, []), (1, t, [2] if t == 0 else [])]
        if t > 0:
            order += [(2, t - 1, []), (3, t - 1, [4] if t == 1 else [])]
    order.append((4, 0, []))
    n_sem = len(arrays)
    for parts in plans:
        for stages in parts:
            held = 1
            for stage in stages:
                n_sem += held * (n_mlp - 1 if stage == "z" else 1)
                held *= 1 if stage == "z" else 2
    shapes = [(n_seq, n_mlp) + v.shape for v in arrays[:4]]
    shapes.append((tokens.shape[0], n_mlp) + tokens.shape[1:])
    return pl.pallas_call(
        functools.partial(spread_kernel, n_seq, n_mlp, plans, (0, 1, 3), order),
        out_shape=[jax.ShapeDtypeStruct(s, BF16) for s in shapes],
        in_specs=[pl.BlockSpec(memory_space=pltpu.VMEM)] * len(arrays),
        out_specs=[pl.BlockSpec(memory_space=pl.ANY)] * len(arrays),
        scratch_shapes=[pltpu.SemaphoreType.DMA((n_sem,)), pltpu.SemaphoreType.DMA((n_sem,))],
        compiler_params=pltpu.CompilerParams(
            collective_id=3, has_side_effects=True, vmem_limit_bytes=VMEM_LIMIT
        ),
        name="spread",
    )(*arrays)


def chip_orders(n_seq):
    chips = list(range(1, n_seq.bit_length() - 1))
    turn = len(chips) // 2
    return chips, chips[turn:] + chips[:turn]


def owners_plan(cols, n_seq, crossed, last):
    orders = chip_orders(n_seq)
    if crossed:
        orders = [o[:1] + ["z"] + o[1:] for o in orders]
    else:
        orders = [o + ["z"] for o in orders]
    tiles = cols // 128
    sizes = [tiles // 2, tiles - tiles // 2]
    if last and tiles >= 8:
        small = tiles // 5
        big = (tiles - 2 * small) // 2
        sizes = [big, big, small, tiles - 2 * big - small]
    units, at = [], 0
    for i in range(0, len(sizes), 2):
        unit = []
        for j in range(2):
            unit.append((at, sizes[i + j] * 128, tuple(orders[j])))
            at += sizes[i + j] * 128
        units.append(unit)
    return units


def owners_shapes(n_seq, n_mlp, rows, width, stages):
    blocks, z = n_seq, n_mlp
    out = []
    for stage in stages:
        if stage == "z":
            arrive = (n_mlp - 1, blocks, rows, width)
            z = 1
        else:
            blocks //= 2
            arrive = (blocks, z, rows, width)
        out.append((arrive, (blocks, z, rows, width)))
    return out


def owners_kernel(n_seq, n_mlp, count, units, *refs):
    ms, mz = lax.axis_index("seq"), lax.axis_index("mlp")
    arrays, vec = refs[:count], refs[count]
    outs, vec_out = refs[count + 1 : 2 * count + 1], refs[2 * count + 1]
    scratch = list(refs[2 * count + 2 :])
    vec_in, vec_sum, ssem, rsem = scratch[-4:]
    n_bits = n_seq.bit_length() - 1
    mine = lambda bit: lax.rem(lax.div(ms, 1 << bit), 2)
    seq_peer = lambda bit: (ms + (1 - 2 * mine(bit)) * (1 << bit), mz)
    core = mine(0)
    used = [0]

    barrier = pltpu.get_barrier_semaphore()
    for bit in range(n_bits):
        pl.semaphore_signal(barrier, inc=1, device_id=seq_peer(bit), device_id_type=MESH)
    for d in range(1, n_mlp):
        pl.semaphore_signal(barrier, inc=1, device_id=(ms, lax.rem(mz + d, n_mlp)), device_id_type=MESH)
    pl.semaphore_wait(barrier, n_bits + n_mlp - 1)

    def send(src, dst, peer):
        i = used[0]
        used[0] += 1
        c = pltpu.make_async_remote_copy(
            src_ref=src, dst_ref=dst, send_sem=ssem.at[i], recv_sem=rsem.at[i],
            device_id=peer, device_id_type=MESH)
        c.start()
        return c

    def load(src, dst):
        i = used[0]
        used[0] += 1
        c = pltpu.make_async_copy(src, dst, rsem.at[i])
        c.start()
        return c

    tasks = []
    for unit in units:
        group = []
        for a, at, width, stages in unit:
            t = {"a": a, "at": at, "cols": pl.ds(at, width), "stages": stages, "recv": [], "sum": []}
            t["own"] = scratch.pop(0)
            for _ in stages:
                t["recv"].append(scratch.pop(0))
                t["sum"].append(scratch.pop(0))
            t["csend"], t["crecv"] = scratch.pop(0), scratch.pop(0)
            left, t["runs"] = list(range(n_bits))[::-1], []
            for stage in stages:
                if stage == "z":
                    t["runs"].append(None)
                    continue
                pos = left.index(stage)
                t["runs"].append((1 << pos, 1 << (len(left) - 1 - pos)))
                left.remove(stage)
            group.append(t)
        tasks.append(group)

    def joined(t, side):
        half = arrays[t["a"]].shape[3]
        return pl.ds(pl.multiple_of(side * half + t["at"], 128), t["csend"].shape[1])

    def begin(t, i):
        stage = t["stages"][i]
        t["wait"] = []
        if stage == "z":
            for d in range(1, n_mlp):
                z = lax.rem(mz + d, n_mlp)
                t["wait"].append(send(t["sum"][i - 1].at[:, z], t["recv"][i].at[d - 1], (ms, z)))
            return
        runs, length = t["runs"][i]
        for j in range(runs):
            away = pl.ds((2 * j + 1 - mine(stage)) * length, length)
            home = pl.ds((2 * j + mine(stage)) * length, length)
            to = pl.ds(j * length, length)
            if i == 0:
                src = arrays[t["a"]].at[away, :, :, t["cols"]]
                t["wait"].append(load(arrays[t["a"]].at[home, :, :, t["cols"]], t["own"].at[to]))
            else:
                src = t["sum"][i - 1].at[away]
            t["wait"].append(send(src, t["recv"][i].at[to], seq_peer(stage)))

    def finish(t, i):
        for c in t["wait"]:
            c.wait()
        stage = t["stages"][i]
        recv, total = t["recv"][i], t["sum"][i]
        blocks, zs = total.shape[0], total.shape[1]
        kind = total.dtype
        if stage == "z":
            for k in range(blocks):
                v = t["sum"][i - 1][k, mz].astype(F32)
                for d in range(1, n_mlp):
                    v = v + recv[d - 1, k].astype(F32)
                total[k, 0] = v.astype(kind)
        else:
            runs, length = t["runs"][i]
            for j in range(runs):

                def add(n, _, j=j):
                    b, q = lax.div(n, zs), lax.rem(n, zs)
                    if i == 0:
                        kept = t["own"][j * length + b, q]
                    else:
                        kept = t["sum"][i - 1][(2 * j + mine(stage)) * length + b, q]
                    v = kept.astype(F32) + recv[j * length + b, q].astype(F32)
                    total[j * length + b, q] = v.astype(kind)
                    return 0

                lax.fori_loop(0, length * zs, add, 0)
        if i + 1 < len(t["stages"]):
            begin(t, i + 1)
        else:
            outs[t["a"]][:, joined(t, core)] = total[core, 0]
            t["csend"][...] = total[1 - core, 0].astype(BF16)
            t["wait"] = [send(t["csend"], t["crecv"], seq_peer(0))]

    def close(t):
        for c in t["wait"]:
            c.wait()
        outs[t["a"]][:, joined(t, 1 - core)] = t["crecv"][...].astype(F32)

    vec_peers = []
    for bit in range(n_mlp.bit_length() - 1):
        side = lax.rem(lax.div(mz, 1 << bit), 2)
        vec_peers.append((ms, mz + (1 - 2 * side) * (1 << bit)))
    vec_peers += [seq_peer(bit) for bit in range(n_bits)]
    vec_state = [None, 0]

    def vec_step():
        copy, i = vec_state
        if copy is not None:
            copy.wait()
            before = vec[...] if i == 1 else vec_sum[i - 2]
            v = before + vec_in[i - 1]
            if i == len(vec_peers):
                vec_out[...] = v
            else:
                vec_sum[i - 1] = v
        vec_state[0] = None
        if i < len(vec_peers):
            src = vec if i == 0 else vec_sum.at[i - 1]
            vec_state[:] = [send(src, vec_in.at[i], vec_peers[i]), i + 1]

    n_stages = len(tasks[0][0]["stages"])
    for group in tasks[:2]:
        for t in group:
            begin(t, 0)
    vec_step()
    for step in range(len(tasks) + n_stages):
        for i in range(n_stages + 1):
            u = step - i
            if not 0 <= u < len(tasks):
                continue
            for t in tasks[u]:
                if i < n_stages:
                    finish(t, i)
                else:
                    close(t)
            if i == 0 and u + 2 < len(tasks):
                for t in tasks[u + 2]:
                    begin(t, 0)
        vec_step()
    while vec_state[0] is not None:
        vec_step()


def owners_call(arrays, vec, n_seq, n_mlp):
    units, scratch, n_sem = [], [], 0
    for a, v in enumerate(arrays):
        plan = owners_plan(v.shape[3], n_seq, a == 0, True)
        units += [[(a,) + part for part in unit] for unit in plan]
    for unit in units:
        for a, at, width, stages in unit:
            rows = arrays[a].shape[2]
            scratch.append(pltpu.VMEM((n_seq // 2, n_mlp, rows, width), BF16))
            shapes = owners_shapes(n_seq, n_mlp, rows, width, stages)
            for i, (arrive, total) in enumerate(shapes):
                scratch.append(pltpu.VMEM(arrive, BF16))
                scratch.append(pltpu.VMEM(total, F32 if i == len(shapes) - 1 else BF16))
            scratch += [pltpu.VMEM((rows, width), BF16)] * 2
            n_sem += 3 * n_seq + n_mlp
    steps = (n_mlp.bit_length() - 1) + (n_seq.bit_length() - 1)
    n_sem += steps
    vmem = pl.BlockSpec(memory_space=pltpu.VMEM)
    outs = pl.pallas_call(
        functools.partial(owners_kernel, n_seq, n_mlp, len(arrays), units),
        out_shape=[jax.ShapeDtypeStruct((v.shape[2], 2 * v.shape[3]), F32) for v in arrays]
        + [jax.ShapeDtypeStruct(vec.shape, F32)],
        in_specs=[pl.BlockSpec(memory_space=pl.ANY)] * len(arrays) + [vmem],
        out_specs=[vmem] * (len(arrays) + 1),
        scratch_shapes=scratch + [
            pltpu.VMEM((steps,) + vec.shape, F32),
            pltpu.VMEM((steps,) + vec.shape, F32),
            pltpu.SemaphoreType.DMA((n_sem,)),
            pltpu.SemaphoreType.DMA((n_sem,)),
        ],
        compiler_params=pltpu.CompilerParams(
            collective_id=2, has_side_effects=True, vmem_limit_bytes=60 << 20
        ),
        name="owners",
    )(*arrays, vec)
    return outs[:-1], outs[-1]


def split_kernel(parts, kept, sides_ref, *refs):
    ins, outs = refs[: 2 * parts], refs[2 * parts + kept :]
    for i in range(parts):
        total = ins[2 * i][...].astype(F32) + ins[2 * i + 1][...].astype(F32)
        outs[i][...] = total.reshape(outs[i].shape).astype(outs[i].dtype)


def split_place(j, pos, blocks, side):
    length = blocks >> (pos + 1)
    return (2 * lax.div(j, length) + side) * length + lax.rem(j, length)


def split_cores(own, got, a, arrays, seq, bufs):
    blocks, rows, cols = got.shape
    half = rows // 2
    left = seq.bits[::-1][:-1]
    own = own.reshape(2 * blocks, 2, half, cols)
    got = got.reshape(blocks, 2, half, cols)
    sides = jnp.stack([seq.mine(0)] + [seq.mine(o[0]) for o in seq.orders])
    block = (1, 1, half, cols)
    ins, args = [], []
    for h in range(2):
        pos = left.index(seq.orders[h][0])
        for flip in (1, 0):

            def at(j, s, h=h, pos=pos, flip=flip):
                side = 1 - s[1 + h] if flip else s[1 + h]
                return split_place(j, pos, blocks, side)

            ins.append(pl.BlockSpec(block, lambda j, s, at=at, h=h: (2 * at(j, s) + s[0], h, 0, 0)))
            ins.append(pl.BlockSpec(block, lambda j, s, at=at, h=h: (at(j, s), h, 0, 0)))
            args += [own, got]
    kept = 0 if bufs is None else 4
    shape = (arrays, blocks // 2, half, cols)
    return pl.pallas_call(
        functools.partial(split_kernel, 4, kept),
        grid_spec=pltpu.PrefetchScalarGridSpec(
            num_scalar_prefetch=1,
            grid=(blocks // 2,),
            in_specs=ins + [pl.BlockSpec(memory_space=pl.ANY)] * kept,
            out_specs=[pl.BlockSpec(block, lambda j, s: (a, j, 0, 0))] * 4,
        ),
        out_shape=[jax.ShapeDtypeStruct(shape, BF16)] * 4,
        input_output_aliases={9 + i: i for i in range(kept)},
        compiler_params=pltpu.CompilerParams(vmem_limit_bytes=VMEM_LIMIT),
        cost_estimate=pl.CostEstimate(flops=0, bytes_accessed=6 * own.size, transcendentals=0),
        name="split_cores",
    )(sides, *args, *(bufs or ()))


def split_chips(keep, got, left, bit, seq):
    arrays, blocks, rows, cols = keep.shape
    pos = left.index(bit)
    block = (1, 1, rows, cols)
    sides = seq.mine(bit)[None]
    ins, args = [], []
    for flip in (1, 0):

        def at(j, s, flip=flip):
            return split_place(j, pos, blocks, 1 - s[0] if flip else s[0])

        ins += [pl.BlockSpec(block, lambda i, j, s, at=at: (i, at(j, s), 0, 0))] * 2
        args += [keep, got]
    return pl.pallas_call(
        functools.partial(split_kernel, 2, 0),
        grid_spec=pltpu.PrefetchScalarGridSpec(
            num_scalar_prefetch=1,
            grid=(arrays, blocks // 2),
            in_specs=ins,
            out_specs=[pl.BlockSpec(block, lambda i, j, s: (i, j, 0, 0))] * 2,
        ),
        out_shape=[jax.ShapeDtypeStruct((arrays, blocks // 2, rows, cols), BF16)] * 2,
        compiler_params=pltpu.CompilerParams(vmem_limit_bytes=VMEM_LIMIT),
        cost_estimate=pl.CostEstimate(flops=0, bytes_accessed=6 * keep.size, transcendentals=0),
        name="split_chips",
    )(sides, *args)


def join_kernel(*refs):
    ins, outs = refs[:4], refs[4:]
    for i, out in enumerate(outs):
        halves = [ins[k][i, 0].astype(F32) + ins[k + 1][i, 0].astype(F32) for k in (0, 2)]
        v = jnp.concatenate(halves, axis=0)
        out[...] = v.T if i == len(outs) - 1 else v


def join_halves(feed_state):
    arrays, _, half, cols = feed_state[0][0].shape
    shapes = [(2 * half, cols)] * (arrays - 1) + [(cols, 2 * half)]
    args = [v for e in feed_state for v in e[:2]]
    vmem = pl.BlockSpec(memory_space=pltpu.VMEM)
    return pl.pallas_call(
        join_kernel,
        out_shape=[jax.ShapeDtypeStruct(v, F32) for v in shapes],
        in_specs=[vmem] * len(args),
        out_specs=[vmem] * arrays,
        compiler_params=pltpu.CompilerParams(vmem_limit_bytes=VMEM_LIMIT),
        cost_estimate=pl.CostEstimate(
            flops=0, bytes_accessed=4 * arrays * 2 * half * cols * 2, transcendentals=0
        ),
        name="join_halves",
    )(*args)


class Seq:
    def __init__(self):
        self.n = lax.axis_size("seq")
        self.me = lax.axis_index("seq")
        self.bits = list(range(self.n.bit_length() - 1))
        chips = self.bits[1:]
        turn = len(chips) // 2
        self.orders = (chips, chips[turn:] + chips[:turn])

    def mine(self, bit):
        return (self.me >> bit) & 1

    def swap(self, v, bit):
        return lax.ppermute(v, "seq", [(i, i ^ (1 << bit)) for i in range(self.n)])


def flat_dot(left, right):
    shape = left.shape
    out = jnp.dot(left.reshape(-1, shape[-1]), right, preferred_element_type=F32)
    return out.reshape(shape[:-1] + (right.shape[1],))


def dot_against(left, right):
    shape = left.shape
    out = lax.dot_general(
        left.reshape(-1, shape[-1]), right, (((1,), (1,)), ((), ())), preferred_element_type=F32
    )
    return out.reshape(shape[:-1] + (right.shape[0],))


def outer_sum(left, right):
    return lax.dot_general(
        left.reshape(-1, left.shape[-1]),
        right.reshape(-1, right.shape[-1]),
        (((0,), (0,)), ((), ())),
        preferred_element_type=F32,
    )


def gated_unit(gate_pre, up_pre):
    return jax.nn.gelu(gate_pre) * up_pre


def norm_back(values, inverse, gain, upstream):
    scaled = upstream * gain
    gain_grad = jnp.sum(upstream * values * inverse, axis=(0, 1))
    inner_mean = jnp.mean(scaled * values, axis=-1, keepdims=True)
    return (inverse * (scaled - values * inner_mean * inverse * inverse), gain_grad)


def per_device(inputs, mixer_gain, branch_weight, input_weight, conv_weight, conv_bias, decay_weight,
               decay_bias, inject_weight, inject_bias, decay_param, output_weight, feed_gain,
               feed_gate, feed_up, feed_down, cotangent):
    both = ("seq", "mlp")
    seq = Seq()
    n_seq, n_mlp = seq.n, lax.axis_size("mlp")
    n_dev = n_seq * n_mlp
    seqs, rows, width = inputs.shape
    taps, r_own = conv_weight.shape
    edge = taps - 1
    head = decay_weight.shape[1]
    r_all = r_own * n_dev
    heads = r_all // head
    d_own = width // n_dev
    ext_rows = rows + PAD
    ext = seqs * ext_rows
    tokens = seqs * rows

    lanes = 128
    small = [conv_weight.T, conv_bias[:, None], decay_bias[:, None], inject_bias[:, None], decay_param[:, None]]
    gains = [jnp.pad(g, (0, r_own - d_own))[:, None] for g in (mixer_gain, feed_gain)]
    small = jnp.concatenate(small + gains, axis=1)
    small = jnp.pad(small, ((0, 0), (0, lanes - small.shape[1])))
    gates_own = jnp.concatenate([decay_weight, inject_weight, small], axis=1)
    n_chunks = 2 if seqs % 2 == 0 else 1
    per = seqs // n_chunks
    chunk = lambda v, c: v[c * per : (c + 1) * per]
    gates_all, full_input, full_branch, full_output, first_cot = spread_call(
        gates_own, input_weight, branch_weight, output_weight, chunk(cotangent, 0), n_seq, n_mlp
    )
    gates_all = gates_all.reshape(r_all, -1)
    full_input, full_branch = (v.reshape(width, r_all) for v in (full_input, full_branch))
    full_output = full_output.reshape(r_all, width)
    grad_rows = [first_cot.reshape(per, n_mlp * rows, width)]
    for c in range(1, n_chunks):
        gates_all, cot = lax.optimization_barrier((gates_all, chunk(cotangent, c)))
        grad_rows.append(lax.all_gather(cot, "mlp", axis=1, tiled=True))
    vectors = gates_all[:, 2 * head :].astype(F32)
    gain_rows = vectors[:, 8:10].reshape(n_dev, r_own, 2)[:, :d_own, :].reshape(width, 2)
    gain_mixer, gain_feed = gain_rows[:, 0], gain_rows[:, 1]
    param = vectors[:, 7]
    vec = jnp.concatenate([vectors[:, :7].T, jax.nn.softplus(-param)[None, :]], axis=0)

    last_tokens = lax.ppermute(inputs[:, rows - edge :, :], both, [(i, i + 1) for i in range(n_dev - 1)])
    x_ext = jnp.concatenate(
        [jnp.zeros((seqs, PAD - edge, width), BF16), last_tokens, inputs], axis=1
    )
    stream_ext = x_ext.astype(F32)
    inverse_ext = norm_inverse(stream_ext)
    normed_ext = (stream_ext * inverse_ext * gain_mixer).astype(BF16).reshape(ext, width)

    params = lambda **k: pltpu.CompilerParams(dimension_semantics=("arbitrary",), vmem_limit_bytes=VMEM_LIMIT, **k)

    def cost(big_dots, arrays):
        whole_mats = 2 * ext * width * r_all
        return pl.CostEstimate(
            flops=big_dots * whole_mats,
            bytes_accessed=big_dots * 2 * width * r_all + arrays * 4 * tokens * r_all,
            transcendentals=4 * tokens * r_all,
        )

    tok_head = pl.BlockSpec((seqs, rows, head), lambda h: (0, 0, h))
    ext_head = pl.BlockSpec((ext, head), lambda h: (0, h))
    vec_head = pl.BlockSpec((8, head), lambda h: (0, h))
    seq_head = pl.BlockSpec((seqs, head), lambda h: (0, h))
    col_head = pl.BlockSpec((width, head), lambda h: (0, h))
    row_head = pl.BlockSpec((head, width), lambda h: (h, 0))
    decay_head = pl.BlockSpec((head, head), lambda h: (h, 0))
    inject_head = pl.BlockSpec((head, head), lambda h: (h, 1))
    whole = lambda *shape: pl.BlockSpec(shape, lambda h: (0,) * len(shape))
    tok = lambda kind: jax.ShapeDtypeStruct((seqs, rows, r_all), kind)
    struct = jax.ShapeDtypeStruct

    conv_in, conv_low, recur, inject, prod, local, ends = pl.pallas_call(
        functools.partial(gates_kernel, seqs),
        grid=(heads,),
        in_specs=[whole(ext, width), col_head, decay_head, inject_head, vec_head],
        out_specs=[ext_head, tok_head, tok_head, tok_head, tok_head, tok_head,
                   pl.BlockSpec((2 * seqs, head), lambda h: (0, h))],
        out_shape=[struct((ext, r_all), BF16), tok(BF16), tok(F32), tok(F32), tok(F32), tok(F32),
                   struct((2 * seqs, r_all), F32)],
        compiler_params=params(),
        cost_estimate=cost(1, 20),
        name="gates",
    )(normed_ext, full_input, gates_all, gates_all, vec)

    state_in = carry_call(ends, seqs, n_seq, n_mlp, False)
    normed = normed_ext.reshape(seqs, ext_rows, width)[:, PAD:, :]
    branch_pre = flat_dot(normed, full_branch)

    state, mixed, mid, feed_low = pl.pallas_call(
        functools.partial(mix_kernel, heads),
        grid=(heads,),
        in_specs=[tok_head, tok_head, tok_head, seq_head, row_head, whole(tokens, width), whole(1, width)],
        out_specs=[tok_head, tok_head, whole(tokens, width), whole(tokens, width)],
        out_shape=[tok(F32), tok(BF16), struct((tokens, width), F32), struct((tokens, width), BF16)],
        scratch_shapes=[pltpu.VMEM((tokens, width), F32)],
        compiler_params=params(),
        cost_estimate=cost(1, 12),
        name="mix",
    )(local, prod, branch_pre, state_in, full_output, inputs.reshape(tokens, width), gain_feed[None, :])
    stream_mid = mid.reshape(seqs, rows, width)

    feed_own = feed_low.reshape(seqs, rows, width)
    row_major = lambda v: with_layout_constraint(v, Layout(major_to_minor=tuple(range(v.ndim))))
    mixed_two = mixed.reshape(tokens, r_all)
    mixed_two = jnp.concatenate([mixed_two, seq.swap(mixed_two, 0)], axis=0)
    normed_two = jnp.concatenate([normed_ext, seq.swap(normed_ext, 0)], axis=0)
    grad_hidden = [dot_against(v, feed_down) for v in grad_rows]
    grad_rows = jnp.concatenate(grad_rows, axis=0)
    feed_rows, hidden, gate_low, up_low, feed_norm_grad = [], [], [], [], []
    for c in range(n_chunks):
        f = row_major(lax.all_gather(chunk(feed_own, c), "mlp", axis=1, tiled=True))
        if c == 0:
            f, grad_hidden, mixed_two, normed_two = lax.optimization_barrier(
                (f, grad_hidden, mixed_two, normed_two)
            )
        else:
            f, back = lax.optimization_barrier((f, back))
            feed_norm_grad.append(lax.psum_scatter(back, "mlp", scatter_dimension=1, tiled=True))
        gate_pre = flat_dot(f, feed_gate)
        up_pre = flat_dot(f, feed_up)
        hidden.append(gated_unit(gate_pre, up_pre).astype(BF16))
        gate_grad, up_grad = jax.vjp(gated_unit, gate_pre, up_pre)[1](grad_hidden[c])
        gate_low.append(gate_grad.astype(BF16))
        up_low.append(up_grad.astype(BF16))
        feed_rows.append(f)
        back = (dot_against(gate_low[-1], feed_gate) + dot_against(up_low[-1], feed_up)).astype(BF16)
    back, feed_rows, hidden, gate_low, up_low = lax.optimization_barrier(
        (back, feed_rows, hidden, gate_low, up_low)
    )
    feed_norm_grad, back, hidden = lax.optimization_barrier((feed_norm_grad, back, hidden))
    feed_norm_grad.append(lax.psum_scatter(back, "mlp", scatter_dimension=1, tiled=True))
    feed_rows, hidden, gate_low, up_low = (
        jnp.concatenate(v, axis=0) for v in (feed_rows, hidden, gate_low, up_low)
    )
    feed_out = flat_dot(hidden, feed_down).astype(BF16)
    bufs = None
    pairs = ((feed_rows, gate_low), (feed_rows, up_low), (grad_rows, hidden))
    for a, (left, right) in enumerate(pairs):
        g = row_major(outer_sum(left, right).astype(BF16)).reshape(n_seq, width // n_seq, feed_gate.shape[1])
        other = lax.dynamic_index_in_dim(
            g.reshape((n_seq // 2, 2) + g.shape[1:]), 1 - seq.mine(0), 1, keepdims=False
        )
        bufs = list(split_cores(g, seq.swap(other, 0), a, len(pairs), seq, bufs))
    feed_norm_grad, feed_out, bufs[1], bufs[3] = lax.optimization_barrier(
        (feed_norm_grad, feed_out, bufs[1], bufs[3])
    )
    chip_bits = seq.bits[::-1][:-1]
    feed_state = [
        (bufs[2 * h + 1], seq.swap(bufs[2 * h], order[0]), [b for b in chip_bits if b != order[0]], order[1:])
        for h, order in enumerate(seq.orders)
    ]
    feed_norm_grad = jnp.concatenate(feed_norm_grad, axis=0).astype(F32)
    feed_out = lax.psum_scatter(feed_out, "mlp", scatter_dimension=1, tiled=True).astype(F32)
    result = (stream_mid + feed_out).astype(BF16)

    feed_inverse = norm_inverse(stream_mid)
    mid_part, feed_gain_grad = norm_back(stream_mid, feed_inverse, gain_feed, feed_norm_grad)
    mid_grad = cotangent.astype(F32) + mid_part
    mid_low = mid_grad.astype(BF16).reshape(tokens, width)

    back_prod, back_local, gbp, back_ends = pl.pallas_call(
        functools.partial(back_scan_kernel, seqs),
        grid=(heads,),
        in_specs=[whole(tokens, width), row_head, tok_head, tok_head, tok_head, vec_head],
        out_specs=[tok_head, tok_head, ext_head, pl.BlockSpec((2 * seqs, head), lambda h: (0, h))],
        out_shape=[tok(F32), tok(F32), struct((ext, r_all), BF16), struct((2 * seqs, r_all), F32)],
        compiler_params=params(),
        cost_estimate=cost(1, 14),
        name="back_scan",
    )(mid_low, full_output, branch_pre, state, recur, vec)
    core = seq.mine(0)

    def pair_operands(left, right):
        half = right.shape[1] // 2
        mine = lax.dynamic_slice_in_dim(right, core * half, half, 1)
        other = lax.dynamic_slice_in_dim(right, (1 - core) * half, half, 1)
        return left, jnp.concatenate([mine, seq.swap(other, 0)], axis=0)

    def pair_grad(left, right):
        g = outer_sum(*pair_operands(left, right)).astype(BF16)
        return g.reshape(n_seq, g.shape[0] // n_seq, g.shape[1])

    output_grad = pair_grad(mixed_two, mid_low)
    back_ends, output_grad = lax.optimization_barrier((back_ends, output_grad))
    adj_in = carry_call(back_ends, seqs, n_seq, n_mlp, True)
    branch_grad = pair_grad(normed_two, gbp)
    adj_in, branch_grad = lax.optimization_barrier((adj_in, branch_grad))
    while feed_state[0][3]:
        nexts = []
        for keep, got, left, order in feed_state:
            send, keep = split_chips(keep, got, left, order[0], seq)
            nexts.append((keep, send, [b for b in left if b != order[0]], order))
        adj_in, sends = lax.optimization_barrier((adj_in, [e[1] for e in nexts]))
        feed_state = [
            (keep, seq.swap(send, order[0]), left, order[1:])
            for (keep, _, left, order), send in zip(nexts, sends)
        ]

    gcin, gdw, giw, gvec, gnorm = pl.pallas_call(
        functools.partial(back_gates_kernel, heads),
        grid=(heads,),
        in_specs=[tok_head, tok_head, seq_head, tok_head, seq_head, tok_head, tok_head, tok_head,
                  ext_head, vec_head, decay_head, inject_head, ext_head, col_head, col_head],
        out_specs=[ext_head, decay_head, decay_head, vec_head, whole(ext, width)],
        out_shape=[struct((ext, r_all), BF16), struct((r_all, head), BF16), struct((r_all, head), BF16),
                   struct((8, r_all), F32), struct((ext, width), F32)],
        compiler_params=params(),
        cost_estimate=cost(2, 20),
        name="back_gates",
    )(back_prod, back_local, adj_in, state, state_in, recur, inject, conv_low,
      conv_in, vec, gates_all, gates_all, gbp, full_branch, full_input)

    weight_grad = pair_grad(normed_two, gcin)
    gates_mine = jnp.where(core == 0, gdw, giw)
    gates_got = seq.swap(jnp.where(core == 0, giw, gdw), 0)
    gates_grad = (gates_mine.astype(F32) + gates_got.astype(F32)).astype(BF16)

    stream_part, mixer_gain_grad = norm_back(
        stream_ext, inverse_ext, gain_mixer, gnorm.reshape(seqs, ext_rows, width)
    )
    next_part = lax.ppermute(
        stream_part[:, PAD - edge : PAD, :], both, [(i + 1, i) for i in range(n_dev - 1)]
    )
    next_part = jnp.pad(next_part, ((0, 0), (rows - edge, 0), (0, 0)))
    input_grad = mid_grad + stream_part[:, PAD:, :] + next_part

    param_grad = gvec[7] * -jax.nn.sigmoid(-param)
    gain_grads = jnp.pad(jnp.stack([mixer_gain_grad, feed_gain_grad]), ((0, 0), (0, r_all - width)))
    total = jnp.concatenate([gvec[:7], param_grad[None, :], gain_grads], axis=0)
    total = jnp.pad(total, ((0, 16 - total.shape[0]), (0, 0)))
    blocks = lambda g: g.reshape(n_seq, n_mlp, -1, g.shape[-1])
    owned, total = owners_call(
        [blocks(g) for g in (output_grad, branch_grad, gates_grad, weight_grad)], total, n_seq, n_mlp
    )
    output_out, branch_out, gates_out, input_out = owned
    decay_out, inject_out = gates_out[:, :head], gates_out[:, head:]
    total, arrived = lax.optimization_barrier((total, [e[1] for e in feed_state]))
    feed_grads = join_halves([(e[0], got) for e, got in zip(feed_state, arrived)])
    place = seq.me * n_mlp + lax.axis_index("mlp")
    tail = lax.dynamic_slice_in_dim(total[:8], place * r_own, r_own, 1)
    gains_out = lax.dynamic_slice_in_dim(total[8:10], place * d_own, d_own, 1)

    return (
        result,
        input_grad,
        gains_out[0],
        branch_out,
        input_out,
        tail[:4],
        tail[4],
        decay_out,
        tail[5],
        inject_out,
        tail[6],
        tail[7],
        output_out,
        gains_out[1],
        feed_grads[0],
        feed_grads[1],
        feed_grads[2],
    )


def solution(mesh):
    both = ("seq", "mlp")
    in_specs = (
        P(None, both, None), P(both), P(both, None), P(both, None), P(None, both), P(both),
        P(both, None), P(both), P(both, None), P(both), P(both), P(both, None), P(both),
        P(None, "mlp"), P(None, "mlp"), P("mlp", None), P(None, both, None),
    )
    out_specs = (
        P(None, both, None), P(None, both, None), P(both), P(both, None), P(both, None), P(None, both),
        P(both), P(both, None), P(both), P(both, None), P(both), P(both), P(both, None), P(both),
        P("seq", "mlp"), P("seq", "mlp"), P("mlp", "seq"),
    )
    return jax.shard_map(
        per_device, mesh=mesh, in_specs=in_specs, out_specs=out_specs, check_vma=False
    )
```
